128 devices in a mesh: seq: 4 (over x_hi, core), blk: 32 (over x_lo, z, y).
Axes of the slice: x: 4 (x_hi: 2, x_lo: 2; x = x_hi * 2 + x_lo), y: 4, z: 4, core: 2. Of those that a mesh axis runs over, the one named last changes fastest.
Arguments:
- residual_in: bfloat16 [32, 512, 2048], P('blk', 'seq'), may hold values from -6 to 6
- segment_ids: int32 [32, 512], P('blk'), may hold values from 0 to 2, never falling along the last dimension, each value on 1 to 256 neighbouring positions
- attn_gain: bfloat16 [2048], replicated, may hold values from 0.5 to 1.5
- w_qkv: bfloat16 [2048, 16, 384], P(None, 'seq')
- w_out: bfloat16 [16, 128, 2048], P('seq'), may hold values from -0.125 to 0.125
- ffn_gain: bfloat16 [2048], replicated, may hold values from 0.5 to 1.5
- w_router: bfloat16 [2048, 32], replicated, may hold values from -0.125 to 0.125
- routes: int32 [32, 512, 8], P('blk', 'seq'), may hold values from 0 to 31, all different within a row; in each aligned block of 128 rows (0 to 127, 128 to 255, ..., all dimensions but the last counted through in order) at most 48 rows name the same one
- w_gate_up: bfloat16 [32, 2048, 2048], P('blk'), may hold values from -0.125 to 0.125
- w_down: bfloat16 [32, 1024, 2048], P('blk'), may hold values from -0.1875 to 0.1875
- page_owner: int32 [32, 32], P('blk'), may hold values from 0 to 31, each once within a row
Outputs:
- residual_out: bfloat16 [32, 512, 2048], P('blk', 'seq')
- kv_cache: bfloat16 [32, 32, 16, 4096], P('blk', None, None, 'seq')
The draws below stay inside these ranges and needn't reach their ends.
Inputs may be any that keep to these rules, and one draw needn't show every extreme that they name: `segment_ids`: within a pack the numbers never fall; 1 to 3 prompts a pack, the longest exactly 256 tokens. `routes`: each token names 8 different experts; among the 128 tokens of one device no expert is named more than 48 times, a bound that some block reaches. `page_owner`: each row is a permutation.
All inputs are finite; a program needn't handle non-finite values.
Results may differ from the reference program's by a relative error of at most 0.025.
Values may be sent and summed in bfloat16 or wider, within the bound.
A program may use at most 128 MiB of HBM per device.

```python
import math
import jax
import jax.numpy as jnp
import numpy as np
from jax import lax

D = 2048
HEADS = 16
HD = 128
FF = 1024
EXPERTS = 32
TOP = 8
TOK_DEV = 128
GROUP_TOK = 512
CAP = 48
PAGE = 16
N_BLK = 32


def draw_w_qkv(key, part):
    base_key = jax.random.fold_in(jax.random.fold_in(key, 11), 0)
    base = jax.random.normal(base_key, (D, HEADS, 3 * HD), jnp.float32) / math.sqrt(D)
    return base.astype(jnp.bfloat16)


def block_scale(key, shape, cuts, smallest, largest):
    level = 1.0
    for position, blocks in cuts:
        draws = jax.random.uniform(jax.random.fold_in(jax.random.fold_in(key, 6), position), (blocks,), jnp.float32, smallest / len(cuts), largest / len(cuts))
        level = level * jnp.repeat(jnp.exp(draws), shape[position] // blocks).reshape((-1,) + (1,) * (len(shape) - 1 - position))
    return level


def split_up(count, total, limit, skew):
    weights = [(1 << 20) // math.isqrt(grade ** skew) + 1 for grade in range(2, count + 1)]
    rest, counts = total - limit - (count - 1), [1] * (count - 1)
    while rest > 0:
        movable = [i for i in range(count - 1) if counts[i] < limit]
        pool, budget = sum([weights[i] for i in movable]), rest
        for i in movable:
            more = min(limit - counts[i], max(1, budget * weights[i] // pool), rest)
            counts[i] = counts[i] + more
            rest = rest - more
    return np.array([limit] + counts)


def ragged_sizes(rng, number_of, total, bound, lean):
    if number_of == 2:
        one = jax.random.randint(rng, (), max(1, total - bound), min(bound, total - 1) + 1)
        return jnp.stack([one, total - one])
    lengths = jnp.asarray(split_up(number_of, total, bound, lean), jnp.int32)
    couples = (number_of - 1) // 2
    donor, taker = lengths[1:1 + 2 * couples:2], lengths[2:2 + 2 * couples:2]
    room = jnp.minimum(donor - 1, bound - taker)
    moved = jax.random.randint(jax.random.fold_in(rng, 1), (couples,), 0, 1 << 20) % (room + 1)
    lengths = lengths.at[1:1 + 2 * couples:2].set(donor - moved).at[2:2 + 2 * couples:2].set(taker + moved)
    return lengths[jax.random.permutation(jax.random.fold_in(rng, 2), number_of)]


def routed_block(own_key, own, number, rows, number_of, top, bound, lean):
    ranking = jax.random.permutation(own_key, number_of)
    heavy_load, common = load_shares(number_of, rows * top, bound, lean, True), load_shares(number_of, rows * top, bound, lean, False)
    places = jnp.arange(number_of)

    def named(lengths, offset_by):
        used = int((lengths > 0).sum())
        fixed = max(1, used // 4)
        passed = fixed + (places - fixed + offset_by * (used - fixed)) % max(1, number_of - fixed)
        return jnp.zeros((number_of,), jnp.int32).at[ranking[jnp.where(places < fixed, places, passed)]].set(jnp.asarray(lengths, jnp.int32))

    lengths = jnp.where(number % 4 == 0, named(heavy_load, number // 4), named(common, number - number // 4 - 1))
    mixed = jax.random.permutation(jax.random.fold_in(own, 3), number_of)
    giver, receiver = mixed[0:number_of // 2 * 2:2], mixed[1:number_of // 2 * 2:2]
    margin = jnp.minimum(lengths[giver] - 1, bound - lengths[receiver]) // 2
    margin = jnp.where((giver == ranking[0]) | (receiver == ranking[0]) | (lengths[receiver] == 0), 0, jnp.maximum(margin, 0))
    passed = jax.random.randint(jax.random.fold_in(own, 4), (number_of // 2,), 0, 1 << 20) % (margin + 1)
    lengths = lengths.at[giver].add(-passed).at[receiver].add(passed)
    items = jnp.searchsorted(jnp.cumsum(lengths), jnp.arange(rows * top), side="right").astype(jnp.int32)
    table = items.reshape(top, rows).T
    table = table[jax.random.permutation(jax.random.fold_in(own, 1), rows)]
    offset_by = jax.random.randint(jax.random.fold_in(own, 2), (rows, 1), 0, top)
    return jnp.take_along_axis(table, (jnp.arange(top)[None, :] + offset_by) % top, axis=1)


def load_shares(number_of, total, bound, slope, full):
    weights = [(1 << 20) // math.isqrt(rank ** slope) + 1 for rank in range(1, number_of + 1)]
    largest = bound if full else min(bound, max(-(-total // number_of), total * weights[0] // sum(weights)))
    least = 1 if total - largest >= number_of - 1 else 0
    holding, surplus = [largest] + [least] * (number_of - 1), total - largest - least * (number_of - 1)
    while surplus > 0:
        movable = [i for i in range(1, number_of) if holding[i] < largest] or [i for i in range(1, number_of) if holding[i] < bound]
        pool, remaining = sum([weights[i] for i in movable]), surplus
        for i in movable:
            more = min(bound - holding[i], max(1, remaining * weights[i] // pool), surplus)
            holding[i] = holding[i] + more
            surplus = surplus - more
    return np.array(holding)


def bell_draw(rng, shape, scale, limit, pieces=(), kind=jnp.bfloat16):
    drawn = scale * jax.random.normal(rng, shape, jnp.float32)
    if pieces:
        drawn = drawn * block_scale(rng, shape, pieces, -0.22, 0.18)
    return jnp.clip(drawn, -limit, limit).astype(kind)


def setup_inputs(seed: int = 0) -> dict:
    arg_keys = jax.random.split(jax.random.key(seed), 12)
    residual_in = bell_draw(arg_keys[0], (N_BLK, GROUP_TOK, D), 1.0, 6.0, ((0, 32), (1, 4)))
    segment_ids = jax.vmap(lambda own: jnp.searchsorted(jnp.cumsum(ragged_sizes(own, 3, GROUP_TOK, GROUP_TOK // 2, 2)), jnp.arange(GROUP_TOK), side="right"))(jax.random.split(arg_keys[1], N_BLK)).reshape((N_BLK, GROUP_TOK)).astype(jnp.int32)
    attn_gain = jnp.clip(1.0 + 0.1 * jax.random.normal(arg_keys[2], (D,), jnp.float32), 0.5, 1.5).astype(jnp.bfloat16)
    w_qkv = draw_w_qkv(jax.random.fold_in(arg_keys[11], 71), 0)
    w_out = bell_draw(arg_keys[4], (HEADS, HD, D), (HEADS * HD) ** -0.5, 0.125, ((0, 4),))
    ffn_gain = jnp.clip(1.0 + 0.1 * jax.random.normal(arg_keys[5], (D,), jnp.float32), 0.5, 1.5).astype(jnp.bfloat16)
    w_router = bell_draw(arg_keys[6], (D, EXPERTS), D ** -0.5, 0.125)
    routes_keys = jax.random.split(jax.random.fold_in(arg_keys[7], 1), N_BLK * GROUP_TOK // TOK_DEV)
    routes_turns = jax.random.permutation(jax.random.fold_in(arg_keys[7], 3), N_BLK * GROUP_TOK // TOK_DEV)
    routes = jax.vmap(lambda own, number: routed_block(jax.random.fold_in(arg_keys[7], 2), own, number, TOK_DEV, EXPERTS, TOP, CAP, 2))(routes_keys, routes_turns).reshape((N_BLK, GROUP_TOK, TOP))
    w_gate_up = bell_draw(arg_keys[8], (EXPERTS, D, 2 * FF), D ** -0.5, 0.125, ((0, 32),))
    w_down = bell_draw(arg_keys[9], (EXPERTS, FF, D), FF ** -0.5, 0.1875, ((0, 32),))
    page_owner = jax.vmap(lambda own: jax.random.permutation(own, N_BLK))(jax.random.split(arg_keys[10], N_BLK)).reshape((N_BLK, N_BLK)).astype(jnp.int32)
    return {"residual_in": residual_in, "segment_ids": segment_ids, "attn_gain": attn_gain, "w_qkv": w_qkv, "w_out": w_out, "ffn_gain": ffn_gain, "w_router": w_router, "routes": routes, "w_gate_up": w_gate_up, "w_down": w_down, "page_owner": page_owner}


EPS = 1e-06

def rms_norm(value, gain):
    wide = value.astype(jnp.float32)
    scale = lax.rsqrt(lax.optimization_barrier(jnp.mean(wide * wide, axis=-1, keepdims=True)) + EPS)
    return (wide * scale * gain.astype(jnp.float32)).astype(jnp.bfloat16)

def reference(residual_in, segment_ids, attn_gain, w_qkv, w_out, ffn_gain, w_router, routes, w_gate_up, w_down, page_owner):
    w_flat = w_qkv.reshape(D, HEADS * 3 * HD)
    w_out_flat = w_out.reshape(HEADS * HD, D)

    def one_group(pair):
        rows, segment_row = pair
        normed = rms_norm(rows, attn_gain)
        qkv = jnp.dot(normed, w_flat, preferred_element_type=jnp.float32).astype(jnp.bfloat16)
        qkv = qkv.reshape(GROUP_TOK, HEADS, 3 * HD)
        query = qkv[:, :, :HD].astype(jnp.float32)
        key = qkv[:, :, HD:2 * HD].astype(jnp.float32)
        value = qkv[:, :, 2 * HD:].astype(jnp.float32)
        scores = jnp.einsum('qhd,khd->hqk', query, key) / math.sqrt(HD)
        same = segment_row[:, None] == segment_row[None, :]
        scores = jnp.where(same[None], scores, jnp.float32(-1e+30))
        top = lax.optimization_barrier(jnp.max(scores, axis=-1, keepdims=True))
        weights = jnp.exp(scores - top)
        probs = (weights / lax.optimization_barrier(jnp.sum(weights, axis=-1, keepdims=True))).astype(jnp.bfloat16)
        context = jnp.einsum('hqk,khd->qhd', probs.astype(jnp.float32), value).astype(jnp.bfloat16)
        mixed = jnp.dot(context.reshape(GROUP_TOK, HEADS * HD), w_out_flat, preferred_element_type=jnp.float32)
        resid = (rows.astype(jnp.float32) + mixed).astype(jnp.bfloat16)
        kv_rows = qkv[:, :, HD:].reshape(GROUP_TOK, HEADS * 2 * HD)
        return (resid, kv_rows)
    resid, kv_rows = lax.map(one_group, (residual_in, segment_ids))
    pages = kv_rows.reshape(N_BLK, N_BLK, PAGE, HEADS * 2 * HD)
    kv_cache = jnp.zeros((N_BLK, N_BLK, PAGE, HEADS * 2 * HD), jnp.bfloat16)
    kv_cache = kv_cache.at[page_owner, jnp.arange(N_BLK, dtype=jnp.int32)[:, None]].set(pages)
    tokens = resid.reshape(N_BLK * GROUP_TOK, D)
    ffn_in = rms_norm(tokens, ffn_gain)
    logits = jnp.dot(ffn_in, w_router, preferred_element_type=jnp.float32)
    gates = jax.nn.sigmoid(logits).astype(jnp.bfloat16)
    route_flat = routes.reshape(-1, TOP)
    expert_ids = jnp.arange(EXPERTS, dtype=jnp.int32)
    chosen = jnp.any(route_flat[:, :, None] == expert_ids[None, None, :], axis=1)
    blocks = chosen.reshape(-1, TOK_DEV, EXPERTS).astype(jnp.int32)
    rank = jnp.cumsum(blocks, axis=1) - 1
    block_count = blocks.shape[0]
    slot_ids = jnp.arange(CAP, dtype=jnp.int32)
    row_ids = jnp.arange(TOK_DEV, dtype=jnp.int32)
    block_ids = jnp.arange(block_count, dtype=jnp.int32)

    def one_expert(total, expert):
        mask_e = blocks[:, :, expert]
        rank_e = rank[:, :, expert]
        hit = (mask_e[:, None, :] == 1) & (rank_e[:, None, :] == slot_ids[None, :, None])
        slot_row = lax.optimization_barrier(jnp.sum(jnp.where(hit, row_ids[None, None, :], 0), axis=2)).astype(jnp.int32)
        pick = (block_ids[:, None] * TOK_DEV + slot_row).reshape(-1).astype(jnp.int32)
        picked = jnp.take(ffn_in, pick, axis=0)
        both = jnp.dot(picked, w_gate_up[expert], preferred_element_type=jnp.float32)
        hidden = (jax.nn.silu(both[:, :FF]) * both[:, FF:]).astype(jnp.bfloat16)
        output = jnp.dot(hidden, w_down[expert], preferred_element_type=jnp.float32)
        back = (block_ids[:, None] * CAP + jnp.clip(rank_e, 0, CAP - 1)).reshape(-1).astype(jnp.int32)
        per_row = jnp.take(output, back, axis=0)
        contrib = (gates[:, expert].astype(jnp.float32)[:, None] * per_row).astype(jnp.bfloat16)
        live = mask_e.reshape(-1)[:, None] == 1
        total = total + jnp.where(live, contrib.astype(jnp.float32), jnp.float32(0.0))
        return (total, None)
    total, _ = lax.scan(one_expert, jnp.zeros((N_BLK * GROUP_TOK, D), jnp.float32), expert_ids)
    residual_out = (tokens.astype(jnp.float32) + total).astype(jnp.bfloat16).reshape(N_BLK, GROUP_TOK, D)
    return (residual_out, kv_cache)
```

```python
import math

import jax
import jax.numpy as jnp
from jax import lax
from jax.experimental import pallas as pl
from jax.experimental.pallas import tpu as pltpu
from jax.sharding import PartitionSpec as P

EPS = 1e-06


def rms_norm(value, gain):
    wide = value.astype(jnp.float32)
    scale = lax.rsqrt(jnp.mean(wide * wide, axis=-1, keepdims=True) + EPS)
    return (wide * scale * gain.astype(jnp.float32)).astype(jnp.bfloat16)


NPOS = 32
CAP = 48
GRP = 8
NGRP = NPOS // GRP
ROWS = GRP * CAP
TILE = 256
MESH = pl.DeviceIdType.MESH


def step_of(position):
    k = lax.rem(position * 3, NPOS)
    dx, dz, dy = lax.div(k, 16), lax.rem(lax.div(k, 4), 4), lax.rem(k, 4)
    return dx, dz, dy


def peer(blk, seq, position, sign, swap=True):
    dx, dz, dy = step_of(position)
    x, z, y = lax.div(blk, 16), lax.rem(lax.div(blk, 4), 4), lax.rem(blk, 4)
    x = lax.rem(x + dx, 2)
    z = lax.rem(z + 4 + sign * dz, 4)
    y = lax.rem(y + 4 + sign * dy, 4)
    other = 2 * dx * (1 - lax.rem(dy + dz, 2)) if swap else 0
    return lax.rem(seq + other, 4), (x * 4 + z) * 4 + y


def experts_kernel(
    resid_ref,
    gain_ref,
    router_ref,
    routes_ref,
    pages_ref,
    gate_up_hbm,
    down_hbm,
    out_ref,
    kv_ref,
    normed,
    rank,
    gates,
    packed,
    recv,
    sent,
    ret,
    hidden,
    gate_up,
    down,
    total,
    weight_sems,
    kv_local_sem,
    out_send,
    out_recv,
    back_send,
    back_recv,
    kv_send,
    kv_recv,
):
    blk = lax.axis_index("blk")
    seq = lax.axis_index("seq")
    load_gate_up = pltpu.make_async_copy(gate_up_hbm, gate_up, weight_sems.at[0])
    load_down = pltpu.make_async_copy(down_hbm, down, weight_sems.at[1])
    load_gate_up.start()
    load_down.start()

    barrier = pltpu.get_barrier_semaphore()

    def greet(j, _):
        pl.semaphore_signal(
            barrier, inc=1, device_id=peer(blk, seq, j, 1), device_id_type=MESH
        )
        return 0

    lax.fori_loop(1, NPOS, greet, 0)

    def greet_swapped(i, _):
        z, y = lax.div(i, 2), lax.rem(i, 2) * 2 + lax.rem(lax.div(i, 2), 2)
        far = (lax.rem(lax.div(blk, 16) + 1, 2)) * 16
        far = far + lax.rem(lax.rem(lax.div(blk, 4), 4) + z, 4) * 4
        far = far + lax.rem(lax.rem(blk, 4) + y, 4)
        pl.semaphore_signal(
            barrier, inc=1, device_id=(seq, far), device_id_type=MESH
        )
        return 0

    lax.fori_loop(0, 8, greet_swapped, 0)

    wide = resid_ref[...].astype(jnp.float32)
    scale = lax.rsqrt(jnp.mean(wide * wide, axis=-1, keepdims=True) + EPS)
    normed[...] = (wide * scale * gain_ref[...].astype(jnp.float32)).astype(jnp.bfloat16)

    tokens = routes_ref.shape[1]
    place = lax.broadcasted_iota(jnp.int32, (NPOS, 1), 0)
    dx, dz, dy = step_of(place)
    expert = lax.rem(lax.div(blk, 16) + dx, 2) * 16
    expert = expert + lax.rem(lax.rem(lax.div(blk, 4), 4) + dz, 4) * 4
    expert = expert + lax.rem(lax.rem(blk, 4) + dy, 4)
    chosen = jnp.zeros((NPOS, tokens), jnp.int32)
    for k in range(routes_ref.shape[0]):
        chosen = jnp.where(routes_ref[k : k + 1, :] == expert, 1, chosen)
    upto = lax.broadcasted_iota(jnp.int32, (tokens, tokens), 0) <= lax.broadcasted_iota(
        jnp.int32, (tokens, tokens), 1
    )
    count = jnp.dot(
        chosen.astype(jnp.bfloat16),
        jnp.where(upto, 1.0, 0.0).astype(jnp.bfloat16),
        preferred_element_type=jnp.float32,
    ).astype(jnp.int32)
    rank[...] = jnp.where(chosen == 1, count - 1, -1)

    slot = lax.broadcasted_iota(jnp.int32, (GRP, CAP, tokens), 1)

    def hits(g):
        rows = rank[pl.ds(pl.multiple_of(g * GRP, GRP), GRP), :]
        return rows[:, None, :] == slot

    def slab(j):
        return pl.ds(pl.multiple_of(j * CAP, CAP), CAP)

    def dispatch(j):
        return pltpu.make_async_remote_copy(
            src_ref=packed.at[slab(j)],
            dst_ref=recv.at[slab(j)],
            send_sem=out_send.at[j],
            recv_sem=out_recv.at[j],
            device_id=peer(blk, seq, j, 1),
            device_id_type=MESH,
        )

    def give_back(j):
        return pltpu.make_async_remote_copy(
            src_ref=sent.at[slab(j)],
            dst_ref=ret.at[slab(j)],
            send_sem=back_send.at[j],
            recv_sem=back_recv.at[j],
            device_id=peer(blk, seq, j, -1),
            device_id_type=MESH,
        )

    def page_copy(j):
        to_seq, to_blk = peer(blk, seq, j, 1, swap=False)
        return pltpu.make_async_remote_copy(
            src_ref=pages_ref.at[to_blk],
            dst_ref=kv_ref.at[blk],
            send_sem=kv_send.at[j],
            recv_sem=kv_recv.at[j],
            device_id=(to_seq, to_blk),
            device_id_type=MESH,
        )

    def page_arrival(j):
        to_seq, from_blk = peer(blk, seq, j, -1, swap=False)
        return pltpu.make_async_remote_copy(
            src_ref=pages_ref.at[from_blk],
            dst_ref=kv_ref.at[from_blk],
            send_sem=kv_send.at[j],
            recv_sem=kv_recv.at[j],
            device_id=(to_seq, from_blk),
            device_id_type=MESH,
        )

    def pack(g):
        one_hot = jnp.where(hits(g), 1.0, 0.0).reshape(ROWS, tokens).astype(jnp.bfloat16)
        rows = pl.ds(pl.multiple_of(g * ROWS, ROWS), ROWS)

        @pl.loop(0, normed.shape[1] // 512)
        def _(n):
            cols = pl.ds(pl.multiple_of(n * 512, 512), 512)
            packed[rows, cols] = jnp.dot(
                one_hot, normed[:, cols], preferred_element_type=jnp.float32
            ).astype(jnp.bfloat16)

    pack(0)
    pl.semaphore_wait(barrier, NPOS - 1 + 8)
    recv[0:CAP, :] = packed[0:CAP, :]

    for g in range(NGRP):
        if g > 0:
            pack(g)
        lax.fori_loop(max(g * GRP, 1), (g + 1) * GRP, lambda j, _: (dispatch(j).start(), 0)[1], 0)

    own_page = pltpu.make_async_copy(pages_ref.at[blk], kv_ref.at[blk], kv_local_sem)
    own_page.start()
    lax.fori_loop(1, NPOS, lambda j, _: (page_copy(j).start(), 0)[1], 0)

    logits = jnp.dot(normed[...], router_ref[...], preferred_element_type=jnp.float32)
    by_expert = jax.nn.sigmoid(logits).astype(jnp.bfloat16)
    order = jnp.where(
        expert == lax.broadcasted_iota(jnp.int32, (NPOS, NPOS), 1), 1.0, 0.0
    ).astype(jnp.bfloat16)
    gates[...] = lax.dot_general(
        order, by_expert, (((1,), (1,)), ((), ())), preferred_element_type=jnp.float32
    )

    load_gate_up.wait()
    load_down.wait()
    ff = down.shape[0]
    width = down.shape[1]

    @pl.loop(0, NGRP)
    def _(g):
        first = jnp.where(g == 0, 1, g * GRP)
        lax.fori_loop(first, (g + 1) * GRP, lambda j, _: (dispatch(j).wait_recv(), 0)[1], 0)
        rows = pl.ds(pl.multiple_of(g * ROWS, ROWS), ROWS)

        @pl.loop(0, ff // TILE)
        def _(f):
            cols = pl.ds(pl.multiple_of(f * TILE, TILE), TILE)
            up_cols = pl.ds(pl.multiple_of(ff + f * TILE, TILE), TILE)
            gate = jnp.dot(recv[rows, :], gate_up[:, cols], preferred_element_type=jnp.float32)
            up = jnp.dot(recv[rows, :], gate_up[:, up_cols], preferred_element_type=jnp.float32)
            hidden[:, cols] = (jax.nn.silu(gate) * up).astype(jnp.bfloat16)

        @pl.loop(0, width // TILE)
        def _(n):
            cols = pl.ds(pl.multiple_of(n * TILE, TILE), TILE)
            sent[rows, cols] = jnp.dot(
                hidden[...], down[:, cols], preferred_element_type=jnp.float32
            ).astype(jnp.bfloat16)

        lax.fori_loop(first, (g + 1) * GRP, lambda j, _: (give_back(j).start(), 0)[1], 0)

    ret[0:CAP, :] = sent[0:CAP, :]
    total[...] = resid_ref[...].astype(jnp.float32)

    @pl.loop(0, NGRP)
    def _(g):
        first = jnp.where(g == 0, 1, g * GRP)
        weight = gates[pl.ds(pl.multiple_of(g * GRP, GRP), GRP), :]
        spread = jnp.where(hits(g), weight[:, None, :], 0.0).reshape(ROWS, tokens)
        spread = spread.T.astype(jnp.bfloat16)
        lax.fori_loop(first, (g + 1) * GRP, lambda j, _: (give_back(j).wait_recv(), 0)[1], 0)
        rows = pl.ds(pl.multiple_of(g * ROWS, ROWS), ROWS)

        @pl.loop(0, width // 512)
        def _(n):
            cols = pl.ds(pl.multiple_of(n * 512, 512), 512)
            total[:, cols] += jnp.dot(spread, ret[rows, cols], preferred_element_type=jnp.float32)

    out_ref[...] = total[...].astype(jnp.bfloat16)

    def drain(j, _):
        page_arrival(j).wait_recv()
        page_copy(j).wait_send()
        dispatch(j).wait_send()
        give_back(j).wait_send()
        return 0

    lax.fori_loop(1, NPOS, drain, 0)
    own_page.wait()


def experts(resid, ffn_gain, w_router, routes, pages, gate_up, down):
    tokens, width = resid.shape
    slots = NPOS * CAP
    vmem = pl.BlockSpec(memory_space=pltpu.VMEM)
    hbm = pl.BlockSpec(memory_space=pl.ANY)
    dma = pltpu.SemaphoreType.DMA
    return pl.pallas_call(
        experts_kernel,
        out_shape=(
            jax.ShapeDtypeStruct((tokens, width), jnp.bfloat16),
            jax.ShapeDtypeStruct(pages.shape, jnp.bfloat16),
        ),
        in_specs=[vmem] * 5 + [hbm] * 2,
        out_specs=(vmem, vmem),
        scratch_shapes=[
            pltpu.VMEM((tokens, width), jnp.bfloat16),
            pltpu.VMEM((NPOS, tokens), jnp.int32),
            pltpu.VMEM((NPOS, tokens), jnp.float32),
            pltpu.VMEM((slots, width), jnp.bfloat16),
            pltpu.VMEM((slots, width), jnp.bfloat16),
            pltpu.VMEM((slots, width), jnp.bfloat16),
            pltpu.VMEM((slots, width), jnp.bfloat16),
            pltpu.VMEM((ROWS, down.shape[0]), jnp.bfloat16),
            pltpu.VMEM(gate_up.shape, jnp.bfloat16),
            pltpu.VMEM(down.shape, jnp.bfloat16),
            pltpu.VMEM((tokens, width), jnp.float32),
            dma((2,)),
            dma,
            dma((NPOS,)),
            dma((NPOS,)),
            dma((NPOS,)),
            dma((NPOS,)),
            dma((NPOS,)),
            dma((NPOS,)),
        ],
        compiler_params=pltpu.CompilerParams(
            collective_id=0, has_side_effects=True, vmem_limit_bytes=58 << 20
        ),
        cost_estimate=pl.CostEstimate(
            flops=2 * slots * 3 * down.shape[0] * width,
            bytes_accessed=16 << 20,
            transcendentals=slots * down.shape[0],
        ),
    )(resid, ffn_gain.reshape(1, width), w_router, routes.T, pages, gate_up, down)


def on_device(
    residual_in,
    segment_ids,
    attn_gain,
    w_qkv,
    w_out,
    ffn_gain,
    w_router,
    routes,
    w_gate_up,
    w_down,
    page_owner,
):
    local_rows = residual_in[0]
    tok_dev = local_rows.shape[0]
    heads_here = w_qkv.shape[1]
    head_dim = w_out.shape[1]
    blk_count = lax.axis_size("blk")
    normed = rms_norm(local_rows, attn_gain)
    w_flat = w_qkv.reshape(w_qkv.shape[0], heads_here * 3 * head_dim)
    qkv = jnp.dot(
        lax.all_gather(normed, "seq", axis=0, tiled=True),
        w_flat,
        preferred_element_type=jnp.float32,
    ).astype(jnp.bfloat16)
    group_len = qkv.shape[0]
    qkv = qkv.reshape(group_len, heads_here, 3 * head_dim)
    query = qkv[:, :, :head_dim]
    key_rows = qkv[:, :, head_dim : 2 * head_dim]
    value_rows = qkv[:, :, 2 * head_dim :]
    scores = jnp.einsum(
        "qhd,khd->hqk", query, key_rows, preferred_element_type=jnp.float32
    ) / math.sqrt(head_dim)
    segment_row = segment_ids[0]
    same = segment_row[:, None] == segment_row[None, :]
    scores = jnp.where(same[None], scores, jnp.float32(-1e30))
    top = jnp.max(scores, axis=-1, keepdims=True)
    weights = jnp.exp(scores - top)
    probs = (weights / jnp.sum(weights, axis=-1, keepdims=True)).astype(jnp.bfloat16)
    context = jnp.einsum(
        "hqk,khd->qhd", probs, value_rows, preferred_element_type=jnp.float32
    ).astype(jnp.bfloat16)
    context_flat = context.reshape(group_len, heads_here * head_dim)
    w_out_flat = w_out.reshape(heads_here * head_dim, w_out.shape[2])
    mixed = lax.psum_scatter(
        jnp.dot(context_flat, w_out_flat, preferred_element_type=jnp.float32).astype(jnp.bfloat16),
        "seq",
        scatter_dimension=0,
        tiled=True,
    ).astype(jnp.float32)
    resid = (local_rows.astype(jnp.float32) + mixed).astype(jnp.bfloat16)
    kv_rows = qkv[:, :, head_dim:].reshape(group_len, heads_here * 2 * head_dim)
    page_len = group_len // blk_count
    pages = kv_rows.reshape(blk_count, page_len, kv_rows.shape[1])
    owners = page_owner[0]
    places = jnp.arange(blk_count, dtype=jnp.int32)
    match = owners[None, :] == places[:, None]
    source_page = jnp.sum(jnp.where(match, places[None, :], 0), axis=1)
    outgoing = jnp.take(pages, source_page, axis=0)
    residual_out, arrived = experts(
        resid, ffn_gain, w_router, routes[0], outgoing, w_gate_up[0], w_down[0]
    )
    return (residual_out[None], arrived[None])


def solution(mesh):
    in_specs = (
        P("blk", "seq", None),
        P("blk", None),
        P(),
        P(None, "seq", None),
        P("seq", None, None),
        P(),
        P(),
        P("blk", "seq", None),
        P("blk", None, None),
        P("blk", None, None),
        P("blk", None),
    )
    out_specs = (P("blk", "seq", None), P("blk", None, None, "seq"))
    return jax.shard_map(
        on_device, mesh=mesh, in_specs=in_specs, out_specs=out_specs, check_vma=False
    )
```

```python
import math

import jax
import jax.numpy as jnp
from jax import lax
from jax.experimental import pallas as pl
from jax.experimental.pallas import tpu as pltpu
from jax.sharding import PartitionSpec as P

EPS = 1e-06
NPOS = 32
CAP = 48
GRP = 8
NGRP = NPOS // GRP
ROWS = GRP * CAP
TILE = 256
HEAD = 128
PARTS = 4
SPAN = 512
MESH = pl.DeviceIdType.MESH


def step_of(position):
    k = lax.rem(position * 3, NPOS)
    dx, dz, dy = lax.div(k, 16), lax.rem(lax.div(k, 4), 4), lax.rem(k, 4)
    return dx, dz, dy


def peer(blk, seq, position, sign, swap=True):
    dx, dz, dy = step_of(position)
    x, z, y = lax.div(blk, 16), lax.rem(lax.div(blk, 4), 4), lax.rem(blk, 4)
    x = lax.rem(x + dx, 2)
    z = lax.rem(z + 4 + sign * dz, 4)
    y = lax.rem(y + 4 + sign * dy, 4)
    other = 2 * dx * (1 - lax.rem(dy + dz, 2)) if swap else 0
    return lax.rem(seq + other, 4), (x * 4 + z) * 4 + y


def layer_kernel(
    rows_ref,
    segment_ref,
    owner_ref,
    attn_gain_ref,
    ffn_gain_ref,
    router_ref,
    routes_ref,
    qkv_hbm,
    out_hbm,
    gate_up_hbm,
    down_hbm,
    out_ref,
    kv_ref,
    queries,
    keys_values,
    pages_ref,
    context,
    partial,
    near_send,
    near_recv,
    far_send,
    far_recv,
    resid,
    normed,
    rank,
    gates,
    packed,
    recv,
    sent,
    ret,
    hidden,
    gate_up,
    down,
    total,
    weight_sems,
    kv_local_sem,
    out_send,
    out_recv,
    back_send,
    back_recv,
    kv_send,
    kv_recv,
    own_sems,
    gather_send,
    gather_recv,
    pass_send,
    pass_recv,
    near_send_sems,
    near_recv_sems,
    far_send_sems,
    far_recv_sems,
):
    blk = lax.axis_index("blk")
    seq = lax.axis_index("seq")
    half = lax.div(seq, 2)
    core = lax.rem(seq, 2)
    mate = seq + 1 - 2 * core
    far = lax.rem(seq + 2, 4)
    tok = rows_ref.shape[0]
    width = rows_ref.shape[1]
    length = 4 * tok
    heads = out_hbm.shape[0] // HEAD
    w_qkv = sent.at[0:width, 0 : qkv_hbm.shape[1]]
    w_out = packed.at[0 : out_hbm.shape[0]]
    everyone = packed.at[out_hbm.shape[0] : out_hbm.shape[0] + length]
    load_qkv = pltpu.make_async_copy(qkv_hbm, w_qkv, weight_sems.at[2])
    load_out = pltpu.make_async_copy(out_hbm, w_out, weight_sems.at[3])
    load_gate_up = pltpu.make_async_copy(gate_up_hbm, gate_up, weight_sems.at[0])
    load_down = pltpu.make_async_copy(down_hbm, down, weight_sems.at[1])
    load_qkv.start()
    load_out.start()

    barrier = pltpu.get_barrier_semaphore()

    def greet(j, _):
        pl.semaphore_signal(
            barrier, inc=1, device_id=peer(blk, seq, j, 1), device_id_type=MESH
        )
        return 0

    lax.fori_loop(1, NPOS, greet, 0)

    def greet_swapped(i, _):
        z, y = lax.div(i, 2), lax.rem(i, 2) * 2 + lax.rem(lax.div(i, 2), 2)
        there = (lax.rem(lax.div(blk, 16) + 1, 2)) * 16
        there = there + lax.rem(lax.rem(lax.div(blk, 4), 4) + z, 4) * 4
        there = there + lax.rem(lax.rem(blk, 4) + y, 4)
        pl.semaphore_signal(
            barrier, inc=1, device_id=(seq, there), device_id_type=MESH
        )
        return 0

    lax.fori_loop(0, 8, greet_swapped, 0)
    for other in (mate, far):
        pl.semaphore_signal(barrier, inc=1, device_id=(other, blk), device_id_type=MESH)

    def block(index):
        return pl.ds(pl.multiple_of(index * tok, tok), tok)

    def norm(wide, gain_ref):
        scale = lax.rsqrt(jnp.mean(wide * wide, axis=-1, keepdims=True) + EPS)
        return (wide * scale * gain_ref[...].astype(jnp.float32)).astype(jnp.bfloat16)

    def send(src, dst, send_sem, recv_sem, to):
        return pltpu.make_async_remote_copy(
            src_ref=src,
            dst_ref=dst,
            send_sem=send_sem,
            recv_sem=recv_sem,
            device_id=(to, blk),
            device_id_type=MESH,
        )

    def piece(index, i):
        rows = tok // PARTS
        return everyone.at[pl.ds(pl.multiple_of(index * tok + i * rows, rows), rows)]

    everyone[block(seq), :] = norm(rows_ref[...].astype(jnp.float32), attn_gain_ref)
    pl.semaphore_wait(barrier, NPOS - 1 + 8 + 2)

    own_out = send(
        everyone.at[block(seq)], everyone.at[block(seq)], own_sems.at[0], own_sems.at[1], mate
    )
    own_in = send(
        everyone.at[block(mate)], everyone.at[block(mate)], own_sems.at[0], own_sems.at[1], mate
    )
    gather_out = [
        send(piece(seq, i), piece(seq, i), gather_send.at[i], gather_recv.at[i], far)
        for i in range(PARTS)
    ]
    gather_in = [
        send(piece(far, i), piece(far, i), gather_send.at[i], gather_recv.at[i], far)
        for i in range(PARTS)
    ]
    far_mate = lax.rem(mate + 2, 4)
    pass_out = [
        send(piece(far, i), piece(far, i), pass_send.at[i], pass_recv.at[i], mate)
        for i in range(PARTS)
    ]
    pass_in = [
        send(piece(far_mate, i), piece(far_mate, i), pass_send.at[i], pass_recv.at[i], mate)
        for i in range(PARTS)
    ]
    for copy in gather_out:
        copy.start()
    own_out.start()

    def two_blocks(index):
        return pl.ds(pl.multiple_of(index * 2 * tok, 2 * tok), 2 * tok)

    def project(index):
        rows = two_blocks(index)

        @pl.loop(0, heads // 2)
        def _(p):
            cols = pl.ds(pl.multiple_of(p * 6 * HEAD, 6 * HEAD), 6 * HEAD)
            both = jnp.dot(
                everyone[rows, :], w_qkv[:, cols], preferred_element_type=jnp.float32
            ).astype(jnp.bfloat16)
            q_cols = pl.ds(pl.multiple_of(p * 2 * HEAD, 2 * HEAD), 2 * HEAD)
            kv_cols = pl.ds(pl.multiple_of(p * 4 * HEAD, 4 * HEAD), 4 * HEAD)
            queries[rows, q_cols] = jnp.concatenate(
                [both[:, 0:HEAD], both[:, 3 * HEAD : 4 * HEAD]], axis=1
            )
            keys_values[rows, kv_cols] = jnp.concatenate(
                [both[:, HEAD : 3 * HEAD], both[:, 4 * HEAD :]], axis=1
            )

    load_qkv.wait()
    load_out.wait()
    load_gate_up.start()
    load_down.start()
    own_in.wait_recv()
    project(half)
    for i in range(PARTS):
        gather_in[i].wait_recv()
        pass_out[i].start()
    for i in range(PARTS):
        pass_in[i].wait_recv()
    project(1 - half)

    def page_copy(j):
        to_seq, to_blk = peer(blk, seq, j, 1, swap=False)
        return pltpu.make_async_remote_copy(
            src_ref=pages_ref.at[to_blk],
            dst_ref=kv_ref.at[blk],
            send_sem=kv_send.at[j],
            recv_sem=kv_recv.at[j],
            device_id=(to_seq, to_blk),
            device_id_type=MESH,
        )

    def page_arrival(j):
        to_seq, from_blk = peer(blk, seq, j, -1, swap=False)
        return pltpu.make_async_remote_copy(
            src_ref=pages_ref.at[from_blk],
            dst_ref=kv_ref.at[from_blk],
            send_sem=kv_send.at[j],
            recv_sem=kv_recv.at[j],
            device_id=(to_seq, from_blk),
            device_id_type=MESH,
        )

    page = length // NPOS
    to_row = lax.broadcasted_iota(jnp.int32, (length, length), 0)
    from_row = lax.broadcasted_iota(jnp.int32, (length, length), 1)
    moves = (lax.rem(to_row, page) == lax.rem(from_row, page)) & (
        lax.div(to_row, page) == owner_ref[...]
    )
    pages_ref[...] = (
        jnp.dot(
            jnp.where(moves, 1.0, 0.0).astype(jnp.bfloat16),
            keys_values[...],
            preferred_element_type=jnp.float32,
        )
        .astype(jnp.bfloat16)
        .reshape(pages_ref.shape)
    )
    own_page = pltpu.make_async_copy(pages_ref.at[blk], kv_ref.at[blk], kv_local_sem)
    own_page.start()
    lax.fori_loop(1, NPOS, lambda j, _: (page_copy(j).start(), 0)[1], 0)

    segment_row = segment_ref[...]
    segment_column = jnp.broadcast_to(segment_row, (HEAD, length)).T

    def attend(index):
        rows = two_blocks(index)
        picked = jnp.where(index == 0, segment_column[0 : 2 * tok], segment_column[2 * tok :])
        same = picked[:, 0:1] == segment_row

        @pl.loop(0, heads)
        def _(head):
            cols = pl.ds(pl.multiple_of(head * HEAD, HEAD), HEAD)
            k_cols = pl.ds(pl.multiple_of(head * 2 * HEAD, HEAD), HEAD)
            v_cols = pl.ds(pl.multiple_of(head * 2 * HEAD + HEAD, HEAD), HEAD)
            scores = lax.dot_general(
                queries[rows, cols],
                keys_values[:, k_cols],
                (((1,), (1,)), ((), ())),
                preferred_element_type=jnp.float32,
            ) * (1.0 / math.sqrt(HEAD))
            scores = jnp.where(same, scores, -1e30)
            weights = jnp.exp(scores - jnp.max(scores, axis=-1, keepdims=True))
            probs = (weights / jnp.sum(weights, axis=-1, keepdims=True)).astype(jnp.bfloat16)
            context[rows, cols] = jnp.dot(
                probs, keys_values[:, v_cols], preferred_element_type=jnp.float32
            ).astype(jnp.bfloat16)

    def column(n):
        return pl.ds(n * SPAN, SPAN)

    def near_copy(which, n):
        return send(
            near_send.at[which, :, column(n)],
            near_recv.at[which, :, column(n)],
            near_send_sems.at[which, n],
            near_recv_sems.at[which, n],
            mate,
        )

    def far_copy(n):
        return send(
            far_send.at[:, column(n)],
            far_recv.at[:, column(n)],
            far_send_sems.at[n],
            far_recv_sems.at[n],
            far,
        )

    def mix(which, index):
        for n in range(width // SPAN):
            partial[:, column(n)] = jnp.dot(
                context[two_blocks(index), :],
                w_out[:, column(n)],
                preferred_element_type=jnp.float32,
            )
            near_send[which, :, column(n)] = partial[block(1 - core), column(n)].astype(
                jnp.bfloat16
            )
            near_copy(which, n).start()

    def reduced(which, n):
        near_copy(which, n).wait_recv()
        return partial[block(core), column(n)] + near_recv[which, :, column(n)].astype(
            jnp.float32
        )

    attend(1 - half)
    mix(0, 1 - half)
    for n in range(width // SPAN):
        far_send[:, column(n)] = reduced(0, n).astype(jnp.bfloat16)
        far_copy(n).start()
    attend(half)
    mix(1, half)
    for n in range(width // SPAN):
        mixed = reduced(1, n)
        far_copy(n).wait_recv()
        mixed = mixed + far_recv[:, column(n)].astype(jnp.float32)
        resid[:, column(n)] = (rows_ref[:, column(n)].astype(jnp.float32) + mixed).astype(
            jnp.bfloat16
        )
    normed[...] = norm(resid[...].astype(jnp.float32), ffn_gain_ref)
    own_out.wait_send()
    for i in range(PARTS):
        gather_out[i].wait_send()
        pass_out[i].wait_send()

    tokens = tok
    place = lax.broadcasted_iota(jnp.int32, (NPOS, 1), 0)
    dx, dz, dy = step_of(place)
    expert = lax.rem(lax.div(blk, 16) + dx, 2) * 16
    expert = expert + lax.rem(lax.rem(lax.div(blk, 4), 4) + dz, 4) * 4
    expert = expert + lax.rem(lax.rem(blk, 4) + dy, 4)
    chosen = jnp.zeros((NPOS, tokens), jnp.int32)
    for k in range(routes_ref.shape[0]):
        chosen = jnp.where(routes_ref[k : k + 1, :] == expert, 1, chosen)
    upto = lax.broadcasted_iota(jnp.int32, (tokens, tokens), 0) <= lax.broadcasted_iota(
        jnp.int32, (tokens, tokens), 1
    )
    count = jnp.dot(
        chosen.astype(jnp.bfloat16),
        jnp.where(upto, 1.0, 0.0).astype(jnp.bfloat16),
        preferred_element_type=jnp.float32,
    ).astype(jnp.int32)
    rank[...] = jnp.where(chosen == 1, count - 1, -1)

    slot = lax.broadcasted_iota(jnp.int32, (GRP, CAP, tokens), 1)

    def hits(g):
        rows = rank[pl.ds(pl.multiple_of(g * GRP, GRP), GRP), :]
        return rows[:, None, :] == slot

    def slab(j):
        return pl.ds(pl.multiple_of(j * CAP, CAP), CAP)

    def dispatch(j):
        return pltpu.make_async_remote_copy(
            src_ref=packed.at[slab(j)],
            dst_ref=recv.at[slab(j)],
            send_sem=out_send.at[j],
            recv_sem=out_recv.at[j],
            device_id=peer(blk, seq, j, 1),
            device_id_type=MESH,
        )

    def give_back(j):
        return pltpu.make_async_remote_copy(
            src_ref=sent.at[slab(j)],
            dst_ref=ret.at[slab(j)],
            send_sem=back_send.at[j],
            recv_sem=back_recv.at[j],
            device_id=peer(blk, seq, j, -1),
            device_id_type=MESH,
        )

    def pack(g):
        one_hot = jnp.where(hits(g), 1.0, 0.0).reshape(ROWS, tokens).astype(jnp.bfloat16)
        rows = pl.ds(pl.multiple_of(g * ROWS, ROWS), ROWS)

        @pl.loop(0, normed.shape[1] // 512)
        def _(n):
            cols = pl.ds(pl.multiple_of(n * 512, 512), 512)
            packed[rows, cols] = jnp.dot(
                one_hot, normed[:, cols], preferred_element_type=jnp.float32
            ).astype(jnp.bfloat16)

    pack(0)
    recv[0:CAP, :] = packed[0:CAP, :]

    for g in range(NGRP):
        if g > 0:
            pack(g)
        lax.fori_loop(max(g * GRP, 1), (g + 1) * GRP, lambda j, _: (dispatch(j).start(), 0)[1], 0)

    logits = jnp.dot(normed[...], router_ref[...], preferred_element_type=jnp.float32)
    by_expert = jax.nn.sigmoid(logits).astype(jnp.bfloat16)
    order = jnp.where(
        expert == lax.broadcasted_iota(jnp.int32, (NPOS, NPOS), 1), 1.0, 0.0
    ).astype(jnp.bfloat16)
    gates[...] = lax.dot_general(
        order, by_expert, (((1,), (1,)), ((), ())), preferred_element_type=jnp.float32
    )

    load_gate_up.wait()
    load_down.wait()
    ff = down.shape[0]

    @pl.loop(0, NGRP)
    def _(g):
        first = jnp.where(g == 0, 1, g * GRP)
        lax.fori_loop(first, (g + 1) * GRP, lambda j, _: (dispatch(j).wait_recv(), 0)[1], 0)
        rows = pl.ds(pl.multiple_of(g * ROWS, ROWS), ROWS)

        @pl.loop(0, ff // TILE)
        def _(f):
            cols = pl.ds(pl.multiple_of(f * TILE, TILE), TILE)
            up_cols = pl.ds(pl.multiple_of(ff + f * TILE, TILE), TILE)
            gate = jnp.dot(recv[rows, :], gate_up[:, cols], preferred_element_type=jnp.float32)
            up = jnp.dot(recv[rows, :], gate_up[:, up_cols], preferred_element_type=jnp.float32)
            hidden[:, cols] = (jax.nn.silu(gate) * up).astype(jnp.bfloat16)

        @pl.loop(0, width // TILE)
        def _(n):
            cols = pl.ds(pl.multiple_of(n * TILE, TILE), TILE)
            sent[rows, cols] = jnp.dot(
                hidden[...], down[:, cols], preferred_element_type=jnp.float32
            ).astype(jnp.bfloat16)

        lax.fori_loop(first, (g + 1) * GRP, lambda j, _: (give_back(j).start(), 0)[1], 0)

    ret[0:CAP, :] = sent[0:CAP, :]
    total[...] = resid[...].astype(jnp.float32)

    @pl.loop(0, NGRP)
    def _(g):
        first = jnp.where(g == 0, 1, g * GRP)
        weight = gates[pl.ds(pl.multiple_of(g * GRP, GRP), GRP), :]
        spread = jnp.where(hits(g), weight[:, None, :], 0.0).reshape(ROWS, tokens)
        spread = spread.T.astype(jnp.bfloat16)
        lax.fori_loop(first, (g + 1) * GRP, lambda j, _: (give_back(j).wait_recv(), 0)[1], 0)
        rows = pl.ds(pl.multiple_of(g * ROWS, ROWS), ROWS)

        @pl.loop(0, width // 512)
        def _(n):
            cols = pl.ds(pl.multiple_of(n * 512, 512), 512)
            total[:, cols] += jnp.dot(spread, ret[rows, cols], preferred_element_type=jnp.float32)

    out_ref[...] = total[...].astype(jnp.bfloat16)

    def drain(j, _):
        page_arrival(j).wait_recv()
        page_copy(j).wait_send()
        dispatch(j).wait_send()
        give_back(j).wait_send()
        return 0

    lax.fori_loop(1, NPOS, drain, 0)
    own_page.wait()
    for n in range(width // SPAN):
        near_copy(0, n).wait_send()
        near_copy(1, n).wait_send()
        far_copy(n).wait_send()


def on_device(
    residual_in,
    segment_ids,
    attn_gain,
    w_qkv,
    w_out,
    ffn_gain,
    w_router,
    routes,
    w_gate_up,
    w_down,
    page_owner,
):
    tokens, width = residual_in.shape[1:]
    heads = w_qkv.shape[1]
    length = segment_ids.shape[1]
    page = length // NPOS
    ff = w_down.shape[1]
    slots = NPOS * CAP
    vmem = pl.BlockSpec(memory_space=pltpu.VMEM)
    hbm = pl.BlockSpec(memory_space=pl.ANY)
    dma = pltpu.SemaphoreType.DMA
    bf16 = jnp.bfloat16
    spans = width // SPAN
    residual_out, kv_cache = pl.pallas_call(
        layer_kernel,
        out_shape=(
            jax.ShapeDtypeStruct((tokens, width), bf16),
            jax.ShapeDtypeStruct((NPOS, page, heads * 2 * HEAD), bf16),
        ),
        in_specs=[vmem] * 7 + [hbm] * 4,
        out_specs=(vmem, vmem),
        scratch_shapes=[
            pltpu.VMEM((length, heads * HEAD), bf16),
            pltpu.VMEM((length, heads * 2 * HEAD), bf16),
            pltpu.VMEM((NPOS, page, heads * 2 * HEAD), bf16),
            pltpu.VMEM((length, heads * HEAD), bf16),
            pltpu.VMEM((2 * tokens, width), jnp.float32),
            pltpu.VMEM((2, tokens, width), bf16),
            pltpu.VMEM((2, tokens, width), bf16),
            pltpu.VMEM((tokens, width), bf16),
            pltpu.VMEM((tokens, width), bf16),
            pltpu.VMEM((tokens, width), bf16),
            pltpu.VMEM((tokens, width), bf16),
            pltpu.VMEM((NPOS, tokens), jnp.int32),
            pltpu.VMEM((NPOS, tokens), jnp.float32),
            pltpu.VMEM((slots, width), bf16),
            pltpu.VMEM((slots, width), bf16),
            pltpu.VMEM((max(slots, width), width), bf16),
            pltpu.VMEM((slots, width), bf16),
            pltpu.VMEM((ROWS, ff), bf16),
            pltpu.VMEM((width, 2 * ff), bf16),
            pltpu.VMEM((ff, width), bf16),
            pltpu.VMEM((tokens, width), jnp.float32),
            dma((4,)),
            dma,
            dma((NPOS,)),
            dma((NPOS,)),
            dma((NPOS,)),
            dma((NPOS,)),
            dma((NPOS,)),
            dma((NPOS,)),
            dma((2,)),
            dma((PARTS,)),
            dma((PARTS,)),
            dma((PARTS,)),
            dma((PARTS,)),
            dma((2, spans)),
            dma((2, spans)),
            dma((spans,)),
            dma((spans,)),
        ],
        compiler_params=pltpu.CompilerParams(
            collective_id=0, has_side_effects=True, vmem_limit_bytes=60 << 20
        ),
    )(
        residual_in[0],
        segment_ids,
        jnp.repeat(page_owner, page, axis=1),
        attn_gain.reshape(1, width),
        ffn_gain.reshape(1, width),
        w_router,
        routes[0].T,
        w_qkv.reshape(width, heads * 3 * HEAD),
        w_out.reshape(heads * HEAD, width),
        w_gate_up[0],
        w_down[0],
    )
    return (residual_out[None], kv_cache[None])


def solution(mesh):
    in_specs = (
        P("blk", "seq", None),
        P("blk", None),
        P(),
        P(None, "seq", None),
        P("seq", None, None),
        P(),
        P(),
        P("blk", "seq", None),
        P("blk", None, None),
        P("blk", None, None),
        P("blk", None),
    )
    out_specs = (P("blk", "seq", None), P("blk", None, None, "seq"))
    return jax.shard_map(
        on_device, mesh=mesh, in_specs=in_specs, out_specs=out_specs, check_vma=False
    )
```

```python
import math

import jax
import jax.numpy as jnp
from jax import lax
from jax.experimental import pallas as pl
from jax.experimental.pallas import tpu as pltpu
from jax.sharding import PartitionSpec as P

EPS = 1e-06
NPOS = 32
CAP = 48
SUB = 16
NGRP = CAP // SUB
ROWS = NPOS * SUB
TILE = 256
HEAD = 128
PARTS = 4
SPAN = 512
MESH = pl.DeviceIdType.MESH


def step_of(position, core):
    k = lax.rem(position * 3, NPOS)
    dx, dz, dy = lax.div(k, 16), lax.rem(lax.div(k, 4), 4), lax.rem(k, 4)
    return dx, dz + core * (dy - dz), dy + core * (dz - dy)


def place_at(blk, position, core, sign):
    dx, dz, dy = step_of(position, core)
    x, z, y = lax.div(blk, 16), lax.rem(lax.div(blk, 4), 4), lax.rem(blk, 4)
    x = lax.rem(x + dx, 2)
    z = lax.rem(z + 4 + sign * dz, 4)
    y = lax.rem(y + 4 + sign * dy, 4)
    return (x * 4 + z) * 4 + y


def peer(blk, seq, position, sign):
    core = lax.rem(seq, 2)
    dx, dz, dy = step_of(position, core)
    other = 2 * dx * (1 - lax.rem(dy + dz, 2))
    return lax.rem(seq + other, 4), place_at(blk, position, core, sign)


def layer_kernel(
    rows_ref,
    segment_ref,
    owner_ref,
    attn_gain_ref,
    ffn_gain_ref,
    router_ref,
    routes_ref,
    qkv_hbm,
    out_hbm,
    gate_up_hbm,
    down_hbm,
    out_ref,
    kv_ref,
    queries,
    keys_values,
    pages_ref,
    context,
    partial,
    near_send,
    near_recv,
    far_send,
    far_recv,
    resid,
    normed,
    rank,
    gates,
    packed,
    recv,
    sent,
    ret,
    hidden,
    gate_up,
    down,
    total,
    weight_sems,
    kv_local_sem,
    out_send,
    out_recv,
    back_send,
    back_recv,
    kv_send,
    kv_recv,
    own_sems,
    gather_send,
    gather_recv,
    pass_send,
    pass_recv,
    near_send_sems,
    near_recv_sems,
    far_send_sems,
    far_recv_sems,
):
    blk = lax.axis_index("blk")
    seq = lax.axis_index("seq")
    half = lax.div(seq, 2)
    core = lax.rem(seq, 2)
    mate = seq + 1 - 2 * core
    far = lax.rem(seq + 2, 4)
    tok = rows_ref.shape[0]
    width = rows_ref.shape[1]
    length = 4 * tok
    heads = out_hbm.shape[0] // HEAD
    w_qkv = sent.at[0:width, 0 : qkv_hbm.shape[1]]
    w_out = packed.at[0 : out_hbm.shape[0]]
    everyone = packed.at[out_hbm.shape[0] : out_hbm.shape[0] + length]
    load_qkv = pltpu.make_async_copy(qkv_hbm, w_qkv, weight_sems.at[2])
    load_out = pltpu.make_async_copy(out_hbm, w_out, weight_sems.at[3])
    load_gate_up = pltpu.make_async_copy(gate_up_hbm, gate_up, weight_sems.at[0])
    load_down = pltpu.make_async_copy(down_hbm, down, weight_sems.at[1])
    load_qkv.start()
    load_out.start()

    barrier = pltpu.get_barrier_semaphore()

    def greet(j, _):
        pl.semaphore_signal(
            barrier, inc=1, device_id=peer(blk, seq, j, 1), device_id_type=MESH
        )
        return 0

    lax.fori_loop(1, NPOS, greet, 0)

    def greet_swapped(i, _):
        z, y = lax.div(i, 2), lax.rem(i, 2) * 2 + lax.rem(lax.div(i, 2), 2)
        there = (lax.rem(lax.div(blk, 16) + 1, 2)) * 16
        there = there + lax.rem(lax.rem(lax.div(blk, 4), 4) + z, 4) * 4
        there = there + lax.rem(lax.rem(blk, 4) + y, 4)
        pl.semaphore_signal(
            barrier, inc=1, device_id=(seq, there), device_id_type=MESH
        )
        return 0

    lax.fori_loop(0, 8, greet_swapped, 0)
    for other in (mate, far):
        pl.semaphore_signal(barrier, inc=1, device_id=(other, blk), device_id_type=MESH)

    def block(index):
        return pl.ds(pl.multiple_of(index * tok, tok), tok)

    def norm(wide, gain_ref):
        scale = lax.rsqrt(jnp.mean(wide * wide, axis=-1, keepdims=True) + EPS)
        return (wide * scale * gain_ref[...].astype(jnp.float32).reshape(1, width)).astype(jnp.bfloat16)

    def send(src, dst, send_sem, recv_sem, to):
        return pltpu.make_async_remote_copy(
            src_ref=src,
            dst_ref=dst,
            send_sem=send_sem,
            recv_sem=recv_sem,
            device_id=(to, blk),
            device_id_type=MESH,
        )

    def piece(index, i):
        rows = tok // PARTS
        return everyone.at[pl.ds(pl.multiple_of(index * tok + i * rows, rows), rows)]

    everyone[block(seq), :] = norm(rows_ref[...].astype(jnp.float32), attn_gain_ref)
    pl.semaphore_wait(barrier, NPOS - 1 + 8 + 2)

    own_out = send(
        everyone.at[block(seq)], everyone.at[block(seq)], own_sems.at[0], own_sems.at[1], mate
    )
    own_in = send(
        everyone.at[block(mate)], everyone.at[block(mate)], own_sems.at[0], own_sems.at[1], mate
    )
    gather_out = [
        send(piece(seq, i), piece(seq, i), gather_send.at[i], gather_recv.at[i], far)
        for i in range(PARTS)
    ]
    gather_in = [
        send(piece(far, i), piece(far, i), gather_send.at[i], gather_recv.at[i], far)
        for i in range(PARTS)
    ]
    far_mate = lax.rem(mate + 2, 4)
    pass_out = [
        send(piece(far, i), piece(far, i), pass_send.at[i], pass_recv.at[i], mate)
        for i in range(PARTS)
    ]
    pass_in = [
        send(piece(far_mate, i), piece(far_mate, i), pass_send.at[i], pass_recv.at[i], mate)
        for i in range(PARTS)
    ]
    for copy in gather_out:
        copy.start()
    own_out.start()

    def two_blocks(index):
        return pl.ds(pl.multiple_of(index * 2 * tok, 2 * tok), 2 * tok)

    def project(index):
        rows = two_blocks(index)

        @pl.loop(0, heads // 2)
        def _(p):
            cols = pl.ds(pl.multiple_of(p * 6 * HEAD, 6 * HEAD), 6 * HEAD)
            both = jnp.dot(
                everyone[rows, :], w_qkv[:, cols], preferred_element_type=jnp.float32
            ).astype(jnp.bfloat16)
            q_cols = pl.ds(pl.multiple_of(p * 2 * HEAD, 2 * HEAD), 2 * HEAD)
            kv_cols = pl.ds(pl.multiple_of(p * 4 * HEAD, 4 * HEAD), 4 * HEAD)
            queries[rows, q_cols] = jnp.concatenate(
                [both[:, 0:HEAD], both[:, 3 * HEAD : 4 * HEAD]], axis=1
            )
            keys_values[rows, kv_cols] = jnp.concatenate(
                [both[:, HEAD : 3 * HEAD], both[:, 4 * HEAD :]], axis=1
            )

    tokens = tok
    expert = place_at(blk, lax.broadcasted_iota(jnp.int32, (NPOS, 1), 0), core, 1)
    chosen = jnp.zeros((NPOS, tokens), jnp.int32)
    for k in range(routes_ref.shape[0]):
        chosen = jnp.where(routes_ref[k : k + 1, :] == expert, 1, chosen)
    upto = lax.broadcasted_iota(jnp.int32, (tokens, tokens), 0) <= lax.broadcasted_iota(
        jnp.int32, (tokens, tokens), 1
    )
    count = jnp.dot(
        chosen.astype(jnp.bfloat16),
        jnp.where(upto, 1.0, 0.0).astype(jnp.bfloat16),
        preferred_element_type=jnp.float32,
    ).astype(jnp.int32)
    rank[...] = jnp.where(chosen == 1, count - 1, -1)
    slot = lax.broadcasted_iota(jnp.int32, (NPOS, SUB, tokens), 1)

    def hits(g):
        return rank[...][:, None, :] == slot + g * SUB

    segment_row = segment_ref[...]
    segment_column = jnp.broadcast_to(segment_row, (HEAD, length)).T

    load_qkv.wait()
    load_out.wait()
    load_gate_up.start()
    load_down.start()
    own_in.wait_recv()
    project(half)
    for i in range(PARTS):
        gather_in[i].wait_recv()
        pass_out[i].start()
    for i in range(PARTS):
        pass_in[i].wait_recv()
    project(1 - half)

    def page_copy(j):
        to_blk = place_at(blk, j, core, 1)
        return pltpu.make_async_remote_copy(
            src_ref=pages_ref.at[to_blk],
            dst_ref=kv_ref.at[blk],
            send_sem=kv_send.at[j],
            recv_sem=kv_recv.at[j],
            device_id=(seq, to_blk),
            device_id_type=MESH,
        )

    def page_arrival(j):
        from_blk = place_at(blk, j, core, -1)
        return pltpu.make_async_remote_copy(
            src_ref=pages_ref.at[from_blk],
            dst_ref=kv_ref.at[from_blk],
            send_sem=kv_send.at[j],
            recv_sem=kv_recv.at[j],
            device_id=(seq, from_blk),
            device_id_type=MESH,
        )

    def attend(index):
        rows = two_blocks(index)
        picked = jnp.where(index == 0, segment_column[0 : 2 * tok], segment_column[2 * tok :])
        same = picked[:, 0:1] == segment_row

        @pl.loop(0, heads)
        def _(head):
            cols = pl.ds(pl.multiple_of(head * HEAD, HEAD), HEAD)
            k_cols = pl.ds(pl.multiple_of(head * 2 * HEAD, HEAD), HEAD)
            v_cols = pl.ds(pl.multiple_of(head * 2 * HEAD + HEAD, HEAD), HEAD)
            scores = lax.dot_general(
                queries[rows, cols],
                keys_values[:, k_cols],
                (((1,), (1,)), ((), ())),
                preferred_element_type=jnp.float32,
            ) * (1.0 / math.sqrt(HEAD))
            scores = jnp.where(same, scores, -1e30)
            weights = jnp.exp(scores - jnp.max(scores, axis=-1, keepdims=True))
            probs = (weights / jnp.sum(weights, axis=-1, keepdims=True)).astype(jnp.bfloat16)
            context[rows, cols] = jnp.dot(
                probs, keys_values[:, v_cols], preferred_element_type=jnp.float32
            ).astype(jnp.bfloat16)

    def column(n):
        return pl.ds(n * SPAN, SPAN)

    def near_copy(which, n):
        return send(
            near_send.at[which, :, column(n)],
            near_recv.at[which, :, column(n)],
            near_send_sems.at[which, n],
            near_recv_sems.at[which, n],
            mate,
        )

    def far_copy(n):
        return send(
            far_send.at[:, column(n)],
            far_recv.at[:, column(n)],
            far_send_sems.at[n],
            far_recv_sems.at[n],
            far,
        )

    def mix(which, index):
        for n in range(width // SPAN):
            partial[:, column(n)] = jnp.dot(
                context[two_blocks(index), :],
                w_out[:, column(n)],
                preferred_element_type=jnp.float32,
            )
            near_send[which, :, column(n)] = partial[block(1 - core), column(n)].astype(
                jnp.bfloat16
            )
            near_copy(which, n).start()

    def reduced(which, n):
        near_copy(which, n).wait_recv()
        return partial[block(core), column(n)] + near_recv[which, :, column(n)].astype(
            jnp.float32
        )

    attend(1 - half)
    mix(0, 1 - half)
    for n in range(width // SPAN):
        far_send[:, column(n)] = reduced(0, n).astype(jnp.bfloat16)
        far_copy(n).start()
    attend(half)
    mix(1, half)
    page = length // NPOS
    spread_owner = lax.div(
        lax.broadcasted_iota(jnp.int32, (NPOS, length), 1), page
    ) == lax.broadcasted_iota(jnp.int32, (NPOS, length), 0)
    owners = jnp.dot(
        jnp.broadcast_to(owner_ref[...], (8, NPOS)).astype(jnp.bfloat16),
        jnp.where(spread_owner, 1.0, 0.0).astype(jnp.bfloat16),
        preferred_element_type=jnp.float32,
    ).astype(jnp.int32)[0:1]
    to_row = lax.broadcasted_iota(jnp.int32, (length, length), 0)
    from_row = lax.broadcasted_iota(jnp.int32, (length, length), 1)
    moves = (lax.rem(to_row, page) == lax.rem(from_row, page)) & (
        lax.div(to_row, page) == owners
    )
    pages_ref[...] = (
        jnp.dot(
            jnp.where(moves, 1.0, 0.0).astype(jnp.bfloat16),
            keys_values[...],
            preferred_element_type=jnp.float32,
        )
        .astype(jnp.bfloat16)
        .reshape(pages_ref.shape)
    )
    own_page = pltpu.make_async_copy(pages_ref.at[blk], kv_ref.at[blk], kv_local_sem)
    own_page.start()
    lax.fori_loop(1, NPOS, lambda j, _: (page_copy(j).start(), 0)[1], 0)

    for n in range(width // SPAN):
        mixed = reduced(1, n)
        far_copy(n).wait_recv()
        mixed = mixed + far_recv[:, column(n)].astype(jnp.float32)
        resid[:, column(n)] = (rows_ref[:, column(n)].astype(jnp.float32) + mixed).astype(
            jnp.bfloat16
        )
    normed[...] = norm(resid[...].astype(jnp.float32), ffn_gain_ref)
    own_out.wait_send()
    for i in range(PARTS):
        gather_out[i].wait_send()
        pass_out[i].wait_send()

    def slab(g, j):
        return pl.ds(pl.multiple_of(g * ROWS + j * SUB, SUB), SUB)

    def others(g):
        return pl.ds(pl.multiple_of(g * ROWS + SUB, SUB), ROWS - SUB)

    def dispatch(g, j):
        return pltpu.make_async_remote_copy(
            src_ref=packed.at[slab(g, j)],
            dst_ref=recv.at[slab(g, j)],
            send_sem=out_send.at[g],
            recv_sem=out_recv.at[g],
            device_id=peer(blk, seq, j, 1),
            device_id_type=MESH,
        )

    def give_back(g, j):
        return pltpu.make_async_remote_copy(
            src_ref=sent.at[slab(g, j)],
            dst_ref=ret.at[slab(g, j)],
            send_sem=back_send.at[g],
            recv_sem=back_recv.at[g],
            device_id=peer(blk, seq, j, -1),
            device_id_type=MESH,
        )

    def dispatch_all(g):
        return pltpu.make_async_remote_copy(
            src_ref=packed.at[others(g)],
            dst_ref=recv.at[others(g)],
            send_sem=out_send.at[g],
            recv_sem=out_recv.at[g],
            device_id=(mate, blk),
            device_id_type=MESH,
        )

    def give_back_all(g):
        return pltpu.make_async_remote_copy(
            src_ref=sent.at[others(g)],
            dst_ref=ret.at[others(g)],
            send_sem=back_send.at[g],
            recv_sem=back_recv.at[g],
            device_id=(mate, blk),
            device_id_type=MESH,
        )

    def pack(g):
        one_hot = jnp.where(hits(g), 1.0, 0.0).reshape(ROWS, tokens).astype(jnp.bfloat16)
        rows = pl.ds(pl.multiple_of(g * ROWS, ROWS), ROWS)

        @pl.loop(0, normed.shape[1] // 512)
        def _(n):
            cols = pl.ds(pl.multiple_of(n * 512, 512), 512)
            packed[rows, cols] = jnp.dot(
                one_hot, normed[:, cols], preferred_element_type=jnp.float32
            ).astype(jnp.bfloat16)

    for g in range(NGRP):
        pack(g)
        lax.fori_loop(1, NPOS, lambda j, _: (dispatch(g, j).start(), 0)[1], 0)
        recv[slab(g, 0), :] = packed[slab(g, 0), :]

    logits = lax.dot_general(
        router_ref[...],
        normed[...],
        (((1,), (1,)), ((), ())),
        preferred_element_type=jnp.float32,
    )
    order = jnp.where(
        expert == lax.broadcasted_iota(jnp.int32, (NPOS, NPOS), 1), 1.0, 0.0
    ).astype(jnp.bfloat16)
    gates[...] = jnp.dot(
        order,
        jax.nn.sigmoid(logits).astype(jnp.bfloat16),
        preferred_element_type=jnp.float32,
    )

    load_gate_up.wait()
    load_down.wait()
    ff = down.shape[0]

    @pl.loop(0, NGRP)
    def _(g):
        dispatch_all(g).wait_recv()
        rows = pl.ds(pl.multiple_of(g * ROWS, ROWS), ROWS)

        @pl.loop(0, ff // TILE)
        def _(f):
            cols = pl.ds(pl.multiple_of(f * TILE, TILE), TILE)
            up_cols = pl.ds(pl.multiple_of(ff + f * TILE, TILE), TILE)
            gate = jnp.dot(recv[rows, :], gate_up[:, cols], preferred_element_type=jnp.float32)
            up = jnp.dot(recv[rows, :], gate_up[:, up_cols], preferred_element_type=jnp.float32)
            hidden[:, cols] = (jax.nn.silu(gate) * up).astype(jnp.bfloat16)

        @pl.loop(0, width // TILE)
        def _(n):
            cols = pl.ds(pl.multiple_of(n * TILE, TILE), TILE)
            sent[rows, cols] = jnp.dot(
                hidden[...], down[:, cols], preferred_element_type=jnp.float32
            ).astype(jnp.bfloat16)

        lax.fori_loop(1, NPOS, lambda j, _: (give_back(g, j).start(), 0)[1], 0)
        ret[slab(g, 0), :] = sent[slab(g, 0), :]

    total[...] = resid[...].astype(jnp.float32)

    @pl.loop(0, NGRP)
    def _(g):
        spread = jnp.where(hits(g), gates[...][:, None, :], 0.0).reshape(ROWS, tokens)
        spread = spread.T.astype(jnp.bfloat16)
        give_back_all(g).wait_recv()
        rows = pl.ds(pl.multiple_of(g * ROWS, ROWS), ROWS)

        @pl.loop(0, width // 512)
        def _(n):
            cols = pl.ds(pl.multiple_of(n * 512, 512), 512)
            total[:, cols] += jnp.dot(spread, ret[rows, cols], preferred_element_type=jnp.float32)

    out_ref[...] = total[...].astype(jnp.bfloat16)

    def drain(j, _):
        page_arrival(j).wait_recv()
        page_copy(j).wait_send()
        return 0

    lax.fori_loop(1, NPOS, drain, 0)
    for g in range(NGRP):
        dispatch_all(g).wait_send()
        give_back_all(g).wait_send()
    own_page.wait()
    for n in range(width // SPAN):
        near_copy(0, n).wait_send()
        near_copy(1, n).wait_send()
        far_copy(n).wait_send()


def on_device(
    residual_in,
    segment_ids,
    attn_gain,
    w_qkv,
    w_out,
    ffn_gain,
    w_router,
    routes,
    w_gate_up,
    w_down,
    page_owner,
):
    tokens, width = residual_in.shape[1:]
    heads = w_qkv.shape[1]
    length = segment_ids.shape[1]
    page = length // NPOS
    ff = w_down.shape[1]
    slots = NPOS * CAP
    vmem = pl.BlockSpec(memory_space=pltpu.VMEM)
    hbm = pl.BlockSpec(memory_space=pl.ANY)
    dma = pltpu.SemaphoreType.DMA
    bf16 = jnp.bfloat16
    spans = width // SPAN
    residual_out, kv_cache = pl.pallas_call(
        layer_kernel,
        out_shape=(
            jax.ShapeDtypeStruct((tokens, width), bf16),
            jax.ShapeDtypeStruct((NPOS, page, heads * 2 * HEAD), bf16),
        ),
        in_specs=[vmem] * 7 + [hbm] * 4,
        out_specs=(vmem, vmem),
        scratch_shapes=[
            pltpu.VMEM((length, heads * HEAD), bf16),
            pltpu.VMEM((length, heads * 2 * HEAD), bf16),
            pltpu.VMEM((NPOS, page, heads * 2 * HEAD), bf16),
            pltpu.VMEM((length, heads * HEAD), bf16),
            pltpu.VMEM((2 * tokens, width), jnp.float32),
            pltpu.VMEM((2, tokens, width), bf16),
            pltpu.VMEM((2, tokens, width), bf16),
            pltpu.VMEM((tokens, width), bf16),
            pltpu.VMEM((tokens, width), bf16),
            pltpu.VMEM((tokens, width), bf16),
            pltpu.VMEM((tokens, width), bf16),
            pltpu.VMEM((NPOS, tokens), jnp.int32),
            pltpu.VMEM((NPOS, tokens), jnp.float32),
            pltpu.VMEM((slots, width), bf16),
            pltpu.VMEM((slots, width), bf16),
            pltpu.VMEM((max(slots, width), width), bf16),
            pltpu.VMEM((slots, width), bf16),
            pltpu.VMEM((ROWS, ff), bf16),
            pltpu.VMEM((width, 2 * ff), bf16),
            pltpu.VMEM((ff, width), bf16),
            pltpu.VMEM((tokens, width), jnp.float32),
            dma((4,)),
            dma,
            dma((NGRP,)),
            dma((NGRP,)),
            dma((NGRP,)),
            dma((NGRP,)),
            dma((NPOS,)),
            dma((NPOS,)),
            dma((2,)),
            dma((PARTS,)),
            dma((PARTS,)),
            dma((PARTS,)),
            dma((PARTS,)),
            dma((2, spans)),
            dma((2, spans)),
            dma((spans,)),
            dma((spans,)),
        ],
        compiler_params=pltpu.CompilerParams(
            collective_id=0, has_side_effects=True, vmem_limit_bytes=60 << 20
        ),
    )(
        residual_in[0],
        segment_ids,
        page_owner,
        attn_gain,
        ffn_gain,
        w_router.T,
        routes[0].T,
        w_qkv.reshape(width, heads * 3 * HEAD),
        w_out.reshape(heads * HEAD, width),
        w_gate_up[0],
        w_down[0],
    )
    return (residual_out[None], kv_cache[None])


def solution(mesh):
    in_specs = (
        P("blk", "seq", None),
        P("blk", None),
        P(),
        P(None, "seq", None),
        P("seq", None, None),
        P(),
        P(),
        P("blk", "seq", None),
        P("blk", None, None),
        P("blk", None, None),
        P("blk", None),
    )
    out_specs = (P("blk", "seq", None), P("blk", None, None, "seq"))
    return jax.shard_map(
        on_device, mesh=mesh, in_specs=in_specs, out_specs=out_specs, check_vma=False
    )
```

```python
import math

import jax
import jax.numpy as jnp
from jax import lax
from jax.experimental import pallas as pl
from jax.experimental.pallas import tpu as pltpu
from jax.sharding import PartitionSpec as P

EPS = 1e-06
NPOS = 32
CAP = 48
SUB = 16
RING = 4
PLANE = 8
ROWS = PLANE * CAP
PIECE = 32
TILE = 256
HEAD = 128
PARTS = 4
SPAN = 512
MESH = pl.DeviceIdType.MESH
SHIFTS = (0, 1, 3, 2)


def step_of(position, core):
    k = lax.rem(position * 11, NPOS)
    dx, dz, dy = lax.div(k, 16), lax.rem(lax.div(k, 4), 4), lax.rem(k, 4)
    return dx, dz + core * (dy - dz), dy + core * (dz - dy)


def place_at(blk, position, core, sign):
    dx, dz, dy = step_of(position, core)
    x, z, y = lax.div(blk, 16), lax.rem(lax.div(blk, 4), 4), lax.rem(blk, 4)
    x = lax.rem(x + dx, 2)
    z = lax.rem(z + 4 + sign * dz, 4)
    y = lax.rem(y + 4 + sign * dy, 4)
    return (x * 4 + z) * 4 + y


def locate(blk, core):
    x, z, y = lax.div(blk, 16), lax.rem(lax.div(blk, 4), 4), lax.rem(blk, 4)
    return x, z + core * (y - z), y + core * (z - y)


def index_of(x, u, v, core):
    z, y = u + core * (v - u), v + core * (u - v)
    return (x * 4 + z) * 4 + y


def along_ring(blk, core, shift):
    x, u, v = locate(blk, core)
    return index_of(x, lax.rem(u + 4 + shift, 4), v, core)


def in_plane(blk, core, position, sign):
    x, u, v = locate(blk, core)
    dx, dv = lax.div(position, 4), lax.rem(position, 4)
    return index_of(lax.rem(x + dx, 2), u, lax.rem(v + 4 + sign * dv, 4), core)


def plane_peer(blk, seq, position, sign):
    core = lax.rem(seq, 2)
    dx, dv = lax.div(position, 4), lax.rem(position, 4)
    other = 2 * dx * (1 - lax.rem(dv, 2))
    return lax.rem(seq + other, 4), in_plane(blk, core, position, sign)


def layer_kernel(
    rows_ref,
    segment_ref,
    owner_ref,
    attn_gain_ref,
    ffn_gain_ref,
    router_ref,
    routes_ref,
    qkv_hbm,
    out_hbm,
    gate_up_hbm,
    down_hbm,
    out_ref,
    kv_ref,
    queries,
    keys_values,
    pages_ref,
    context,
    partial,
    near_send,
    near_recv,
    far_send,
    far_recv,
    resid,
    blocks,
    routed,
    sums_out,
    sums_in,
    rank,
    gates,
    packed,
    recv,
    sent,
    ret,
    hidden,
    gate_up,
    down,
    total,
    weight_sems,
    kv_local_sem,
    out_send,
    out_recv,
    back_send,
    back_recv,
    kv_send,
    kv_recv,
    own_sems,
    gather_send,
    gather_recv,
    pass_send,
    pass_recv,
    near_send_sems,
    near_recv_sems,
    far_send_sems,
    far_recv_sems,
    route_send,
    route_recv,
    ring_send,
    ring_recv,
    sum_send,
    sum_recv,
):
    blk = lax.axis_index("blk")
    seq = lax.axis_index("seq")
    half = lax.div(seq, 2)
    core = lax.rem(seq, 2)
    mate = seq + 1 - 2 * core
    far = lax.rem(seq + 2, 4)
    tok = rows_ref.shape[0]
    width = rows_ref.shape[1]
    length = 4 * tok
    heads = out_hbm.shape[0] // HEAD
    w_qkv = sent.at[0:width, 0 : qkv_hbm.shape[1]]
    w_out = packed.at[0 : out_hbm.shape[0]]
    everyone = packed.at[out_hbm.shape[0] : out_hbm.shape[0] + length]
    load_qkv = pltpu.make_async_copy(qkv_hbm, w_qkv, weight_sems.at[2])
    load_out = pltpu.make_async_copy(out_hbm, w_out, weight_sems.at[3])
    load_gate_up = pltpu.make_async_copy(gate_up_hbm, gate_up, weight_sems.at[0])
    load_down = pltpu.make_async_copy(down_hbm, down, weight_sems.at[1])
    load_qkv.start()
    load_out.start()

    barrier = pltpu.get_barrier_semaphore()

    def greet(j, _):
        pl.semaphore_signal(
            barrier,
            inc=1,
            device_id=(seq, place_at(blk, j, core, 1)),
            device_id_type=MESH,
        )
        return 0

    lax.fori_loop(1, NPOS, greet, 0)
    for crossing in (4, 6):
        pl.semaphore_signal(
            barrier,
            inc=1,
            device_id=plane_peer(blk, seq, crossing, 1),
            device_id_type=MESH,
        )
    for other in (mate, far):
        pl.semaphore_signal(barrier, inc=1, device_id=(other, blk), device_id_type=MESH)

    def block(index):
        return pl.ds(pl.multiple_of(index * tok, tok), tok)

    def norm(wide, gain_ref):
        scale = lax.rsqrt(jnp.mean(wide * wide, axis=-1, keepdims=True) + EPS)
        return (wide * scale * gain_ref[...].astype(jnp.float32).reshape(1, width)).astype(jnp.bfloat16)

    def send(src, dst, send_sem, recv_sem, to):
        return pltpu.make_async_remote_copy(
            src_ref=src,
            dst_ref=dst,
            send_sem=send_sem,
            recv_sem=recv_sem,
            device_id=(to, blk),
            device_id_type=MESH,
        )

    def piece(index, i):
        rows = tok // PARTS
        return everyone.at[pl.ds(pl.multiple_of(index * tok + i * rows, rows), rows)]

    everyone[block(seq), :] = norm(rows_ref[...].astype(jnp.float32), attn_gain_ref)
    pl.semaphore_wait(barrier, NPOS - 1 + 2 + 2)

    def route_copy(g):
        return pltpu.make_async_remote_copy(
            src_ref=routes_ref,
            dst_ref=routed.at[g],
            send_sem=route_send.at[g],
            recv_sem=route_recv.at[g],
            device_id=(seq, along_ring(blk, core, SHIFTS[g])),
            device_id_type=MESH,
        )


    own_out = send(
        everyone.at[block(seq)], everyone.at[block(seq)], own_sems.at[0], own_sems.at[1], mate
    )
    own_in = send(
        everyone.at[block(mate)], everyone.at[block(mate)], own_sems.at[0], own_sems.at[1], mate
    )
    gather_out = [
        send(piece(seq, i), piece(seq, i), gather_send.at[i], gather_recv.at[i], far)
        for i in range(PARTS)
    ]
    gather_in = [
        send(piece(far, i), piece(far, i), gather_send.at[i], gather_recv.at[i], far)
        for i in range(PARTS)
    ]
    far_mate = lax.rem(mate + 2, 4)
    pass_out = [
        send(piece(far, i), piece(far, i), pass_send.at[i], pass_recv.at[i], mate)
        for i in range(PARTS)
    ]
    pass_in = [
        send(piece(far_mate, i), piece(far_mate, i), pass_send.at[i], pass_recv.at[i], mate)
        for i in range(PARTS)
    ]
    for copy in gather_out:
        copy.start()
    own_out.start()
    for g in range(1, RING):
        route_copy(g).start()

    def two_blocks(index):
        return pl.ds(pl.multiple_of(index * 2 * tok, 2 * tok), 2 * tok)

    def project(index):
        rows = two_blocks(index)

        @pl.loop(0, heads // 2)
        def _(p):
            cols = pl.ds(pl.multiple_of(p * 6 * HEAD, 6 * HEAD), 6 * HEAD)
            both = jnp.dot(
                everyone[rows, :], w_qkv[:, cols], preferred_element_type=jnp.float32
            ).astype(jnp.bfloat16)
            q_cols = pl.ds(pl.multiple_of(p * 2 * HEAD, 2 * HEAD), 2 * HEAD)
            kv_cols = pl.ds(pl.multiple_of(p * 4 * HEAD, 4 * HEAD), 4 * HEAD)
            queries[rows, q_cols] = jnp.concatenate(
                [both[:, 0:HEAD], both[:, 3 * HEAD : 4 * HEAD]], axis=1
            )
            keys_values[rows, kv_cols] = jnp.concatenate(
                [both[:, HEAD : 3 * HEAD], both[:, 4 * HEAD :]], axis=1
            )

    tokens = tok
    expert = in_plane(blk, core, lax.broadcasted_iota(jnp.int32, (PLANE, 1), 0), 1)
    slot = lax.broadcasted_iota(jnp.int32, (PLANE, CAP, tokens), 1)

    def rank_tokens():
        upto = lax.broadcasted_iota(jnp.int32, (tokens, tokens), 0) <= lax.broadcasted_iota(
            jnp.int32, (tokens, tokens), 1
        )
        for g in range(RING):
            if g > 0:
                route_copy(g).wait_recv()
            chosen = jnp.zeros((PLANE, tokens), jnp.int32)
            for k in range(routes_ref.shape[0]):
                named = routes_ref[k : k + 1, :] if g == 0 else routed[g, k : k + 1, :]
                chosen = jnp.where(named == expert, 1, chosen)
            count = jnp.dot(
                chosen.astype(jnp.bfloat16),
                jnp.where(upto, 1.0, 0.0).astype(jnp.bfloat16),
                preferred_element_type=jnp.float32,
            ).astype(jnp.int32)
            rank[g] = jnp.where(chosen == 1, count - 1, -1)

    def hits(g):
        return rank[g][:, None, :] == slot

    segment_row = segment_ref[...]
    segment_column = jnp.broadcast_to(segment_row, (HEAD, length)).T

    load_qkv.wait()
    load_out.wait()
    load_gate_up.start()
    load_down.start()
    own_in.wait_recv()
    project(half)
    rank_tokens()
    for i in range(PARTS):
        gather_in[i].wait_recv()
        pass_out[i].start()
    for i in range(PARTS):
        pass_in[i].wait_recv()
    project(1 - half)

    def page_copy(j):
        to_blk = place_at(blk, j, core, 1)
        return pltpu.make_async_remote_copy(
            src_ref=pages_ref.at[to_blk],
            dst_ref=kv_ref.at[blk],
            send_sem=kv_send.at[j],
            recv_sem=kv_recv.at[j],
            device_id=(seq, to_blk),
            device_id_type=MESH,
        )

    def page_arrival(j):
        from_blk = place_at(blk, j, core, -1)
        return pltpu.make_async_remote_copy(
            src_ref=pages_ref.at[from_blk],
            dst_ref=kv_ref.at[from_blk],
            send_sem=kv_send.at[j],
            recv_sem=kv_recv.at[j],
            device_id=(seq, from_blk),
            device_id_type=MESH,
        )

    def attend(index):
        rows = two_blocks(index)
        picked = jnp.where(index == 0, segment_column[0 : 2 * tok], segment_column[2 * tok :])
        same = picked[:, 0:1] == segment_row

        @pl.loop(0, heads)
        def _(head):
            cols = pl.ds(pl.multiple_of(head * HEAD, HEAD), HEAD)
            k_cols = pl.ds(pl.multiple_of(head * 2 * HEAD, HEAD), HEAD)
            v_cols = pl.ds(pl.multiple_of(head * 2 * HEAD + HEAD, HEAD), HEAD)
            scores = lax.dot_general(
                queries[rows, cols],
                keys_values[:, k_cols],
                (((1,), (1,)), ((), ())),
                preferred_element_type=jnp.float32,
            ) * (1.0 / math.sqrt(HEAD))
            scores = jnp.where(same, scores, -1e30)
            weights = jnp.exp(scores - jnp.max(scores, axis=-1, keepdims=True))
            probs = (weights / jnp.sum(weights, axis=-1, keepdims=True)).astype(jnp.bfloat16)
            context[rows, cols] = jnp.dot(
                probs, keys_values[:, v_cols], preferred_element_type=jnp.float32
            ).astype(jnp.bfloat16)

    def column(n):
        return pl.ds(n * SPAN, SPAN)

    def near_copy(which, n):
        return send(
            near_send.at[which, :, column(n)],
            near_recv.at[which, :, column(n)],
            near_send_sems.at[which, n],
            near_recv_sems.at[which, n],
            mate,
        )

    def far_copy(n):
        return send(
            far_send.at[:, column(n)],
            far_recv.at[:, column(n)],
            far_send_sems.at[n],
            far_recv_sems.at[n],
            far,
        )

    def mix(which, index):
        for n in range(width // SPAN):
            partial[:, column(n)] = jnp.dot(
                context[two_blocks(index), :],
                w_out[:, column(n)],
                preferred_element_type=jnp.float32,
            )
            near_send[which, :, column(n)] = partial[block(1 - core), column(n)].astype(
                jnp.bfloat16
            )
            near_copy(which, n).start()

    def reduced(which, n):
        near_copy(which, n).wait_recv()
        return partial[block(core), column(n)] + near_recv[which, :, column(n)].astype(
            jnp.float32
        )

    attend(1 - half)
    mix(0, 1 - half)
    for n in range(width // SPAN):
        far_send[:, column(n)] = reduced(0, n).astype(jnp.bfloat16)
        far_copy(n).start()
    attend(half)
    mix(1, half)
    page = length // NPOS
    spread_owner = lax.div(
        lax.broadcasted_iota(jnp.int32, (NPOS, length), 1), page
    ) == lax.broadcasted_iota(jnp.int32, (NPOS, length), 0)
    owners = jnp.dot(
        jnp.broadcast_to(owner_ref[...], (8, NPOS)).astype(jnp.bfloat16),
        jnp.where(spread_owner, 1.0, 0.0).astype(jnp.bfloat16),
        preferred_element_type=jnp.float32,
    ).astype(jnp.int32)[0:1]
    to_row = lax.broadcasted_iota(jnp.int32, (length, length), 0)
    from_row = lax.broadcasted_iota(jnp.int32, (length, length), 1)
    moves = (lax.rem(to_row, page) == lax.rem(from_row, page)) & (
        lax.div(to_row, page) == owners
    )
    pages_ref[...] = (
        jnp.dot(
            jnp.where(moves, 1.0, 0.0).astype(jnp.bfloat16),
            keys_values[...],
            preferred_element_type=jnp.float32,
        )
        .astype(jnp.bfloat16)
        .reshape(pages_ref.shape)
    )
    own_page = pltpu.make_async_copy(pages_ref.at[blk], kv_ref.at[blk], kv_local_sem)
    own_page.start()
    lax.fori_loop(1, NPOS, lambda j, _: (page_copy(j).start(), 0)[1], 0)

    for n in range(width // SPAN):
        mixed = reduced(1, n)
        far_copy(n).wait_recv()
        mixed = mixed + far_recv[:, column(n)].astype(jnp.float32)
        resid[:, column(n)] = (rows_ref[:, column(n)].astype(jnp.float32) + mixed).astype(
            jnp.bfloat16
        )
    blocks[0:tokens, :] = norm(resid[...].astype(jnp.float32), ffn_gain_ref)
    own_out.wait_send()
    for i in range(PARTS):
        gather_out[i].wait_send()
        pass_out[i].wait_send()

    def ring_piece(g, i):
        rows = pl.ds(pl.multiple_of(i * PIECE, PIECE), PIECE)
        to_rows = pl.ds(pl.multiple_of(g * tokens + i * PIECE, PIECE), PIECE)
        return pltpu.make_async_remote_copy(
            src_ref=blocks.at[rows],
            dst_ref=blocks.at[to_rows],
            send_sem=ring_send.at[g],
            recv_sem=ring_recv.at[g],
            device_id=(seq, along_ring(blk, core, SHIFTS[g])),
            device_id_type=MESH,
        )

    def ring_all(g):
        return pltpu.make_async_remote_copy(
            src_ref=blocks.at[0:tokens],
            dst_ref=blocks.at[pl.ds(g * tokens, tokens)],
            send_sem=ring_send.at[g],
            recv_sem=ring_recv.at[g],
            device_id=(mate, blk),
            device_id_type=MESH,
        )

    def sum_piece(g, i):
        rows = pl.ds(pl.multiple_of(i * PIECE, PIECE), PIECE)
        return pltpu.make_async_remote_copy(
            src_ref=sums_out.at[g - 1, rows],
            dst_ref=sums_in.at[g - 1, rows],
            send_sem=sum_send.at[g],
            recv_sem=sum_recv.at[g],
            device_id=(seq, along_ring(blk, core, -SHIFTS[g])),
            device_id_type=MESH,
        )

    def sum_all(g):
        return pltpu.make_async_remote_copy(
            src_ref=sums_out.at[g - 1],
            dst_ref=sums_in.at[g - 1],
            send_sem=sum_send.at[g],
            recv_sem=sum_recv.at[g],
            device_id=(mate, blk),
            device_id_type=MESH,
        )

    def slab(g, p):
        return pl.ds(pl.multiple_of(g * ROWS + p * CAP, SUB), CAP)

    def others(g):
        return pl.ds(pl.multiple_of(g * ROWS + CAP, SUB), ROWS - CAP)

    def nth(g, i):
        p = lax.rem((lax.rem(i, PLANE - 1) + 1) * 3, PLANE)
        start = g * ROWS + p * CAP + lax.div(i, PLANE - 1) * SUB
        return p, pl.ds(pl.multiple_of(start, SUB), SUB)

    def dispatch(g, i):
        p, rows = nth(g, i)
        return pltpu.make_async_remote_copy(
            src_ref=packed.at[rows],
            dst_ref=recv.at[rows],
            send_sem=out_send.at[g],
            recv_sem=out_recv.at[g],
            device_id=plane_peer(blk, seq, p, 1),
            device_id_type=MESH,
        )

    def give_back(g, i):
        p, rows = nth(g, i)
        return pltpu.make_async_remote_copy(
            src_ref=sent.at[rows],
            dst_ref=ret.at[rows],
            send_sem=back_send.at[g],
            recv_sem=back_recv.at[g],
            device_id=plane_peer(blk, seq, p, -1),
            device_id_type=MESH,
        )

    def dispatch_all(g):
        return pltpu.make_async_remote_copy(
            src_ref=packed.at[others(g)],
            dst_ref=recv.at[others(g)],
            send_sem=out_send.at[g],
            recv_sem=out_recv.at[g],
            device_id=(mate, blk),
            device_id_type=MESH,
        )

    def give_back_all(g):
        return pltpu.make_async_remote_copy(
            src_ref=sent.at[others(g)],
            dst_ref=ret.at[others(g)],
            send_sem=back_send.at[g],
            recv_sem=back_recv.at[g],
            device_id=(mate, blk),
            device_id_type=MESH,
        )

    def pack(g):
        one_hot = jnp.where(hits(g), 1.0, 0.0).reshape(ROWS, tokens).astype(jnp.bfloat16)
        rows = pl.ds(g * ROWS, ROWS)

        @pl.loop(0, width // 512)
        def _(n):
            cols = pl.ds(pl.multiple_of(n * 512, 512), 512)
            packed[rows, cols] = jnp.dot(
                one_hot,
                blocks[g * tokens : (g + 1) * tokens, cols],
                preferred_element_type=jnp.float32,
            ).astype(jnp.bfloat16)

    copies = (PLANE - 1) * (CAP // SUB)
    pieces = tokens // PIECE
    for g in range(1, RING):
        lax.fori_loop(0, pieces, lambda i, _: (ring_piece(g, i).start(), 0)[1], 0)
    for g in range(RING):
        if g > 0:
            ring_all(g).wait_recv()
        pack(g)
        lax.fori_loop(0, copies, lambda i, _: (dispatch(g, i).start(), 0)[1], 0)
        recv[slab(g, 0), :] = packed[slab(g, 0), :]

    order = jnp.where(
        expert == lax.broadcasted_iota(jnp.int32, (PLANE, NPOS), 1), 1.0, 0.0
    ).astype(jnp.bfloat16)
    for g in range(RING):
        logits = lax.dot_general(
            router_ref[...],
            blocks[g * tokens : (g + 1) * tokens, :],
            (((1,), (1,)), ((), ())),
            preferred_element_type=jnp.float32,
        )
        gates[g] = jnp.dot(
            order,
            jax.nn.sigmoid(logits).astype(jnp.bfloat16),
            preferred_element_type=jnp.float32,
        )

    load_gate_up.wait()
    load_down.wait()
    ff = down.shape[0]

    @pl.loop(0, RING)
    def _(g):
        dispatch_all(g).wait_recv()
        rows = pl.ds(pl.multiple_of(g * ROWS, ROWS), ROWS)

        @pl.loop(0, ff // TILE)
        def _(f):
            cols = pl.ds(pl.multiple_of(f * TILE, TILE), TILE)
            up_cols = pl.ds(pl.multiple_of(ff + f * TILE, TILE), TILE)
            gate = jnp.dot(recv[rows, :], gate_up[:, cols], preferred_element_type=jnp.float32)
            up = jnp.dot(recv[rows, :], gate_up[:, up_cols], preferred_element_type=jnp.float32)
            hidden[:, cols] = (jax.nn.silu(gate) * up).astype(jnp.bfloat16)

        @pl.loop(0, width // TILE)
        def _(n):
            cols = pl.ds(pl.multiple_of(n * TILE, TILE), TILE)
            sent[rows, cols] = jnp.dot(
                hidden[...], down[:, cols], preferred_element_type=jnp.float32
            ).astype(jnp.bfloat16)

        lax.fori_loop(0, copies, lambda i, _: (give_back(g, i).start(), 0)[1], 0)
        ret[slab(g, 0), :] = sent[slab(g, 0), :]

    for g in range(RING):
        spread = jnp.where(hits(g), gates[g][:, None, :], 0.0).reshape(ROWS, tokens)
        spread = spread.T.astype(jnp.bfloat16)
        give_back_all(g).wait_recv()

        @pl.loop(0, width // 512)
        def _(n):
            cols = pl.ds(pl.multiple_of(n * 512, 512), 512)
            mixture = jnp.dot(
                spread,
                ret[g * ROWS : (g + 1) * ROWS, cols],
                preferred_element_type=jnp.float32,
            )
            if g == 0:
                total[:, cols] = resid[:, cols].astype(jnp.float32) + mixture
            else:
                sums_out[g - 1, :, cols] = mixture.astype(jnp.bfloat16)

        if g > 0:
            lax.fori_loop(0, pieces, lambda i, _: (sum_piece(g, i).start(), 0)[1], 0)

    for g in range(1, RING):
        sum_all(g).wait_recv()
        if g < RING - 1:
            total[...] += sums_in[g - 1].astype(jnp.float32)
        else:
            out_ref[...] = (total[...] + sums_in[g - 1].astype(jnp.float32)).astype(
                jnp.bfloat16
            )

    def drain(j, _):
        page_arrival(j).wait_recv()
        page_copy(j).wait_send()
        return 0

    lax.fori_loop(1, NPOS, drain, 0)
    for g in range(RING):
        dispatch_all(g).wait_send()
        give_back_all(g).wait_send()
        if g > 0:
            route_copy(g).wait_send()
            ring_all(g).wait_send()
            sum_all(g).wait_send()
    own_page.wait()
    for n in range(width // SPAN):
        near_copy(0, n).wait_send()
        near_copy(1, n).wait_send()
        far_copy(n).wait_send()


def on_device(
    residual_in,
    segment_ids,
    attn_gain,
    w_qkv,
    w_out,
    ffn_gain,
    w_router,
    routes,
    w_gate_up,
    w_down,
    page_owner,
):
    tokens, width = residual_in.shape[1:]
    heads = w_qkv.shape[1]
    length = segment_ids.shape[1]
    page = length // NPOS
    ff = w_down.shape[1]
    slots = NPOS * CAP
    vmem = pl.BlockSpec(memory_space=pltpu.VMEM)
    hbm = pl.BlockSpec(memory_space=pl.ANY)
    dma = pltpu.SemaphoreType.DMA
    bf16 = jnp.bfloat16
    spans = width // SPAN
    residual_out, kv_cache = pl.pallas_call(
        layer_kernel,
        out_shape=(
            jax.ShapeDtypeStruct((tokens, width), bf16),
            jax.ShapeDtypeStruct((NPOS, page, heads * 2 * HEAD), bf16),
        ),
        in_specs=[vmem] * 7 + [hbm] * 4,
        out_specs=(vmem, hbm),
        scratch_shapes=[
            pltpu.VMEM((length, heads * HEAD), bf16),
            pltpu.VMEM((length, heads * 2 * HEAD), bf16),
            pltpu.VMEM((NPOS, page, heads * 2 * HEAD), bf16),
            pltpu.VMEM((length, heads * HEAD), bf16),
            pltpu.VMEM((2 * tokens, width), jnp.float32),
            pltpu.VMEM((2, tokens, width), bf16),
            pltpu.VMEM((2, tokens, width), bf16),
            pltpu.VMEM((tokens, width), bf16),
            pltpu.VMEM((tokens, width), bf16),
            pltpu.VMEM((tokens, width), bf16),
            pltpu.VMEM((RING * tokens, width), bf16),
            pltpu.VMEM((RING,) + routes.shape[2:] + (tokens,), jnp.int32),
            pltpu.VMEM((RING - 1, tokens, width), bf16),
            pltpu.VMEM((RING - 1, tokens, width), bf16),
            pltpu.VMEM((RING, PLANE, tokens), jnp.int32),
            pltpu.VMEM((RING, PLANE, tokens), jnp.float32),
            pltpu.VMEM((slots, width), bf16),
            pltpu.VMEM((slots, width), bf16),
            pltpu.VMEM((max(slots, width), width), bf16),
            pltpu.VMEM((slots, width), bf16),
            pltpu.VMEM((ROWS, ff), bf16),
            pltpu.VMEM((width, 2 * ff), bf16),
            pltpu.VMEM((ff, width), bf16),
            pltpu.VMEM((tokens, width), jnp.float32),
            dma((4,)),
            dma,
            dma((RING,)),
            dma((RING,)),
            dma((RING,)),
            dma((RING,)),
            dma((NPOS,)),
            dma((NPOS,)),
            dma((2,)),
            dma((PARTS,)),
            dma((PARTS,)),
            dma((PARTS,)),
            dma((PARTS,)),
            dma((2, spans)),
            dma((2, spans)),
            dma((spans,)),
            dma((spans,)),
            dma((RING,)),
            dma((RING,)),
            dma((RING,)),
            dma((RING,)),
            dma((RING,)),
            dma((RING,)),
        ],
        compiler_params=pltpu.CompilerParams(
            collective_id=0, has_side_effects=True, vmem_limit_bytes=60 << 20
        ),
    )(
        residual_in[0],
        segment_ids,
        page_owner,
        attn_gain,
        ffn_gain,
        w_router.T,
        routes[0].T,
        w_qkv.reshape(width, heads * 3 * HEAD),
        w_out.reshape(heads * HEAD, width),
        w_gate_up[0],
        w_down[0],
    )
    return (residual_out[None], kv_cache[None])


def solution(mesh):
    in_specs = (
        P("blk", "seq", None),
        P("blk", None),
        P(),
        P(None, "seq", None),
        P("seq", None, None),
        P(),
        P(),
        P("blk", "seq", None),
        P("blk", None, None),
        P("blk", None, None),
        P("blk", None),
    )
    out_specs = (P("blk", "seq", None), P("blk", None, None, "seq"))
    return jax.shard_map(
        on_device, mesh=mesh, in_specs=in_specs, out_specs=out_specs, check_vma=False
    )
```

```python
import math

import jax
import jax.numpy as jnp
from jax import lax
from jax.experimental import pallas as pl
from jax.experimental.pallas import tpu as pltpu
from jax.sharding import PartitionSpec as P

EPS = 1e-06
NPOS = 32
CAP = 48
SUB = 16
RING = 4
PLANE = 8
ROWS = PLANE * CAP
PIECE = 32
LOAD = 256
TURN = 64
TILE = 256
HEAD = 128
PARTS = 4
SPAN = 512
MESH = pl.DeviceIdType.MESH
SHIFTS = (1, 3, 2, 0)
OWN = RING - 1


def step_of(position, core):
    k = lax.rem(position * 11, NPOS)
    dx, dz, dy = lax.div(k, 16), lax.rem(lax.div(k, 4), 4), lax.rem(k, 4)
    return dx, dz + core * (dy - dz), dy + core * (dz - dy)


def place_at(blk, position, core, sign):
    dx, dz, dy = step_of(position, core)
    x, z, y = lax.div(blk, 16), lax.rem(lax.div(blk, 4), 4), lax.rem(blk, 4)
    x = lax.rem(x + dx, 2)
    z = lax.rem(z + 4 + sign * dz, 4)
    y = lax.rem(y + 4 + sign * dy, 4)
    return (x * 4 + z) * 4 + y


def locate(blk, core):
    x, z, y = lax.div(blk, 16), lax.rem(lax.div(blk, 4), 4), lax.rem(blk, 4)
    return x, z + core * (y - z), y + core * (z - y)


def index_of(x, u, v, core):
    z, y = u + core * (v - u), v + core * (u - v)
    return (x * 4 + z) * 4 + y


def along_ring(blk, core, shift):
    x, u, v = locate(blk, core)
    return index_of(x, lax.rem(u + 4 + shift, 4), v, core)


def in_plane(blk, core, position, sign):
    x, u, v = locate(blk, core)
    dx, dv = lax.div(position, 4), lax.rem(position, 4)
    return index_of(lax.rem(x + dx, 2), u, lax.rem(v + 4 + sign * dv, 4), core)


def plane_peer(blk, seq, position, sign):
    core = lax.rem(seq, 2)
    dx, dv = lax.div(position, 4), lax.rem(position, 4)
    other = 2 * dx * (1 - lax.rem(dv, 2))
    return lax.rem(seq + other, 4), in_plane(blk, core, position, sign)


def layer_kernel(
    rows_ref,
    segment_ref,
    owner_ref,
    attn_gain_ref,
    ffn_gain_ref,
    router_ref,
    routes_ref,
    qkv_hbm,
    out_hbm,
    gate_up_hbm,
    down_hbm,
    out_ref,
    kv_ref,
    queries,
    keys_values,
    pages_ref,
    context,
    partial,
    near_send,
    near_recv,
    far_send,
    far_recv,
    resid,
    blocks,
    routed,
    sums_out,
    sums_in,
    rank,
    gates,
    packed,
    recv,
    sent,
    ret,
    hidden,
    gate_up,
    down,
    total,
    weight_sems,
    kv_local_sem,
    out_send,
    out_recv,
    back_send,
    back_recv,
    kv_send,
    kv_recv,
    own_sems,
    gather_send,
    gather_recv,
    pass_send,
    pass_recv,
    near_send_sems,
    near_recv_sems,
    far_send_sems,
    far_recv_sems,
    staged,
    stage_sems,
    route_send,
    route_recv,
    ring_send,
    ring_recv,
    sum_send,
    sum_recv,
):
    blk = lax.axis_index("blk")
    seq = lax.axis_index("seq")
    half = lax.div(seq, 2)
    core = lax.rem(seq, 2)
    mate = seq + 1 - 2 * core
    far = lax.rem(seq + 2, 4)
    tok = rows_ref.shape[0]
    width = rows_ref.shape[1]
    length = 4 * tok
    heads = out_hbm.shape[0] // HEAD
    columns = qkv_hbm.shape[2]
    w_qkv = sent.at[0:width, 0 : heads * columns]
    w_out = packed.at[0 : out_hbm.shape[0]]
    everyone = packed.at[out_hbm.shape[0] : out_hbm.shape[0] + length]

    def load_qkv(i):
        rows = pl.ds(pl.multiple_of(i * LOAD, LOAD), LOAD)
        return pltpu.make_async_copy(
            qkv_hbm.at[rows], staged.at[lax.rem(i, 2)], stage_sems.at[lax.rem(i, 2)]
        )

    load_out = pltpu.make_async_copy(out_hbm, w_out, weight_sems.at[3])
    load_gate_up = pltpu.make_async_copy(gate_up_hbm, gate_up, weight_sems.at[0])
    load_down = pltpu.make_async_copy(down_hbm, down, weight_sems.at[1])
    load_qkv(0).start()
    load_qkv(1).start()
    load_out.start()

    barrier = pltpu.get_barrier_semaphore()

    def greet(j, _):
        pl.semaphore_signal(
            barrier,
            inc=1,
            device_id=(seq, place_at(blk, j, core, 1)),
            device_id_type=MESH,
        )
        return 0

    lax.fori_loop(1, NPOS, greet, 0)
    for crossing in (4, 6):
        pl.semaphore_signal(
            barrier,
            inc=1,
            device_id=plane_peer(blk, seq, crossing, 1),
            device_id_type=MESH,
        )
    for other in (mate, far):
        pl.semaphore_signal(barrier, inc=1, device_id=(other, blk), device_id_type=MESH)

    def block(index):
        return pl.ds(pl.multiple_of(index * tok, tok), tok)

    def norm(wide, gain_ref):
        scale = lax.rsqrt(jnp.mean(wide * wide, axis=-1, keepdims=True) + EPS)
        return (wide * scale * gain_ref[...].astype(jnp.float32).reshape(1, width)).astype(jnp.bfloat16)

    def send(src, dst, send_sem, recv_sem, to):
        return pltpu.make_async_remote_copy(
            src_ref=src,
            dst_ref=dst,
            send_sem=send_sem,
            recv_sem=recv_sem,
            device_id=(to, blk),
            device_id_type=MESH,
        )

    def piece(index, i):
        rows = tok // PARTS
        return everyone.at[pl.ds(pl.multiple_of(index * tok + i * rows, rows), rows)]

    everyone[block(seq), :] = norm(rows_ref[...].astype(jnp.float32), attn_gain_ref)
    pl.semaphore_wait(barrier, NPOS - 1 + 2 + 2)

    def route_copy(g):
        return pltpu.make_async_remote_copy(
            src_ref=routes_ref,
            dst_ref=routed.at[g],
            send_sem=route_send.at[g],
            recv_sem=route_recv.at[g],
            device_id=(seq, along_ring(blk, core, SHIFTS[g])),
            device_id_type=MESH,
        )


    own_out = send(
        everyone.at[block(seq)], everyone.at[block(seq)], own_sems.at[0], own_sems.at[1], mate
    )
    own_in = send(
        everyone.at[block(mate)], everyone.at[block(mate)], own_sems.at[0], own_sems.at[1], mate
    )
    gather_out = [
        send(piece(seq, i), piece(seq, i), gather_send.at[i], gather_recv.at[i], far)
        for i in range(PARTS)
    ]
    gather_in = [
        send(piece(far, i), piece(far, i), gather_send.at[i], gather_recv.at[i], far)
        for i in range(PARTS)
    ]
    far_mate = lax.rem(mate + 2, 4)
    pass_out = [
        send(piece(far, i), piece(far, i), pass_send.at[i], pass_recv.at[i], mate)
        for i in range(PARTS)
    ]
    pass_in = [
        send(piece(far_mate, i), piece(far_mate, i), pass_send.at[i], pass_recv.at[i], mate)
        for i in range(PARTS)
    ]
    for copy in gather_out:
        copy.start()
    own_out.start()
    for g in range(OWN):
        route_copy(g).start()

    def two_blocks(index):
        return pl.ds(pl.multiple_of(index * 2 * tok, 2 * tok), 2 * tok)

    def project(index):
        rows = two_blocks(index)

        @pl.loop(0, heads // 2)
        def _(p):
            cols = pl.ds(pl.multiple_of(p * 6 * HEAD, 6 * HEAD), 6 * HEAD)
            both = jnp.dot(
                everyone[rows, :], w_qkv[:, cols], preferred_element_type=jnp.float32
            ).astype(jnp.bfloat16)
            q_cols = pl.ds(pl.multiple_of(p * 2 * HEAD, 2 * HEAD), 2 * HEAD)
            kv_cols = pl.ds(pl.multiple_of(p * 4 * HEAD, 4 * HEAD), 4 * HEAD)
            queries[rows, q_cols] = jnp.concatenate(
                [both[:, 0:HEAD], both[:, 3 * HEAD : 4 * HEAD]], axis=1
            )
            keys_values[rows, kv_cols] = jnp.concatenate(
                [both[:, HEAD : 3 * HEAD], both[:, 4 * HEAD :]], axis=1
            )

    tokens = tok
    expert = in_plane(blk, core, lax.broadcasted_iota(jnp.int32, (PLANE, 1), 0), 1)
    slot = lax.broadcasted_iota(jnp.int32, (PLANE, CAP, tokens), 1)

    own_rows = slice(OWN * tokens, RING * tokens)

    def rank_tokens():
        upto = lax.broadcasted_iota(jnp.int32, (tokens, tokens), 0) <= lax.broadcasted_iota(
            jnp.int32, (tokens, tokens), 1
        )
        for g in range(RING):
            if g != OWN:
                route_copy(g).wait_recv()
            chosen = jnp.zeros((PLANE, tokens), jnp.int32)
            for k in range(routes_ref.shape[0]):
                named = routes_ref[k : k + 1, :] if g == OWN else routed[g, k : k + 1, :]
                chosen = jnp.where(named == expert, 1, chosen)
            count = jnp.dot(
                chosen.astype(jnp.bfloat16),
                jnp.where(upto, 1.0, 0.0).astype(jnp.bfloat16),
                preferred_element_type=jnp.float32,
            ).astype(jnp.int32)
            rank[g] = jnp.where(chosen == 1, count - 1, -1)

    def hits(g):
        return rank[g][:, None, :] == slot

    segment_row = segment_ref[...]
    segment_column = jnp.broadcast_to(segment_row, (HEAD, length)).T

    loads = width // LOAD

    @pl.loop(0, loads)
    def _(i):
        load_qkv(i).wait()

        @pl.loop(0, LOAD // TURN)
        def _(t):
            some = staged[lax.rem(i, 2), pl.ds(pl.multiple_of(t * TURN, TURN), TURN)]
            rows = pl.ds(pl.multiple_of(i * LOAD + t * TURN, TURN), TURN)
            for head in range(heads):
                w_qkv[rows, head * columns : (head + 1) * columns] = some[:, head, :]

        @pl.when(i < loads - 2)
        def _():
            load_qkv(i + 2).start()

    load_out.wait()
    load_gate_up.start()
    load_down.start()
    own_in.wait_recv()
    for i in range(PARTS // 2):
        gather_in[i].wait_recv()
        pass_out[i].start()
    project(half)
    rank_tokens()
    for i in range(PARTS // 2, PARTS):
        gather_in[i].wait_recv()
        pass_out[i].start()
    for i in range(PARTS):
        pass_in[i].wait_recv()
    project(1 - half)

    def page_copy(j):
        to_blk = place_at(blk, j, core, 1)
        return pltpu.make_async_remote_copy(
            src_ref=pages_ref.at[to_blk],
            dst_ref=kv_ref.at[blk],
            send_sem=kv_send.at[j],
            recv_sem=kv_recv.at[j],
            device_id=(seq, to_blk),
            device_id_type=MESH,
        )

    def page_arrival(j):
        from_blk = place_at(blk, j, core, -1)
        return pltpu.make_async_remote_copy(
            src_ref=pages_ref.at[from_blk],
            dst_ref=kv_ref.at[from_blk],
            send_sem=kv_send.at[j],
            recv_sem=kv_recv.at[j],
            device_id=(seq, from_blk),
            device_id_type=MESH,
        )

    def attend(index):
        rows = two_blocks(index)
        picked = jnp.where(index == 0, segment_column[0 : 2 * tok], segment_column[2 * tok :])
        same = picked[:, 0:1] == segment_row

        @pl.loop(0, heads)
        def _(head):
            cols = pl.ds(pl.multiple_of(head * HEAD, HEAD), HEAD)
            k_cols = pl.ds(pl.multiple_of(head * 2 * HEAD, HEAD), HEAD)
            v_cols = pl.ds(pl.multiple_of(head * 2 * HEAD + HEAD, HEAD), HEAD)
            scores = lax.dot_general(
                queries[rows, cols],
                keys_values[:, k_cols],
                (((1,), (1,)), ((), ())),
                preferred_element_type=jnp.float32,
            ) * (1.0 / math.sqrt(HEAD))
            scores = jnp.where(same, scores, -1e30)
            weights = jnp.exp(scores - jnp.max(scores, axis=-1, keepdims=True))
            probs = (weights / jnp.sum(weights, axis=-1, keepdims=True)).astype(jnp.bfloat16)
            context[rows, cols] = jnp.dot(
                probs, keys_values[:, v_cols], preferred_element_type=jnp.float32
            ).astype(jnp.bfloat16)

    def column(n):
        return pl.ds(n * SPAN, SPAN)

    def near_copy(which, n):
        return send(
            near_send.at[which, :, column(n)],
            near_recv.at[which, :, column(n)],
            near_send_sems.at[which, n],
            near_recv_sems.at[which, n],
            mate,
        )

    def far_copy(n):
        return send(
            far_send.at[:, column(n)],
            far_recv.at[:, column(n)],
            far_send_sems.at[n],
            far_recv_sems.at[n],
            far,
        )

    def mix(which, index):
        for n in range(width // SPAN):
            partial[:, column(n)] = jnp.dot(
                context[two_blocks(index), :],
                w_out[:, column(n)],
                preferred_element_type=jnp.float32,
            )
            near_send[which, :, column(n)] = partial[block(1 - core), column(n)].astype(
                jnp.bfloat16
            )
            near_copy(which, n).start()

    def reduced(which, n):
        near_copy(which, n).wait_recv()
        return partial[block(core), column(n)] + near_recv[which, :, column(n)].astype(
            jnp.float32
        )

    attend(1 - half)
    mix(0, 1 - half)
    for n in range(width // SPAN):
        far_send[:, column(n)] = reduced(0, n).astype(jnp.bfloat16)
        far_copy(n).start()
    attend(half)
    mix(1, half)
    page = length // NPOS
    spread_owner = lax.div(
        lax.broadcasted_iota(jnp.int32, (NPOS, length), 1), page
    ) == lax.broadcasted_iota(jnp.int32, (NPOS, length), 0)
    owners = jnp.dot(
        jnp.broadcast_to(owner_ref[...], (8, NPOS)).astype(jnp.bfloat16),
        jnp.where(spread_owner, 1.0, 0.0).astype(jnp.bfloat16),
        preferred_element_type=jnp.float32,
    ).astype(jnp.int32)[0:1]
    to_row = lax.broadcasted_iota(jnp.int32, (length, length), 0)
    from_row = lax.broadcasted_iota(jnp.int32, (length, length), 1)
    moves = (lax.rem(to_row, page) == lax.rem(from_row, page)) & (
        lax.div(to_row, page) == owners
    )
    pages_ref[...] = (
        jnp.dot(
            jnp.where(moves, 1.0, 0.0).astype(jnp.bfloat16),
            keys_values[...],
            preferred_element_type=jnp.float32,
        )
        .astype(jnp.bfloat16)
        .reshape(pages_ref.shape)
    )
    own_page = pltpu.make_async_copy(pages_ref.at[blk], kv_ref.at[blk], kv_local_sem)
    own_page.start()
    lax.fori_loop(1, NPOS, lambda j, _: (page_copy(j).start(), 0)[1], 0)

    for n in range(width // SPAN):
        mixed = reduced(1, n)
        far_copy(n).wait_recv()
        mixed = mixed + far_recv[:, column(n)].astype(jnp.float32)
        resid[:, column(n)] = (rows_ref[:, column(n)].astype(jnp.float32) + mixed).astype(
            jnp.bfloat16
        )
    blocks[own_rows, :] = norm(resid[...].astype(jnp.float32), ffn_gain_ref)
    own_out.wait_send()
    for i in range(PARTS):
        gather_out[i].wait_send()
        pass_out[i].wait_send()

    def ring_piece(g, i):
        rows = pl.ds(pl.multiple_of(OWN * tokens + i * PIECE, PIECE), PIECE)
        to_rows = pl.ds(pl.multiple_of(g * tokens + i * PIECE, PIECE), PIECE)
        return pltpu.make_async_remote_copy(
            src_ref=blocks.at[rows],
            dst_ref=blocks.at[to_rows],
            send_sem=ring_send.at[g],
            recv_sem=ring_recv.at[g],
            device_id=(seq, along_ring(blk, core, SHIFTS[g])),
            device_id_type=MESH,
        )

    def ring_all(g):
        return pltpu.make_async_remote_copy(
            src_ref=blocks.at[own_rows],
            dst_ref=blocks.at[pl.ds(g * tokens, tokens)],
            send_sem=ring_send.at[g],
            recv_sem=ring_recv.at[g],
            device_id=(mate, blk),
            device_id_type=MESH,
        )

    def sum_piece(g, i):
        rows = pl.ds(pl.multiple_of(i * PIECE, PIECE), PIECE)
        return pltpu.make_async_remote_copy(
            src_ref=sums_out.at[g, rows],
            dst_ref=sums_in.at[g, rows],
            send_sem=sum_send.at[g],
            recv_sem=sum_recv.at[g],
            device_id=(seq, along_ring(blk, core, -SHIFTS[g])),
            device_id_type=MESH,
        )

    def sum_all(g):
        return pltpu.make_async_remote_copy(
            src_ref=sums_out.at[g],
            dst_ref=sums_in.at[g],
            send_sem=sum_send.at[g],
            recv_sem=sum_recv.at[g],
            device_id=(mate, blk),
            device_id_type=MESH,
        )

    def slab(g, p):
        return pl.ds(pl.multiple_of(g * ROWS + p * CAP, SUB), CAP)

    def others(g):
        return pl.ds(pl.multiple_of(g * ROWS + CAP, SUB), ROWS - CAP)

    def nth(g, i):
        p = lax.rem((lax.rem(i, PLANE - 1) + 1) * 3, PLANE)
        start = g * ROWS + p * CAP + lax.div(i, PLANE - 1) * SUB
        return p, pl.ds(pl.multiple_of(start, SUB), SUB)

    def dispatch(g, i):
        p, rows = nth(g, i)
        return pltpu.make_async_remote_copy(
            src_ref=packed.at[rows],
            dst_ref=recv.at[rows],
            send_sem=out_send.at[g],
            recv_sem=out_recv.at[g],
            device_id=plane_peer(blk, seq, p, 1),
            device_id_type=MESH,
        )

    def give_back(g, i):
        p, rows = nth(g, i)
        return pltpu.make_async_remote_copy(
            src_ref=sent.at[rows],
            dst_ref=ret.at[rows],
            send_sem=back_send.at[g],
            recv_sem=back_recv.at[g],
            device_id=plane_peer(blk, seq, p, -1),
            device_id_type=MESH,
        )

    def dispatch_all(g):
        return pltpu.make_async_remote_copy(
            src_ref=packed.at[others(g)],
            dst_ref=recv.at[others(g)],
            send_sem=out_send.at[g],
            recv_sem=out_recv.at[g],
            device_id=(mate, blk),
            device_id_type=MESH,
        )

    def give_back_all(g):
        return pltpu.make_async_remote_copy(
            src_ref=sent.at[others(g)],
            dst_ref=ret.at[others(g)],
            send_sem=back_send.at[g],
            recv_sem=back_recv.at[g],
            device_id=(mate, blk),
            device_id_type=MESH,
        )

    def pack(g):
        one_hot = jnp.where(hits(g), 1.0, 0.0).reshape(ROWS, tokens).astype(jnp.bfloat16)
        rows = pl.ds(g * ROWS, ROWS)

        @pl.loop(0, width // 512)
        def _(n):
            cols = pl.ds(pl.multiple_of(n * 512, 512), 512)
            packed[rows, cols] = jnp.dot(
                one_hot,
                blocks[g * tokens : (g + 1) * tokens, cols],
                preferred_element_type=jnp.float32,
            ).astype(jnp.bfloat16)

    copies = (PLANE - 1) * (CAP // SUB)
    pieces = tokens // PIECE
    for g in range(OWN):
        lax.fori_loop(0, pieces, lambda i, _: (ring_piece(g, i).start(), 0)[1], 0)
    for g in range(RING):
        if g != OWN:
            ring_all(g).wait_recv()
        pack(g)
        lax.fori_loop(0, copies, lambda i, _: (dispatch(g, i).start(), 0)[1], 0)
        recv[slab(g, 0), :] = packed[slab(g, 0), :]

    order = jnp.where(
        expert == lax.broadcasted_iota(jnp.int32, (PLANE, NPOS), 1), 1.0, 0.0
    ).astype(jnp.bfloat16)
    for g in range(RING):
        logits = lax.dot_general(
            router_ref[...],
            blocks[g * tokens : (g + 1) * tokens, :],
            (((1,), (1,)), ((), ())),
            preferred_element_type=jnp.float32,
        )
        gates[g] = jnp.dot(
            order,
            jax.nn.sigmoid(logits).astype(jnp.bfloat16),
            preferred_element_type=jnp.float32,
        )

    load_gate_up.wait()
    load_down.wait()
    ff = down.shape[0]

    @pl.loop(0, RING)
    def _(g):
        dispatch_all(g).wait_recv()
        rows = pl.ds(pl.multiple_of(g * ROWS, ROWS), ROWS)

        @pl.loop(0, ff // TILE)
        def _(f):
            cols = pl.ds(pl.multiple_of(f * TILE, TILE), TILE)
            up_cols = pl.ds(pl.multiple_of(ff + f * TILE, TILE), TILE)
            gate = jnp.dot(recv[rows, :], gate_up[:, cols], preferred_element_type=jnp.float32)
            up = jnp.dot(recv[rows, :], gate_up[:, up_cols], preferred_element_type=jnp.float32)
            hidden[:, cols] = (jax.nn.silu(gate) * up).astype(jnp.bfloat16)

        @pl.loop(0, width // TILE)
        def _(n):
            cols = pl.ds(pl.multiple_of(n * TILE, TILE), TILE)
            sent[rows, cols] = jnp.dot(
                hidden[...], down[:, cols], preferred_element_type=jnp.float32
            ).astype(jnp.bfloat16)

        lax.fori_loop(0, copies, lambda i, _: (give_back(g, i).start(), 0)[1], 0)
        ret[slab(g, 0), :] = sent[slab(g, 0), :]

    for g in range(RING):
        spread = jnp.where(hits(g), gates[g][:, None, :], 0.0).reshape(ROWS, tokens)
        spread = spread.T.astype(jnp.bfloat16)
        give_back_all(g).wait_recv()

        @pl.loop(0, width // 512)
        def _(n):
            cols = pl.ds(pl.multiple_of(n * 512, 512), 512)
            mixture = jnp.dot(
                spread,
                ret[g * ROWS : (g + 1) * ROWS, cols],
                preferred_element_type=jnp.float32,
            )
            if g == OWN:
                total[:, cols] = resid[:, cols].astype(jnp.float32) + mixture
            else:
                sums_out[g, :, cols] = mixture.astype(jnp.bfloat16)

        if g != OWN:
            lax.fori_loop(0, pieces, lambda i, _: (sum_piece(g, i).start(), 0)[1], 0)

    for g in range(OWN):
        sum_all(g).wait_recv()
    summed = total[...]
    for g in range(OWN):
        summed = summed + sums_in[g].astype(jnp.float32)
    out_ref[...] = summed.astype(jnp.bfloat16)

    def drain(j, _):
        page_arrival(j).wait_recv()
        page_copy(j).wait_send()
        return 0

    lax.fori_loop(1, NPOS, drain, 0)
    for g in range(RING):
        dispatch_all(g).wait_send()
        give_back_all(g).wait_send()
        if g != OWN:
            route_copy(g).wait_send()
            ring_all(g).wait_send()
            sum_all(g).wait_send()
    own_page.wait()
    for n in range(width // SPAN):
        near_copy(0, n).wait_send()
        near_copy(1, n).wait_send()
        far_copy(n).wait_send()


def on_device(
    residual_in,
    segment_ids,
    attn_gain,
    w_qkv,
    w_out,
    ffn_gain,
    w_router,
    routes,
    w_gate_up,
    w_down,
    page_owner,
):
    tokens, width = residual_in.shape[1:]
    heads = w_qkv.shape[1]
    length = segment_ids.shape[1]
    page = length // NPOS
    ff = w_down.shape[1]
    slots = NPOS * CAP
    vmem = pl.BlockSpec(memory_space=pltpu.VMEM)
    hbm = pl.BlockSpec(memory_space=pl.ANY)
    dma = pltpu.SemaphoreType.DMA
    bf16 = jnp.bfloat16
    spans = width // SPAN
    residual_out, kv_cache = pl.pallas_call(
        layer_kernel,
        out_shape=(
            jax.ShapeDtypeStruct((tokens, width), bf16),
            jax.ShapeDtypeStruct((NPOS, page, heads * 2 * HEAD), bf16),
        ),
        in_specs=[vmem] * 7 + [hbm] * 4,
        out_specs=(vmem, hbm),
        scratch_shapes=[
            pltpu.VMEM((length, heads * HEAD), bf16),
            pltpu.VMEM((length, heads * 2 * HEAD), bf16),
            pltpu.VMEM((NPOS, page, heads * 2 * HEAD), bf16),
            pltpu.VMEM((length, heads * HEAD), bf16),
            pltpu.VMEM((2 * tokens, width), jnp.float32),
            pltpu.VMEM((2, tokens, width), bf16),
            pltpu.VMEM((2, tokens, width), bf16),
            pltpu.VMEM((tokens, width), bf16),
            pltpu.VMEM((tokens, width), bf16),
            pltpu.VMEM((tokens, width), bf16),
            pltpu.VMEM((RING * tokens, width), bf16),
            pltpu.VMEM((RING,) + routes.shape[2:] + (tokens,), jnp.int32),
            pltpu.VMEM((RING - 1, tokens, width), bf16),
            pltpu.VMEM((RING - 1, tokens, width), bf16),
            pltpu.VMEM((RING, PLANE, tokens), jnp.int32),
            pltpu.VMEM((RING, PLANE, tokens), jnp.float32),
            pltpu.VMEM((slots, width), bf16),
            pltpu.VMEM((slots, width), bf16),
            pltpu.VMEM((max(slots, width), width), bf16),
            pltpu.VMEM((slots, width), bf16),
            pltpu.VMEM((ROWS, ff), bf16),
            pltpu.VMEM((width, 2 * ff), bf16),
            pltpu.VMEM((ff, width), bf16),
            pltpu.VMEM((tokens, width), jnp.float32),
            dma((4,)),
            dma,
            dma((RING,)),
            dma((RING,)),
            dma((RING,)),
            dma((RING,)),
            dma((NPOS,)),
            dma((NPOS,)),
            dma((2,)),
            dma((PARTS,)),
            dma((PARTS,)),
            dma((PARTS,)),
            dma((PARTS,)),
            dma((2, spans)),
            dma((2, spans)),
            dma((spans,)),
            dma((spans,)),
            pltpu.VMEM((2, LOAD) + w_qkv.shape[1:], bf16),
            dma((2,)),
            dma((RING,)),
            dma((RING,)),
            dma((RING,)),
            dma((RING,)),
            dma((RING,)),
            dma((RING,)),
        ],
        compiler_params=pltpu.CompilerParams(
            collective_id=0, has_side_effects=True, vmem_limit_bytes=60 << 20
        ),
    )(
        residual_in[0],
        segment_ids,
        page_owner,
        attn_gain,
        ffn_gain,
        w_router.T,
        routes[0].T,
        w_qkv,
        w_out.reshape(heads * HEAD, width),
        w_gate_up[0],
        w_down[0],
    )
    return (residual_out[None], kv_cache[None])


def solution(mesh):
    in_specs = (
        P("blk", "seq", None),
        P("blk", None),
        P(),
        P(None, "seq", None),
        P("seq", None, None),
        P(),
        P(),
        P("blk", "seq", None),
        P("blk", None, None),
        P("blk", None, None),
        P("blk", None),
    )
    out_specs = (P("blk", "seq", None), P("blk", None, None, "seq"))
    return jax.shard_map(
        on_device, mesh=mesh, in_specs=in_specs, out_specs=out_specs, check_vma=False
    )
```

```python
import math

import jax
import jax.numpy as jnp
from jax import lax
from jax.experimental import pallas as pl
from jax.experimental.pallas import tpu as pltpu
from jax.sharding import PartitionSpec as P

EPS = 1e-06
NPOS = 32
CAP = 48
SUB = 16
RING = 4
PLANE = 8
ROWS = PLANE * CAP
PIECE = 32
LOAD = 256
TURN = 64
TILE = 256
HEAD = 128
PARTS = 4
SPAN = 512
MESH = pl.DeviceIdType.MESH
SHIFTS = (1, 3, 2, 0)
OWN = RING - 1


def step_of(position, core):
    k = lax.rem(position * 11, NPOS)
    dx, dz, dy = lax.div(k, 16), lax.rem(lax.div(k, 4), 4), lax.rem(k, 4)
    return dx, dz + core * (dy - dz), dy + core * (dz - dy)


def place_at(blk, position, core, sign):
    dx, dz, dy = step_of(position, core)
    x, z, y = lax.div(blk, 16), lax.rem(lax.div(blk, 4), 4), lax.rem(blk, 4)
    x = lax.rem(x + dx, 2)
    z = lax.rem(z + 4 + sign * dz, 4)
    y = lax.rem(y + 4 + sign * dy, 4)
    return (x * 4 + z) * 4 + y


def locate(blk, core):
    x, z, y = lax.div(blk, 16), lax.rem(lax.div(blk, 4), 4), lax.rem(blk, 4)
    return x, z + core * (y - z), y + core * (z - y)


def index_of(x, u, v, core):
    z, y = u + core * (v - u), v + core * (u - v)
    return (x * 4 + z) * 4 + y


def along_ring(blk, core, shift):
    x, u, v = locate(blk, core)
    return index_of(x, lax.rem(u + 4 + shift, 4), v, core)


def in_plane(blk, core, position, sign):
    x, u, v = locate(blk, core)
    dx, dv = lax.div(position, 4), lax.rem(position, 4)
    return index_of(lax.rem(x + dx, 2), u, lax.rem(v + 4 + sign * dv, 4), core)


def plane_peer(blk, seq, position, sign):
    core = lax.rem(seq, 2)
    dx, dv = lax.div(position, 4), lax.rem(position, 4)
    other = 2 * dx * (1 - lax.rem(dv, 2))
    return lax.rem(seq + other, 4), in_plane(blk, core, position, sign)


def layer_kernel(
    rows_ref,
    segment_ref,
    owner_ref,
    attn_gain_ref,
    ffn_gain_ref,
    router_ref,
    routes_ref,
    qkv_hbm,
    out_hbm,
    gate_up_hbm,
    down_hbm,
    out_ref,
    kv_ref,
    queries,
    keys_values,
    pages_ref,
    context,
    partial,
    near_send,
    near_recv,
    far_send,
    far_recv,
    resid,
    blocks,
    routed,
    sums_out,
    sums_in,
    rank,
    gates,
    packed,
    recv,
    sent,
    ret,
    hidden,
    gate_up,
    down,
    total,
    weight_sems,
    kv_local_sem,
    out_send,
    out_recv,
    back_send,
    back_recv,
    kv_send,
    kv_recv,
    own_sems,
    gather_send,
    gather_recv,
    pass_send,
    pass_recv,
    near_send_sems,
    near_recv_sems,
    far_send_sems,
    far_recv_sems,
    staged,
    stage_sems,
    route_send,
    route_recv,
    ring_send,
    ring_recv,
    sum_send,
    sum_recv,
):
    blk = lax.axis_index("blk")
    seq = lax.axis_index("seq")
    half = lax.div(seq, 2)
    core = lax.rem(seq, 2)
    mate = seq + 1 - 2 * core
    far = lax.rem(seq + 2, 4)
    tok = rows_ref.shape[0]
    width = rows_ref.shape[1]
    length = 4 * tok
    heads = out_hbm.shape[0] // HEAD
    columns = qkv_hbm.shape[2]
    w_qkv = sent.at[0:width, 0 : heads * columns]
    w_out = packed.at[0 : out_hbm.shape[0]]
    everyone = packed.at[out_hbm.shape[0] : out_hbm.shape[0] + length]

    def load_qkv(i):
        rows = pl.ds(pl.multiple_of(i * LOAD, LOAD), LOAD)
        return pltpu.make_async_copy(
            qkv_hbm.at[rows], staged.at[lax.rem(i, 2)], stage_sems.at[lax.rem(i, 2)]
        )

    load_out = pltpu.make_async_copy(out_hbm, w_out, weight_sems.at[3])
    load_gate_up = pltpu.make_async_copy(gate_up_hbm, gate_up, weight_sems.at[0])
    load_down = pltpu.make_async_copy(down_hbm, down, weight_sems.at[1])
    load_qkv(0).start()
    load_qkv(1).start()
    load_out.start()

    barrier = pltpu.get_barrier_semaphore()

    def greet(j, _):
        pl.semaphore_signal(
            barrier,
            inc=1,
            device_id=(seq, place_at(blk, j, core, 1)),
            device_id_type=MESH,
        )
        return 0

    lax.fori_loop(1, NPOS, greet, 0)
    for crossing in (4, 6):
        pl.semaphore_signal(
            barrier,
            inc=1,
            device_id=plane_peer(blk, seq, crossing, 1),
            device_id_type=MESH,
        )
    for other in (mate, far):
        pl.semaphore_signal(barrier, inc=1, device_id=(other, blk), device_id_type=MESH)

    def block(index):
        return pl.ds(pl.multiple_of(index * tok, tok), tok)

    def norm(wide, gain_ref):
        scale = lax.rsqrt(jnp.mean(wide * wide, axis=-1, keepdims=True) + EPS)
        return (wide * scale * gain_ref[...].astype(jnp.float32).reshape(1, width)).astype(jnp.bfloat16)

    def send(src, dst, send_sem, recv_sem, to):
        return pltpu.make_async_remote_copy(
            src_ref=src,
            dst_ref=dst,
            send_sem=send_sem,
            recv_sem=recv_sem,
            device_id=(to, blk),
            device_id_type=MESH,
        )

    def piece(index, i):
        rows = tok // PARTS
        return everyone.at[pl.ds(pl.multiple_of(index * tok + i * rows, rows), rows)]

    everyone[block(seq), :] = norm(rows_ref[...].astype(jnp.float32), attn_gain_ref)
    pl.semaphore_wait(barrier, NPOS - 1 + 2 + 2)

    def route_copy(g):
        return pltpu.make_async_remote_copy(
            src_ref=routes_ref,
            dst_ref=routed.at[g],
            send_sem=route_send.at[g],
            recv_sem=route_recv.at[g],
            device_id=(seq, along_ring(blk, core, SHIFTS[g])),
            device_id_type=MESH,
        )


    own_out = send(
        everyone.at[block(seq)], everyone.at[block(seq)], own_sems.at[0], own_sems.at[1], mate
    )
    own_in = send(
        everyone.at[block(mate)], everyone.at[block(mate)], own_sems.at[0], own_sems.at[1], mate
    )
    gather_out = [
        send(piece(seq, i), piece(seq, i), gather_send.at[i], gather_recv.at[i], far)
        for i in range(PARTS)
    ]
    gather_in = [
        send(piece(far, i), piece(far, i), gather_send.at[i], gather_recv.at[i], far)
        for i in range(PARTS)
    ]
    far_mate = lax.rem(mate + 2, 4)
    pass_out = [
        send(piece(far, i), piece(far, i), pass_send.at[i], pass_recv.at[i], mate)
        for i in range(PARTS)
    ]
    pass_in = [
        send(piece(far_mate, i), piece(far_mate, i), pass_send.at[i], pass_recv.at[i], mate)
        for i in range(PARTS)
    ]
    for copy in gather_out:
        copy.start()
    own_out.start()
    for g in range(OWN):
        route_copy(g).start()

    def two_blocks(index):
        return pl.ds(pl.multiple_of(index * 2 * tok, 2 * tok), 2 * tok)

    def project(index):
        rows = two_blocks(index)

        @pl.loop(0, heads // 2)
        def _(p):
            cols = pl.ds(pl.multiple_of(p * 6 * HEAD, 6 * HEAD), 6 * HEAD)
            both = jnp.dot(
                everyone[rows, :], w_qkv[:, cols], preferred_element_type=jnp.float32
            ).astype(jnp.bfloat16)
            q_cols = pl.ds(pl.multiple_of(p * 2 * HEAD, 2 * HEAD), 2 * HEAD)
            kv_cols = pl.ds(pl.multiple_of(p * 4 * HEAD, 4 * HEAD), 4 * HEAD)
            queries[rows, q_cols] = jnp.concatenate(
                [both[:, 0:HEAD], both[:, 3 * HEAD : 4 * HEAD]], axis=1
            )
            keys_values[rows, kv_cols] = jnp.concatenate(
                [both[:, HEAD : 3 * HEAD], both[:, 4 * HEAD :]], axis=1
            )

    tokens = tok
    expert = in_plane(blk, core, lax.broadcasted_iota(jnp.int32, (PLANE, 1), 0), 1)
    slot = lax.broadcasted_iota(jnp.int32, (PLANE, CAP, tokens), 1)

    own_rows = slice(OWN * tokens, RING * tokens)

    def rank_tokens():
        upto = lax.broadcasted_iota(jnp.int32, (tokens, tokens), 0) <= lax.broadcasted_iota(
            jnp.int32, (tokens, tokens), 1
        )
        for g in range(RING):
            if g != OWN:
                route_copy(g).wait_recv()
            chosen = jnp.zeros((PLANE, tokens), jnp.int32)
            for k in range(routes_ref.shape[0]):
                named = routes_ref[k : k + 1, :] if g == OWN else routed[g, k : k + 1, :]
                chosen = jnp.where(named == expert, 1, chosen)
            count = jnp.dot(
                chosen.astype(jnp.bfloat16),
                jnp.where(upto, 1.0, 0.0).astype(jnp.bfloat16),
                preferred_element_type=jnp.float32,
            ).astype(jnp.int32)
            rank[g] = jnp.where(chosen == 1, count - 1, -1)

    def hits(g):
        return rank[g][:, None, :] == slot

    segment_row = segment_ref[...]
    segment_column = jnp.broadcast_to(segment_row, (HEAD, length)).T

    loads = width // LOAD

    @pl.loop(0, loads)
    def _(i):
        load_qkv(i).wait()

        @pl.loop(0, LOAD // TURN)
        def _(t):
            some = staged[lax.rem(i, 2), pl.ds(pl.multiple_of(t * TURN, TURN), TURN)]
            rows = pl.ds(pl.multiple_of(i * LOAD + t * TURN, TURN), TURN)
            for head in range(heads):
                w_qkv[rows, head * columns : (head + 1) * columns] = some[:, head, :]

        @pl.when(i < loads - 2)
        def _():
            load_qkv(i + 2).start()

    load_out.wait()
    load_gate_up.start()
    load_down.start()
    own_in.wait_recv()
    for i in range(PARTS // 2):
        gather_in[i].wait_recv()
        pass_out[i].start()
    project(half)
    rank_tokens()
    for i in range(PARTS // 2, PARTS):
        gather_in[i].wait_recv()
        pass_out[i].start()
    for i in range(PARTS):
        pass_in[i].wait_recv()
    project(1 - half)

    def page_copy(j):
        to_blk = place_at(blk, j, core, 1)
        return pltpu.make_async_remote_copy(
            src_ref=pages_ref.at[to_blk],
            dst_ref=kv_ref.at[blk],
            send_sem=kv_send.at[j],
            recv_sem=kv_recv.at[j],
            device_id=(seq, to_blk),
            device_id_type=MESH,
        )

    def page_arrival(j):
        from_blk = place_at(blk, j, core, -1)
        return pltpu.make_async_remote_copy(
            src_ref=pages_ref.at[from_blk],
            dst_ref=kv_ref.at[from_blk],
            send_sem=kv_send.at[j],
            recv_sem=kv_recv.at[j],
            device_id=(seq, from_blk),
            device_id_type=MESH,
        )

    def attend(index):
        rows = two_blocks(index)
        picked = jnp.where(index == 0, segment_column[0 : 2 * tok], segment_column[2 * tok :])
        same = picked[:, 0:1] == segment_row

        @pl.loop(0, heads)
        def _(head):
            cols = pl.ds(pl.multiple_of(head * HEAD, HEAD), HEAD)
            k_cols = pl.ds(pl.multiple_of(head * 2 * HEAD, HEAD), HEAD)
            v_cols = pl.ds(pl.multiple_of(head * 2 * HEAD + HEAD, HEAD), HEAD)
            scores = lax.dot_general(
                queries[rows, cols],
                keys_values[:, k_cols],
                (((1,), (1,)), ((), ())),
                preferred_element_type=jnp.float32,
            ) * (1.0 / math.sqrt(HEAD))
            scores = jnp.where(same, scores, -1e30)
            weights = jnp.exp(scores - jnp.max(scores, axis=-1, keepdims=True))
            probs = (weights / jnp.sum(weights, axis=-1, keepdims=True)).astype(jnp.bfloat16)
            context[rows, cols] = jnp.dot(
                probs, keys_values[:, v_cols], preferred_element_type=jnp.float32
            ).astype(jnp.bfloat16)

    def column(n):
        return pl.ds(n * SPAN, SPAN)

    def strip(r):
        return pl.ds(r * PIECE, PIECE)

    def near_copy(which, r):
        return send(
            near_send.at[which, strip(r)],
            near_recv.at[which, strip(r)],
            near_send_sems.at[which, r],
            near_recv_sems.at[which, r],
            mate,
        )

    def far_copy(r):
        return send(
            far_send.at[strip(r)],
            far_recv.at[strip(r)],
            far_send_sems.at[r],
            far_recv_sems.at[r],
            far,
        )

    strips = tok // PIECE

    def mix(which, index):
        for n in range(width // SPAN):
            partial[:, column(n)] = jnp.dot(
                context[two_blocks(index), :],
                w_out[:, column(n)],
                preferred_element_type=jnp.float32,
            )
            near_send[which, :, column(n)] = partial[block(1 - core), column(n)].astype(
                jnp.bfloat16
            )
        for r in range(strips):
            near_copy(which, r).start()

    def reduced(which, r):
        near_copy(which, r).wait_recv()
        own = partial[pl.ds(pl.multiple_of(core * tok + r * PIECE, PIECE), PIECE), :]
        return own + near_recv[which, strip(r), :].astype(jnp.float32)

    def ring_piece(g, i):
        rows = pl.ds(pl.multiple_of(OWN * tokens + i * PIECE, PIECE), PIECE)
        to_rows = pl.ds(pl.multiple_of(g * tokens + i * PIECE, PIECE), PIECE)
        return pltpu.make_async_remote_copy(
            src_ref=blocks.at[rows],
            dst_ref=blocks.at[to_rows],
            send_sem=ring_send.at[g],
            recv_sem=ring_recv.at[g],
            device_id=(seq, along_ring(blk, core, SHIFTS[g])),
            device_id_type=MESH,
        )

    attend(1 - half)
    mix(0, 1 - half)
    for r in range(strips):
        far_send[strip(r), :] = reduced(0, r).astype(jnp.bfloat16)
        far_copy(r).start()
    page = length // NPOS
    spread_owner = lax.div(
        lax.broadcasted_iota(jnp.int32, (NPOS, length), 1), page
    ) == lax.broadcasted_iota(jnp.int32, (NPOS, length), 0)
    owners = jnp.dot(
        jnp.broadcast_to(owner_ref[...], (8, NPOS)).astype(jnp.bfloat16),
        jnp.where(spread_owner, 1.0, 0.0).astype(jnp.bfloat16),
        preferred_element_type=jnp.float32,
    ).astype(jnp.int32)[0:1]
    to_row = lax.broadcasted_iota(jnp.int32, (length, length), 0)
    from_row = lax.broadcasted_iota(jnp.int32, (length, length), 1)
    moves = (lax.rem(to_row, page) == lax.rem(from_row, page)) & (
        lax.div(to_row, page) == owners
    )
    pages_ref[...] = (
        jnp.dot(
            jnp.where(moves, 1.0, 0.0).astype(jnp.bfloat16),
            keys_values[...],
            preferred_element_type=jnp.float32,
        )
        .astype(jnp.bfloat16)
        .reshape(pages_ref.shape)
    )
    own_page = pltpu.make_async_copy(pages_ref.at[blk], kv_ref.at[blk], kv_local_sem)
    own_page.start()
    lax.fori_loop(1, NPOS, lambda j, _: (page_copy(j).start(), 0)[1], 0)

    attend(half)
    mix(1, half)
    for r in range(strips):
        mixed = reduced(1, r)
        far_copy(r).wait_recv()
        mixed = mixed + far_recv[strip(r), :].astype(jnp.float32)
        summed = (rows_ref[strip(r), :].astype(jnp.float32) + mixed).astype(jnp.bfloat16)
        resid[strip(r), :] = summed
        blocks[pl.ds(OWN * tokens + r * PIECE, PIECE), :] = norm(
            summed.astype(jnp.float32), ffn_gain_ref
        )
        for g in range(OWN):
            ring_piece(g, r).start()
    own_out.wait_send()
    for i in range(PARTS):
        gather_out[i].wait_send()
        pass_out[i].wait_send()

    def ring_all(g):
        return pltpu.make_async_remote_copy(
            src_ref=blocks.at[own_rows],
            dst_ref=blocks.at[pl.ds(g * tokens, tokens)],
            send_sem=ring_send.at[g],
            recv_sem=ring_recv.at[g],
            device_id=(mate, blk),
            device_id_type=MESH,
        )

    def sum_piece(g, i):
        rows = pl.ds(pl.multiple_of(i * PIECE, PIECE), PIECE)
        return pltpu.make_async_remote_copy(
            src_ref=sums_out.at[g, rows],
            dst_ref=sums_in.at[g, rows],
            send_sem=sum_send.at[g],
            recv_sem=sum_recv.at[g],
            device_id=(seq, along_ring(blk, core, -SHIFTS[g])),
            device_id_type=MESH,
        )

    def sum_all(g):
        return pltpu.make_async_remote_copy(
            src_ref=sums_out.at[g],
            dst_ref=sums_in.at[g],
            send_sem=sum_send.at[g],
            recv_sem=sum_recv.at[g],
            device_id=(mate, blk),
            device_id_type=MESH,
        )

    def slab(g, p):
        return pl.ds(pl.multiple_of(g * ROWS + p * CAP, SUB), CAP)

    def others(g):
        return pl.ds(pl.multiple_of(g * ROWS + CAP, SUB), ROWS - CAP)

    def nth(g, i):
        p = lax.rem((lax.rem(i, PLANE - 1) + 1) * 3, PLANE)
        start = g * ROWS + p * CAP + lax.div(i, PLANE - 1) * SUB
        return p, pl.ds(pl.multiple_of(start, SUB), SUB)

    def dispatch(g, i):
        p, rows = nth(g, i)
        return pltpu.make_async_remote_copy(
            src_ref=packed.at[rows],
            dst_ref=recv.at[rows],
            send_sem=out_send.at[g],
            recv_sem=out_recv.at[g],
            device_id=plane_peer(blk, seq, p, 1),
            device_id_type=MESH,
        )

    def give_back(g, i):
        p, rows = nth(g, i)
        return pltpu.make_async_remote_copy(
            src_ref=sent.at[rows],
            dst_ref=ret.at[rows],
            send_sem=back_send.at[g],
            recv_sem=back_recv.at[g],
            device_id=plane_peer(blk, seq, p, -1),
            device_id_type=MESH,
        )

    def dispatch_all(g):
        return pltpu.make_async_remote_copy(
            src_ref=packed.at[others(g)],
            dst_ref=recv.at[others(g)],
            send_sem=out_send.at[g],
            recv_sem=out_recv.at[g],
            device_id=(mate, blk),
            device_id_type=MESH,
        )

    def give_back_all(g):
        return pltpu.make_async_remote_copy(
            src_ref=sent.at[others(g)],
            dst_ref=ret.at[others(g)],
            send_sem=back_send.at[g],
            recv_sem=back_recv.at[g],
            device_id=(mate, blk),
            device_id_type=MESH,
        )

    def pack(g):
        one_hot = jnp.where(hits(g), 1.0, 0.0).reshape(ROWS, tokens).astype(jnp.bfloat16)
        rows = pl.ds(g * ROWS, ROWS)

        @pl.loop(0, width // 512)
        def _(n):
            cols = pl.ds(pl.multiple_of(n * 512, 512), 512)
            packed[rows, cols] = jnp.dot(
                one_hot,
                blocks[g * tokens : (g + 1) * tokens, cols],
                preferred_element_type=jnp.float32,
            ).astype(jnp.bfloat16)

    copies = (PLANE - 1) * (CAP // SUB)
    pieces = tokens // PIECE
    for g in range(RING):
        if g != OWN:
            ring_all(g).wait_recv()
        pack(g)
        lax.fori_loop(0, copies, lambda i, _: (dispatch(g, i).start(), 0)[1], 0)
        recv[slab(g, 0), :] = packed[slab(g, 0), :]

    order = jnp.where(
        expert == lax.broadcasted_iota(jnp.int32, (PLANE, NPOS), 1), 1.0, 0.0
    ).astype(jnp.bfloat16)
    for g in range(RING):
        logits = lax.dot_general(
            router_ref[...],
            blocks[g * tokens : (g + 1) * tokens, :],
            (((1,), (1,)), ((), ())),
            preferred_element_type=jnp.float32,
        )
        gates[g] = jnp.dot(
            order,
            jax.nn.sigmoid(logits).astype(jnp.bfloat16),
            preferred_element_type=jnp.float32,
        )

    load_gate_up.wait()
    load_down.wait()
    ff = down.shape[0]

    @pl.loop(0, RING)
    def _(g):
        dispatch_all(g).wait_recv()
        rows = pl.ds(pl.multiple_of(g * ROWS, ROWS), ROWS)

        @pl.loop(0, ff // TILE)
        def _(f):
            cols = pl.ds(pl.multiple_of(f * TILE, TILE), TILE)
            up_cols = pl.ds(pl.multiple_of(ff + f * TILE, TILE), TILE)
            gate = jnp.dot(recv[rows, :], gate_up[:, cols], preferred_element_type=jnp.float32)
            up = jnp.dot(recv[rows, :], gate_up[:, up_cols], preferred_element_type=jnp.float32)
            hidden[:, cols] = (jax.nn.silu(gate) * up).astype(jnp.bfloat16)

        @pl.loop(0, width // TILE)
        def _(n):
            cols = pl.ds(pl.multiple_of(n * TILE, TILE), TILE)
            sent[rows, cols] = jnp.dot(
                hidden[...], down[:, cols], preferred_element_type=jnp.float32
            ).astype(jnp.bfloat16)

        lax.fori_loop(0, copies, lambda i, _: (give_back(g, i).start(), 0)[1], 0)
        ret[slab(g, 0), :] = sent[slab(g, 0), :]

    for g in range(RING):
        spread = jnp.where(hits(g), gates[g][:, None, :], 0.0).reshape(ROWS, tokens)
        spread = spread.T.astype(jnp.bfloat16)
        give_back_all(g).wait_recv()

        @pl.loop(0, width // 512)
        def _(n):
            cols = pl.ds(pl.multiple_of(n * 512, 512), 512)
            mixture = jnp.dot(
                spread,
                ret[g * ROWS : (g + 1) * ROWS, cols],
                preferred_element_type=jnp.float32,
            )
            if g == OWN:
                total[:, cols] = resid[:, cols].astype(jnp.float32) + mixture
            else:
                sums_out[g, :, cols] = mixture.astype(jnp.bfloat16)

        if g != OWN:
            lax.fori_loop(0, pieces, lambda i, _: (sum_piece(g, i).start(), 0)[1], 0)

    for g in range(OWN):
        sum_all(g).wait_recv()
    summed = total[...]
    for g in range(OWN):
        summed = summed + sums_in[g].astype(jnp.float32)
    out_ref[...] = summed.astype(jnp.bfloat16)

    def drain(j, _):
        page_arrival(j).wait_recv()
        page_copy(j).wait_send()
        return 0

    lax.fori_loop(1, NPOS, drain, 0)
    for g in range(RING):
        dispatch_all(g).wait_send()
        give_back_all(g).wait_send()
        if g != OWN:
            route_copy(g).wait_send()
            ring_all(g).wait_send()
            sum_all(g).wait_send()
    own_page.wait()
    for r in range(strips):
        near_copy(0, r).wait_send()
        near_copy(1, r).wait_send()
        far_copy(r).wait_send()


def on_device(
    residual_in,
    segment_ids,
    attn_gain,
    w_qkv,
    w_out,
    ffn_gain,
    w_router,
    routes,
    w_gate_up,
    w_down,
    page_owner,
):
    tokens, width = residual_in.shape[1:]
    heads = w_qkv.shape[1]
    length = segment_ids.shape[1]
    page = length // NPOS
    ff = w_down.shape[1]
    slots = NPOS * CAP
    vmem = pl.BlockSpec(memory_space=pltpu.VMEM)
    hbm = pl.BlockSpec(memory_space=pl.ANY)
    dma = pltpu.SemaphoreType.DMA
    bf16 = jnp.bfloat16
    strips = tokens // PIECE
    residual_out, kv_cache = pl.pallas_call(
        layer_kernel,
        out_shape=(
            jax.ShapeDtypeStruct((tokens, width), bf16),
            jax.ShapeDtypeStruct((NPOS, page, heads * 2 * HEAD), bf16),
        ),
        in_specs=[vmem] * 7 + [hbm] * 4,
        out_specs=(vmem, hbm),
        scratch_shapes=[
            pltpu.VMEM((length, heads * HEAD), bf16),
            pltpu.VMEM((length, heads * 2 * HEAD), bf16),
            pltpu.VMEM((NPOS, page, heads * 2 * HEAD), bf16),
            pltpu.VMEM((length, heads * HEAD), bf16),
            pltpu.VMEM((2 * tokens, width), jnp.float32),
            pltpu.VMEM((2, tokens, width), bf16),
            pltpu.VMEM((2, tokens, width), bf16),
            pltpu.VMEM((tokens, width), bf16),
            pltpu.VMEM((tokens, width), bf16),
            pltpu.VMEM((tokens, width), bf16),
            pltpu.VMEM((RING * tokens, width), bf16),
            pltpu.VMEM((RING,) + routes.shape[2:] + (tokens,), jnp.int32),
            pltpu.VMEM((RING - 1, tokens, width), bf16),
            pltpu.VMEM((RING - 1, tokens, width), bf16),
            pltpu.VMEM((RING, PLANE, tokens), jnp.int32),
            pltpu.VMEM((RING, PLANE, tokens), jnp.float32),
            pltpu.VMEM((slots, width), bf16),
            pltpu.VMEM((slots, width), bf16),
            pltpu.VMEM((max(slots, width), width), bf16),
            pltpu.VMEM((slots, width), bf16),
            pltpu.VMEM((ROWS, ff), bf16),
            pltpu.VMEM((width, 2 * ff), bf16),
            pltpu.VMEM((ff, width), bf16),
            pltpu.VMEM((tokens, width), jnp.float32),
            dma((4,)),
            dma,
            dma((RING,)),
            dma((RING,)),
            dma((RING,)),
            dma((RING,)),
            dma((NPOS,)),
            dma((NPOS,)),
            dma((2,)),
            dma((PARTS,)),
            dma((PARTS,)),
            dma((PARTS,)),
            dma((PARTS,)),
            dma((2, strips)),
            dma((2, strips)),
            dma((strips,)),
            dma((strips,)),
            pltpu.VMEM((2, LOAD) + w_qkv.shape[1:], bf16),
            dma((2,)),
            dma((RING,)),
            dma((RING,)),
            dma((RING,)),
            dma((RING,)),
            dma((RING,)),
            dma((RING,)),
        ],
        compiler_params=pltpu.CompilerParams(
            collective_id=0, has_side_effects=True, vmem_limit_bytes=60 << 20
        ),
    )(
        residual_in[0],
        segment_ids,
        page_owner,
        attn_gain,
        ffn_gain,
        w_router.T,
        routes[0].T,
        w_qkv,
        w_out.reshape(heads * HEAD, width),
        w_gate_up[0],
        w_down[0],
    )
    return (residual_out[None], kv_cache[None])


def solution(mesh):
    in_specs = (
        P("blk", "seq", None),
        P("blk", None),
        P(),
        P(None, "seq", None),
        P("seq", None, None),
        P(),
        P(),
        P("blk", "seq", None),
        P("blk", None, None),
        P("blk", None, None),
        P("blk", None),
    )
    out_specs = (P("blk", "seq", None), P("blk", None, None, "seq"))
    return jax.shard_map(
        on_device, mesh=mesh, in_specs=in_specs, out_specs=out_specs, check_vma=False
    )
```

```python
import math

import jax
import jax.numpy as jnp
from jax import lax
from jax.experimental import pallas as pl
from jax.experimental.pallas import tpu as pltpu
from jax.sharding import PartitionSpec as P

EPS = 1e-06
NPOS = 32
CAP = 48
SUB = 16
RING = 4
PLANE = 8
ROWS = PLANE * CAP
PIECE = 32
LOAD = 256
TURN = 64
TILE = 256
HEAD = 128
PARTS = 4
SPAN = 512
MESH = pl.DeviceIdType.MESH
SHIFTS = (1, 3, 2, 0)
OWN = RING - 1


def step_of(position, core):
    k = lax.rem(position * 11, NPOS)
    dx, dz, dy = lax.div(k, 16), lax.rem(lax.div(k, 4), 4), lax.rem(k, 4)
    return dx, dz + core * (dy - dz), dy + core * (dz - dy)


def place_at(blk, position, core, sign):
    dx, dz, dy = step_of(position, core)
    x, z, y = lax.div(blk, 16), lax.rem(lax.div(blk, 4), 4), lax.rem(blk, 4)
    x = lax.rem(x + dx, 2)
    z = lax.rem(z + 4 + sign * dz, 4)
    y = lax.rem(y + 4 + sign * dy, 4)
    return (x * 4 + z) * 4 + y


def locate(blk, core):
    x, z, y = lax.div(blk, 16), lax.rem(lax.div(blk, 4), 4), lax.rem(blk, 4)
    return x, z + core * (y - z), y + core * (z - y)


def index_of(x, u, v, core):
    z, y = u + core * (v - u), v + core * (u - v)
    return (x * 4 + z) * 4 + y


def along_ring(blk, core, shift):
    x, u, v = locate(blk, core)
    return index_of(x, lax.rem(u + 4 + shift, 4), v, core)


def in_plane(blk, core, position, sign):
    x, u, v = locate(blk, core)
    dx, dv = lax.div(position, 4), lax.rem(position, 4)
    return index_of(lax.rem(x + dx, 2), u, lax.rem(v + 4 + sign * dv, 4), core)


def plane_peer(blk, seq, position, sign):
    core = lax.rem(seq, 2)
    dx, dv = lax.div(position, 4), lax.rem(position, 4)
    other = 2 * dx * (1 - lax.rem(dv, 2))
    return lax.rem(seq + other, 4), in_plane(blk, core, position, sign)


def layer_kernel(
    rows_ref,
    segment_ref,
    owner_ref,
    attn_gain_ref,
    ffn_gain_ref,
    router_ref,
    routes_ref,
    qkv_hbm,
    out_hbm,
    gate_up_hbm,
    down_hbm,
    out_ref,
    kv_ref,
    queries,
    keys_values,
    pages_ref,
    context,
    partial,
    near_send,
    near_recv,
    far_send,
    far_recv,
    resid,
    blocks,
    routed,
    sums_out,
    sums_in,
    rank,
    gates,
    packed,
    recv,
    sent,
    ret,
    hidden,
    gate_up,
    down,
    total,
    weight_sems,
    kv_local_sem,
    out_send,
    out_recv,
    back_send,
    back_recv,
    kv_send,
    kv_recv,
    own_sems,
    gather_send,
    gather_recv,
    pass_send,
    pass_recv,
    near_send_sems,
    near_recv_sems,
    far_send_sems,
    far_recv_sems,
    staged,
    stage_sems,
    route_send,
    route_recv,
    ring_send,
    ring_recv,
    sum_send,
    sum_recv,
):
    blk = lax.axis_index("blk")
    seq = lax.axis_index("seq")
    half = lax.div(seq, 2)
    core = lax.rem(seq, 2)
    mate = seq + 1 - 2 * core
    far = lax.rem(seq + 2, 4)
    tok = rows_ref.shape[0]
    width = rows_ref.shape[1]
    length = 4 * tok
    heads = out_hbm.shape[0] // HEAD
    columns = qkv_hbm.shape[2]
    w_qkv = sent.at[0:width, 0 : heads * columns]
    w_out = packed.at[0 : out_hbm.shape[0]]
    everyone = packed.at[out_hbm.shape[0] : out_hbm.shape[0] + length]

    def load_qkv(i):
        rows = pl.ds(pl.multiple_of(i * LOAD, LOAD), LOAD)
        return pltpu.make_async_copy(
            qkv_hbm.at[rows], staged.at[lax.rem(i, 2)], stage_sems.at[lax.rem(i, 2)]
        )

    load_out = pltpu.make_async_copy(out_hbm, w_out, weight_sems.at[3])
    load_gate_up = pltpu.make_async_copy(gate_up_hbm, gate_up, weight_sems.at[0])
    load_down = pltpu.make_async_copy(down_hbm, down, weight_sems.at[1])
    load_qkv(0).start()
    load_qkv(1).start()
    load_out.start()

    barrier = pltpu.get_barrier_semaphore()

    def greet(j, _):
        pl.semaphore_signal(
            barrier,
            inc=1,
            device_id=(seq, place_at(blk, j, core, 1)),
            device_id_type=MESH,
        )
        return 0

    lax.fori_loop(1, NPOS, greet, 0)
    for crossing in (4, 6):
        pl.semaphore_signal(
            barrier,
            inc=1,
            device_id=plane_peer(blk, seq, crossing, 1),
            device_id_type=MESH,
        )
    for other in (mate, far):
        pl.semaphore_signal(barrier, inc=1, device_id=(other, blk), device_id_type=MESH)

    def block(index):
        return pl.ds(pl.multiple_of(index * tok, tok), tok)

    def norm(wide, gain_ref):
        scale = lax.rsqrt(jnp.mean(wide * wide, axis=-1, keepdims=True) + EPS)
        return (wide * scale * gain_ref[...].astype(jnp.float32).reshape(1, width)).astype(jnp.bfloat16)

    def send(src, dst, send_sem, recv_sem, to):
        return pltpu.make_async_remote_copy(
            src_ref=src,
            dst_ref=dst,
            send_sem=send_sem,
            recv_sem=recv_sem,
            device_id=(to, blk),
            device_id_type=MESH,
        )

    def piece(index, i):
        rows = tok // PARTS
        return everyone.at[pl.ds(pl.multiple_of(index * tok + i * rows, rows), rows)]

    everyone[block(seq), :] = norm(rows_ref[...].astype(jnp.float32), attn_gain_ref)
    pl.semaphore_wait(barrier, NPOS - 1 + 2 + 2)

    def route_copy(g):
        return pltpu.make_async_remote_copy(
            src_ref=routes_ref,
            dst_ref=routed.at[g],
            send_sem=route_send.at[g],
            recv_sem=route_recv.at[g],
            device_id=(seq, along_ring(blk, core, SHIFTS[g])),
            device_id_type=MESH,
        )


    own_out = send(
        everyone.at[block(seq)], everyone.at[block(seq)], own_sems.at[0], own_sems.at[1], mate
    )
    own_in = send(
        everyone.at[block(mate)], everyone.at[block(mate)], own_sems.at[0], own_sems.at[1], mate
    )
    gather_out = [
        send(piece(seq, i), piece(seq, i), gather_send.at[i], gather_recv.at[i], far)
        for i in range(PARTS)
    ]
    gather_in = [
        send(piece(far, i), piece(far, i), gather_send.at[i], gather_recv.at[i], far)
        for i in range(PARTS)
    ]
    far_mate = lax.rem(mate + 2, 4)
    pass_out = [
        send(piece(far, i), piece(far, i), pass_send.at[i], pass_recv.at[i], mate)
        for i in range(PARTS)
    ]
    pass_in = [
        send(piece(far_mate, i), piece(far_mate, i), pass_send.at[i], pass_recv.at[i], mate)
        for i in range(PARTS)
    ]
    for copy in gather_out:
        copy.start()
    own_out.start()
    for g in range(OWN):
        route_copy(g).start()

    def two_blocks(index):
        return pl.ds(pl.multiple_of(index * 2 * tok, 2 * tok), 2 * tok)

    def project(index):
        rows = two_blocks(index)

        @pl.loop(0, heads // 2)
        def _(p):
            cols = pl.ds(pl.multiple_of(p * 6 * HEAD, 6 * HEAD), 6 * HEAD)
            both = jnp.dot(
                everyone[rows, :], w_qkv[:, cols], preferred_element_type=jnp.float32
            ).astype(jnp.bfloat16)
            q_cols = pl.ds(pl.multiple_of(p * 2 * HEAD, 2 * HEAD), 2 * HEAD)
            kv_cols = pl.ds(pl.multiple_of(p * 4 * HEAD, 4 * HEAD), 4 * HEAD)
            queries[rows, q_cols] = jnp.concatenate(
                [both[:, 0:HEAD], both[:, 3 * HEAD : 4 * HEAD]], axis=1
            )
            keys_values[rows, kv_cols] = jnp.concatenate(
                [both[:, HEAD : 3 * HEAD], both[:, 4 * HEAD :]], axis=1
            )

    tokens = tok
    expert = in_plane(blk, core, lax.broadcasted_iota(jnp.int32, (PLANE, 1), 0), 1)
    slot = lax.broadcasted_iota(jnp.int32, (PLANE, CAP, tokens), 1)

    own_rows = slice(OWN * tokens, RING * tokens)

    def rank_tokens():
        upto = lax.broadcasted_iota(jnp.int32, (tokens, tokens), 0) <= lax.broadcasted_iota(
            jnp.int32, (tokens, tokens), 1
        )
        for g in range(RING):
            if g != OWN:
                route_copy(g).wait_recv()
            chosen = jnp.zeros((PLANE, tokens), jnp.int32)
            for k in range(routes_ref.shape[0]):
                named = routes_ref[k : k + 1, :] if g == OWN else routed[g, k : k + 1, :]
                chosen = jnp.where(named == expert, 1, chosen)
            count = jnp.dot(
                chosen.astype(jnp.bfloat16),
                jnp.where(upto, 1.0, 0.0).astype(jnp.bfloat16),
                preferred_element_type=jnp.float32,
            ).astype(jnp.int32)
            rank[g] = jnp.where(chosen == 1, count - 1, -1)

    def hits(g):
        return rank[g][:, None, :] == slot

    segment_row = segment_ref[...]
    segment_column = jnp.broadcast_to(segment_row, (HEAD, length)).T

    loads = width // LOAD

    @pl.loop(0, loads)
    def _(i):
        load_qkv(i).wait()

        @pl.loop(0, LOAD // TURN)
        def _(t):
            some = staged[lax.rem(i, 2), pl.ds(pl.multiple_of(t * TURN, TURN), TURN)]
            rows = pl.ds(pl.multiple_of(i * LOAD + t * TURN, TURN), TURN)
            for head in range(heads):
                w_qkv[rows, head * columns : (head + 1) * columns] = some[:, head, :]

        @pl.when(i < loads - 2)
        def _():
            load_qkv(i + 2).start()

    load_out.wait()
    load_gate_up.start()
    load_down.start()
    own_in.wait_recv()
    for i in range(PARTS // 2):
        gather_in[i].wait_recv()
        pass_out[i].start()
    project(half)
    rank_tokens()
    for i in range(PARTS // 2, PARTS):
        gather_in[i].wait_recv()
        pass_out[i].start()
    for i in range(PARTS):
        pass_in[i].wait_recv()
    project(1 - half)

    def page_copy(j):
        to_blk = place_at(blk, j, core, 1)
        return pltpu.make_async_remote_copy(
            src_ref=pages_ref.at[to_blk],
            dst_ref=kv_ref.at[blk],
            send_sem=kv_send.at[j],
            recv_sem=kv_recv.at[j],
            device_id=(seq, to_blk),
            device_id_type=MESH,
        )

    def page_arrival(j):
        from_blk = place_at(blk, j, core, -1)
        return pltpu.make_async_remote_copy(
            src_ref=pages_ref.at[from_blk],
            dst_ref=kv_ref.at[from_blk],
            send_sem=kv_send.at[j],
            recv_sem=kv_recv.at[j],
            device_id=(seq, from_blk),
            device_id_type=MESH,
        )

    def attend(index):
        rows = two_blocks(index)
        picked = jnp.where(index == 0, segment_column[0 : 2 * tok], segment_column[2 * tok :])
        same = picked[:, 0:1] == segment_row

        @pl.loop(0, heads)
        def _(head):
            cols = pl.ds(pl.multiple_of(head * HEAD, HEAD), HEAD)
            k_cols = pl.ds(pl.multiple_of(head * 2 * HEAD, HEAD), HEAD)
            v_cols = pl.ds(pl.multiple_of(head * 2 * HEAD + HEAD, HEAD), HEAD)
            scores = lax.dot_general(
                queries[rows, cols],
                keys_values[:, k_cols],
                (((1,), (1,)), ((), ())),
                preferred_element_type=jnp.float32,
            ) * (1.0 / math.sqrt(HEAD))
            scores = jnp.where(same, scores, -1e30)
            weights = jnp.exp(scores - jnp.max(scores, axis=-1, keepdims=True))
            probs = (weights / jnp.sum(weights, axis=-1, keepdims=True)).astype(jnp.bfloat16)
            context[rows, cols] = jnp.dot(
                probs, keys_values[:, v_cols], preferred_element_type=jnp.float32
            ).astype(jnp.bfloat16)

    def column(n):
        return pl.ds(n * SPAN, SPAN)

    def strip(r):
        return pl.ds(r * PIECE, PIECE)

    def near_copy(which, r):
        return send(
            near_send.at[which, strip(r)],
            near_recv.at[which, strip(r)],
            near_send_sems.at[which, r],
            near_recv_sems.at[which, r],
            mate,
        )

    def far_copy(r):
        return send(
            far_send.at[strip(r)],
            far_recv.at[strip(r)],
            far_send_sems.at[r],
            far_recv_sems.at[r],
            far,
        )

    strips = tok // PIECE

    def mix(which, index):
        for n in range(width // SPAN):
            partial[:, column(n)] = jnp.dot(
                context[two_blocks(index), :],
                w_out[:, column(n)],
                preferred_element_type=jnp.float32,
            )
            near_send[which, :, column(n)] = partial[block(1 - core), column(n)].astype(
                jnp.bfloat16
            )
        for r in range(strips):
            near_copy(which, r).start()

    def reduced(which, r):
        near_copy(which, r).wait_recv()
        own = partial[pl.ds(pl.multiple_of(core * tok + r * PIECE, PIECE), PIECE), :]
        return own + near_recv[which, strip(r), :].astype(jnp.float32)

    def ring_piece(g, i):
        rows = pl.ds(pl.multiple_of(OWN * tokens + i * PIECE, PIECE), PIECE)
        to_rows = pl.ds(pl.multiple_of(g * tokens + i * PIECE, PIECE), PIECE)
        return pltpu.make_async_remote_copy(
            src_ref=blocks.at[rows],
            dst_ref=blocks.at[to_rows],
            send_sem=ring_send.at[g],
            recv_sem=ring_recv.at[g],
            device_id=(seq, along_ring(blk, core, SHIFTS[g])),
            device_id_type=MESH,
        )

    page = length // NPOS
    spread_owner = lax.div(
        lax.broadcasted_iota(jnp.int32, (NPOS, length), 1), page
    ) == lax.broadcasted_iota(jnp.int32, (NPOS, length), 0)
    owners = jnp.dot(
        jnp.broadcast_to(owner_ref[...], (8, NPOS)).astype(jnp.bfloat16),
        jnp.where(spread_owner, 1.0, 0.0).astype(jnp.bfloat16),
        preferred_element_type=jnp.float32,
    ).astype(jnp.int32)[0:1]
    to_row = lax.broadcasted_iota(jnp.int32, (length, length), 0)
    from_row = lax.broadcasted_iota(jnp.int32, (length, length), 1)
    moves = (lax.rem(to_row, page) == lax.rem(from_row, page)) & (
        lax.div(to_row, page) == owners
    )
    pages_ref[...] = (
        jnp.dot(
            jnp.where(moves, 1.0, 0.0).astype(jnp.bfloat16),
            keys_values[...],
            preferred_element_type=jnp.float32,
        )
        .astype(jnp.bfloat16)
        .reshape(pages_ref.shape)
    )
    own_page = pltpu.make_async_copy(pages_ref.at[blk], kv_ref.at[blk], kv_local_sem)
    own_page.start()
    lax.fori_loop(1, NPOS, lambda j, _: (page_copy(j).start(), 0)[1], 0)

    attend(1 - half)
    mix(0, 1 - half)
    for r in range(strips):
        far_send[strip(r), :] = reduced(0, r).astype(jnp.bfloat16)
        far_copy(r).start()
    attend(half)
    mix(1, half)
    for r in range(strips):
        mixed = reduced(1, r)
        far_copy(r).wait_recv()
        mixed = mixed + far_recv[strip(r), :].astype(jnp.float32)
        summed = (rows_ref[strip(r), :].astype(jnp.float32) + mixed).astype(jnp.bfloat16)
        resid[strip(r), :] = summed
        blocks[pl.ds(OWN * tokens + r * PIECE, PIECE), :] = norm(
            summed.astype(jnp.float32), ffn_gain_ref
        )
        for g in range(OWN):
            ring_piece(g, r).start()
    own_out.wait_send()
    for i in range(PARTS):
        gather_out[i].wait_send()
        pass_out[i].wait_send()

    def ring_all(g):
        return pltpu.make_async_remote_copy(
            src_ref=blocks.at[own_rows],
            dst_ref=blocks.at[pl.ds(g * tokens, tokens)],
            send_sem=ring_send.at[g],
            recv_sem=ring_recv.at[g],
            device_id=(mate, blk),
            device_id_type=MESH,
        )

    def sum_piece(g, i):
        rows = pl.ds(pl.multiple_of(i * PIECE, PIECE), PIECE)
        return pltpu.make_async_remote_copy(
            src_ref=sums_out.at[g, rows],
            dst_ref=sums_in.at[g, rows],
            send_sem=sum_send.at[g],
            recv_sem=sum_recv.at[g],
            device_id=(seq, along_ring(blk, core, -SHIFTS[g])),
            device_id_type=MESH,
        )

    def sum_all(g):
        return pltpu.make_async_remote_copy(
            src_ref=sums_out.at[g],
            dst_ref=sums_in.at[g],
            send_sem=sum_send.at[g],
            recv_sem=sum_recv.at[g],
            device_id=(mate, blk),
            device_id_type=MESH,
        )

    def slab(g, p):
        return pl.ds(pl.multiple_of(g * ROWS + p * CAP, SUB), CAP)

    def others(g):
        return pl.ds(pl.multiple_of(g * ROWS + CAP, SUB), ROWS - CAP)

    def nth(g, i):
        p = lax.rem((lax.rem(i, PLANE - 1) + 1) * 3, PLANE)
        start = g * ROWS + p * CAP + lax.div(i, PLANE - 1) * SUB
        return p, pl.ds(pl.multiple_of(start, SUB), SUB)

    def dispatch(g, i):
        p, rows = nth(g, i)
        return pltpu.make_async_remote_copy(
            src_ref=packed.at[rows],
            dst_ref=recv.at[rows],
            send_sem=out_send.at[g],
            recv_sem=out_recv.at[g],
            device_id=plane_peer(blk, seq, p, 1),
            device_id_type=MESH,
        )

    def give_back(g, i):
        p, rows = nth(g, i)
        return pltpu.make_async_remote_copy(
            src_ref=sent.at[rows],
            dst_ref=ret.at[rows],
            send_sem=back_send.at[g],
            recv_sem=back_recv.at[g],
            device_id=plane_peer(blk, seq, p, -1),
            device_id_type=MESH,
        )

    def dispatch_all(g):
        return pltpu.make_async_remote_copy(
            src_ref=packed.at[others(g)],
            dst_ref=recv.at[others(g)],
            send_sem=out_send.at[g],
            recv_sem=out_recv.at[g],
            device_id=(mate, blk),
            device_id_type=MESH,
        )

    def give_back_all(g):
        return pltpu.make_async_remote_copy(
            src_ref=sent.at[others(g)],
            dst_ref=ret.at[others(g)],
            send_sem=back_send.at[g],
            recv_sem=back_recv.at[g],
            device_id=(mate, blk),
            device_id_type=MESH,
        )

    def pack(g):
        one_hot = jnp.where(hits(g), 1.0, 0.0).reshape(ROWS, tokens).astype(jnp.bfloat16)
        rows = pl.ds(g * ROWS, ROWS)

        @pl.loop(0, width // 512)
        def _(n):
            cols = pl.ds(pl.multiple_of(n * 512, 512), 512)
            packed[rows, cols] = jnp.dot(
                one_hot,
                blocks[g * tokens : (g + 1) * tokens, cols],
                preferred_element_type=jnp.float32,
            ).astype(jnp.bfloat16)

    copies = (PLANE - 1) * (CAP // SUB)
    pieces = tokens // PIECE
    for g in (OWN, 0, 1, 2):
        if g != OWN:
            ring_all(g).wait_recv()
        pack(g)
        lax.fori_loop(0, copies, lambda i, _: (dispatch(g, i).start(), 0)[1], 0)
        recv[slab(g, 0), :] = packed[slab(g, 0), :]

    order = jnp.where(
        expert == lax.broadcasted_iota(jnp.int32, (PLANE, NPOS), 1), 1.0, 0.0
    ).astype(jnp.bfloat16)
    for g in range(RING):
        logits = lax.dot_general(
            router_ref[...],
            blocks[g * tokens : (g + 1) * tokens, :],
            (((1,), (1,)), ((), ())),
            preferred_element_type=jnp.float32,
        )
        gates[g] = jnp.dot(
            order,
            jax.nn.sigmoid(logits).astype(jnp.bfloat16),
            preferred_element_type=jnp.float32,
        )

    load_gate_up.wait()
    load_down.wait()
    ff = down.shape[0]

    @pl.loop(0, RING)
    def _(g):
        dispatch_all(g).wait_recv()
        rows = pl.ds(pl.multiple_of(g * ROWS, ROWS), ROWS)

        @pl.loop(0, ff // TILE)
        def _(f):
            cols = pl.ds(pl.multiple_of(f * TILE, TILE), TILE)
            up_cols = pl.ds(pl.multiple_of(ff + f * TILE, TILE), TILE)
            gate = jnp.dot(recv[rows, :], gate_up[:, cols], preferred_element_type=jnp.float32)
            up = jnp.dot(recv[rows, :], gate_up[:, up_cols], preferred_element_type=jnp.float32)
            hidden[:, cols] = (jax.nn.silu(gate) * up).astype(jnp.bfloat16)

        @pl.loop(0, width // TILE)
        def _(n):
            cols = pl.ds(pl.multiple_of(n * TILE, TILE), TILE)
            sent[rows, cols] = jnp.dot(
                hidden[...], down[:, cols], preferred_element_type=jnp.float32
            ).astype(jnp.bfloat16)

        lax.fori_loop(0, copies, lambda i, _: (give_back(g, i).start(), 0)[1], 0)
        ret[slab(g, 0), :] = sent[slab(g, 0), :]

    for g in range(RING):
        spread = jnp.where(hits(g), gates[g][:, None, :], 0.0).reshape(ROWS, tokens)
        spread = spread.T.astype(jnp.bfloat16)
        give_back_all(g).wait_recv()

        @pl.loop(0, width // 512)
        def _(n):
            cols = pl.ds(pl.multiple_of(n * 512, 512), 512)
            mixture = jnp.dot(
                spread,
                ret[g * ROWS : (g + 1) * ROWS, cols],
                preferred_element_type=jnp.float32,
            )
            if g == OWN:
                total[:, cols] = resid[:, cols].astype(jnp.float32) + mixture
            else:
                sums_out[g, :, cols] = mixture.astype(jnp.bfloat16)

        if g != OWN:
            lax.fori_loop(0, pieces, lambda i, _: (sum_piece(g, i).start(), 0)[1], 0)

    for g in range(OWN):
        sum_all(g).wait_recv()
    summed = total[...]
    for g in range(OWN):
        summed = summed + sums_in[g].astype(jnp.float32)
    out_ref[...] = summed.astype(jnp.bfloat16)

    def drain(j, _):
        page_arrival(j).wait_recv()
        page_copy(j).wait_send()
        return 0

    lax.fori_loop(1, NPOS, drain, 0)
    for g in range(RING):
        dispatch_all(g).wait_send()
        give_back_all(g).wait_send()
        if g != OWN:
            route_copy(g).wait_send()
            ring_all(g).wait_send()
            sum_all(g).wait_send()
    own_page.wait()
    for r in range(strips):
        near_copy(0, r).wait_send()
        near_copy(1, r).wait_send()
        far_copy(r).wait_send()


def on_device(
    residual_in,
    segment_ids,
    attn_gain,
    w_qkv,
    w_out,
    ffn_gain,
    w_router,
    routes,
    w_gate_up,
    w_down,
    page_owner,
):
    tokens, width = residual_in.shape[1:]
    heads = w_qkv.shape[1]
    length = segment_ids.shape[1]
    page = length // NPOS
    ff = w_down.shape[1]
    slots = NPOS * CAP
    vmem = pl.BlockSpec(memory_space=pltpu.VMEM)
    hbm = pl.BlockSpec(memory_space=pl.ANY)
    dma = pltpu.SemaphoreType.DMA
    bf16 = jnp.bfloat16
    strips = tokens // PIECE
    residual_out, kv_cache = pl.pallas_call(
        layer_kernel,
        out_shape=(
            jax.ShapeDtypeStruct((tokens, width), bf16),
            jax.ShapeDtypeStruct((NPOS, page, heads * 2 * HEAD), bf16),
        ),
        in_specs=[vmem] * 7 + [hbm] * 4,
        out_specs=(vmem, hbm),
        scratch_shapes=[
            pltpu.VMEM((length, heads * HEAD), bf16),
            pltpu.VMEM((length, heads * 2 * HEAD), bf16),
            pltpu.VMEM((NPOS, page, heads * 2 * HEAD), bf16),
            pltpu.VMEM((length, heads * HEAD), bf16),
            pltpu.VMEM((2 * tokens, width), jnp.float32),
            pltpu.VMEM((2, tokens, width), bf16),
            pltpu.VMEM((2, tokens, width), bf16),
            pltpu.VMEM((tokens, width), bf16),
            pltpu.VMEM((tokens, width), bf16),
            pltpu.VMEM((tokens, width), bf16),
            pltpu.VMEM((RING * tokens, width), bf16),
            pltpu.VMEM((RING,) + routes.shape[2:] + (tokens,), jnp.int32),
            pltpu.VMEM((RING - 1, tokens, width), bf16),
            pltpu.VMEM((RING - 1, tokens, width), bf16),
            pltpu.VMEM((RING, PLANE, tokens), jnp.int32),
            pltpu.VMEM((RING, PLANE, tokens), jnp.float32),
            pltpu.VMEM((slots, width), bf16),
            pltpu.VMEM((slots, width), bf16),
            pltpu.VMEM((max(slots, width), width), bf16),
            pltpu.VMEM((slots, width), bf16),
            pltpu.VMEM((ROWS, ff), bf16),
            pltpu.VMEM((width, 2 * ff), bf16),
            pltpu.VMEM((ff, width), bf16),
            pltpu.VMEM((tokens, width), jnp.float32),
            dma((4,)),
            dma,
            dma((RING,)),
            dma((RING,)),
            dma((RING,)),
            dma((RING,)),
            dma((NPOS,)),
            dma((NPOS,)),
            dma((2,)),
            dma((PARTS,)),
            dma((PARTS,)),
            dma((PARTS,)),
            dma((PARTS,)),
            dma((2, strips)),
            dma((2, strips)),
            dma((strips,)),
            dma((strips,)),
            pltpu.VMEM((2, LOAD) + w_qkv.shape[1:], bf16),
            dma((2,)),
            dma((RING,)),
            dma((RING,)),
            dma((RING,)),
            dma((RING,)),
            dma((RING,)),
            dma((RING,)),
        ],
        compiler_params=pltpu.CompilerParams(
            collective_id=0, has_side_effects=True, vmem_limit_bytes=60 << 20
        ),
    )(
        residual_in[0],
        segment_ids,
        page_owner,
        attn_gain,
        ffn_gain,
        w_router.T,
        routes[0].T,
        w_qkv,
        w_out.reshape(heads * HEAD, width),
        w_gate_up[0],
        w_down[0],
    )
    return (residual_out[None], kv_cache[None])


def solution(mesh):
    in_specs = (
        P("blk", "seq", None),
        P("blk", None),
        P(),
        P(None, "seq", None),
        P("seq", None, None),
        P(),
        P(),
        P("blk", "seq", None),
        P("blk", None, None),
        P("blk", None, None),
        P("blk", None),
    )
    out_specs = (P("blk", "seq", None), P("blk", None, None, "seq"))
    return jax.shard_map(
        on_device, mesh=mesh, in_specs=in_specs, out_specs=out_specs, check_vma=False
    )
```

```python
import math

import jax
import jax.numpy as jnp
from jax import lax
from jax.experimental import pallas as pl
from jax.experimental.pallas import tpu as pltpu
from jax.sharding import PartitionSpec as P

EPS = 1e-06
NPOS = 32
CAP = 48
SUB = 16
RING = 4
PLANE = 8
ROWS = PLANE * CAP
PIECE = 32
LOAD = 256
TURN = 64
TILE = 256
HEAD = 128
PARTS = 4
SPAN = 512
MESH = pl.DeviceIdType.MESH
SHIFTS = (1, 3, 2, 0)
OWN = RING - 1


def step_of(position, core):
    k = lax.rem(position * 11, NPOS)
    dx, dz, dy = lax.div(k, 16), lax.rem(lax.div(k, 4), 4), lax.rem(k, 4)
    return dx, dz + core * (dy - dz), dy + core * (dz - dy)


def place_at(blk, position, core, sign):
    dx, dz, dy = step_of(position, core)
    x, z, y = lax.div(blk, 16), lax.rem(lax.div(blk, 4), 4), lax.rem(blk, 4)
    x = lax.rem(x + dx, 2)
    z = lax.rem(z + 4 + sign * dz, 4)
    y = lax.rem(y + 4 + sign * dy, 4)
    return (x * 4 + z) * 4 + y


def locate(blk, core):
    x, z, y = lax.div(blk, 16), lax.rem(lax.div(blk, 4), 4), lax.rem(blk, 4)
    return x, z + core * (y - z), y + core * (z - y)


def index_of(x, u, v, core):
    z, y = u + core * (v - u), v + core * (u - v)
    return (x * 4 + z) * 4 + y


def along_ring(blk, core, shift):
    x, u, v = locate(blk, core)
    return index_of(x, lax.rem(u + 4 + shift, 4), v, core)


def in_plane(blk, core, position, sign):
    x, u, v = locate(blk, core)
    dx, dv = lax.div(position, 4), lax.rem(position, 4)
    return index_of(lax.rem(x + dx, 2), u, lax.rem(v + 4 + sign * dv, 4), core)


def plane_peer(blk, seq, position, sign):
    core = lax.rem(seq, 2)
    dx, dv = lax.div(position, 4), lax.rem(position, 4)
    other = 2 * dx * (1 - lax.rem(dv, 2))
    return lax.rem(seq + other, 4), in_plane(blk, core, position, sign)


def layer_kernel(
    rows_ref,
    segment_ref,
    owner_ref,
    attn_gain_ref,
    ffn_gain_ref,
    router_ref,
    routes_ref,
    qkv_hbm,
    out_hbm,
    gate_up_hbm,
    down_hbm,
    out_ref,
    kv_ref,
    queries,
    keys_values,
    pages_ref,
    context,
    partial,
    near_send,
    near_recv,
    far_send,
    far_recv,
    resid,
    blocks,
    routed,
    sums_out,
    sums_in,
    rank,
    gates,
    packed,
    recv,
    sent,
    ret,
    hidden,
    gate_up,
    down,
    total,
    weight_sems,
    kv_local_sem,
    out_send,
    out_recv,
    back_send,
    back_recv,
    kv_send,
    kv_recv,
    own_sems,
    gather_send,
    gather_recv,
    pass_send,
    pass_recv,
    near_send_sems,
    near_recv_sems,
    far_send_sems,
    far_recv_sems,
    staged,
    stage_sems,
    route_send,
    route_recv,
    ring_send,
    ring_recv,
    sum_send,
    sum_recv,
):
    blk = lax.axis_index("blk")
    seq = lax.axis_index("seq")
    half = lax.div(seq, 2)
    core = lax.rem(seq, 2)
    mate = seq + 1 - 2 * core
    far = lax.rem(seq + 2, 4)
    tok = rows_ref.shape[0]
    width = rows_ref.shape[1]
    length = 4 * tok
    heads = out_hbm.shape[0] // HEAD
    columns = qkv_hbm.shape[2]
    w_qkv = sent.at[0:width, 0 : heads * columns]
    w_out = packed.at[0 : out_hbm.shape[0]]
    everyone = packed.at[out_hbm.shape[0] : out_hbm.shape[0] + length]

    def load_qkv(i):
        rows = pl.ds(pl.multiple_of(i * LOAD, LOAD), LOAD)
        return pltpu.make_async_copy(
            qkv_hbm.at[rows], staged.at[lax.rem(i, 2)], stage_sems.at[lax.rem(i, 2)]
        )

    load_out = pltpu.make_async_copy(out_hbm, w_out, weight_sems.at[3])
    load_gate_up = pltpu.make_async_copy(gate_up_hbm, gate_up, weight_sems.at[0])
    load_down = pltpu.make_async_copy(down_hbm, down, weight_sems.at[1])
    load_qkv(0).start()
    load_qkv(1).start()
    load_out.start()

    barrier = pltpu.get_barrier_semaphore()

    def greet(j, _):
        pl.semaphore_signal(
            barrier,
            inc=1,
            device_id=(seq, place_at(blk, j, core, 1)),
            device_id_type=MESH,
        )
        return 0

    lax.fori_loop(1, NPOS, greet, 0)
    for crossing in (4, 6):
        pl.semaphore_signal(
            barrier,
            inc=1,
            device_id=plane_peer(blk, seq, crossing, 1),
            device_id_type=MESH,
        )
    for other in (mate, far):
        pl.semaphore_signal(barrier, inc=1, device_id=(other, blk), device_id_type=MESH)

    def block(index):
        return pl.ds(pl.multiple_of(index * tok, tok), tok)

    def norm(wide, gain_ref):
        scale = lax.rsqrt(jnp.mean(wide * wide, axis=-1, keepdims=True) + EPS)
        return (wide * scale * gain_ref[...].astype(jnp.float32).reshape(1, width)).astype(jnp.bfloat16)

    def send(src, dst, send_sem, recv_sem, to):
        return pltpu.make_async_remote_copy(
            src_ref=src,
            dst_ref=dst,
            send_sem=send_sem,
            recv_sem=recv_sem,
            device_id=(to, blk),
            device_id_type=MESH,
        )

    def piece(index, i):
        rows = tok // PARTS
        return everyone.at[pl.ds(pl.multiple_of(index * tok + i * rows, rows), rows)]

    everyone[block(seq), :] = norm(rows_ref[...].astype(jnp.float32), attn_gain_ref)
    pl.semaphore_wait(barrier, NPOS - 1 + 2 + 2)

    def route_copy(g):
        return pltpu.make_async_remote_copy(
            src_ref=routes_ref,
            dst_ref=routed.at[g],
            send_sem=route_send.at[g],
            recv_sem=route_recv.at[g],
            device_id=(seq, along_ring(blk, core, SHIFTS[g])),
            device_id_type=MESH,
        )


    own_out = send(
        everyone.at[block(seq)], everyone.at[block(seq)], own_sems.at[0], own_sems.at[1], mate
    )
    own_in = send(
        everyone.at[block(mate)], everyone.at[block(mate)], own_sems.at[0], own_sems.at[1], mate
    )
    gather_out = [
        send(piece(seq, i), piece(seq, i), gather_send.at[i], gather_recv.at[i], far)
        for i in range(PARTS)
    ]
    gather_in = [
        send(piece(far, i), piece(far, i), gather_send.at[i], gather_recv.at[i], far)
        for i in range(PARTS)
    ]
    far_mate = lax.rem(mate + 2, 4)
    pass_out = [
        send(piece(far, i), piece(far, i), pass_send.at[i], pass_recv.at[i], mate)
        for i in range(PARTS)
    ]
    pass_in = [
        send(piece(far_mate, i), piece(far_mate, i), pass_send.at[i], pass_recv.at[i], mate)
        for i in range(PARTS)
    ]
    for copy in gather_out:
        copy.start()
    own_out.start()
    for g in range(OWN):
        route_copy(g).start()

    def two_blocks(index):
        return pl.ds(pl.multiple_of(index * 2 * tok, 2 * tok), 2 * tok)

    def project(index):
        rows = two_blocks(index)

        @pl.loop(0, heads // 2)
        def _(p):
            cols = pl.ds(pl.multiple_of(p * 6 * HEAD, 6 * HEAD), 6 * HEAD)
            both = jnp.dot(
                everyone[rows, :], w_qkv[:, cols], preferred_element_type=jnp.float32
            ).astype(jnp.bfloat16)
            q_cols = pl.ds(pl.multiple_of(p * 2 * HEAD, 2 * HEAD), 2 * HEAD)
            kv_cols = pl.ds(pl.multiple_of(p * 4 * HEAD, 4 * HEAD), 4 * HEAD)
            queries[rows, q_cols] = jnp.concatenate(
                [both[:, 0:HEAD], both[:, 3 * HEAD : 4 * HEAD]], axis=1
            )
            keys_values[rows, kv_cols] = jnp.concatenate(
                [both[:, HEAD : 3 * HEAD], both[:, 4 * HEAD :]], axis=1
            )

    tokens = tok
    expert = in_plane(blk, core, lax.broadcasted_iota(jnp.int32, (PLANE, 1), 0), 1)
    slot = lax.broadcasted_iota(jnp.int32, (PLANE, CAP, tokens), 1)

    own_rows = slice(OWN * tokens, RING * tokens)

    def rank_tokens():
        upto = lax.broadcasted_iota(jnp.int32, (tokens, tokens), 0) <= lax.broadcasted_iota(
            jnp.int32, (tokens, tokens), 1
        )
        for g in range(RING):
            if g != OWN:
                route_copy(g).wait_recv()
            chosen = jnp.zeros((PLANE, tokens), jnp.int32)
            for k in range(routes_ref.shape[0]):
                named = routes_ref[k : k + 1, :] if g == OWN else routed[g, k : k + 1, :]
                chosen = jnp.where(named == expert, 1, chosen)
            count = jnp.dot(
                chosen.astype(jnp.bfloat16),
                jnp.where(upto, 1.0, 0.0).astype(jnp.bfloat16),
                preferred_element_type=jnp.float32,
            ).astype(jnp.int32)
            rank[g] = jnp.where(chosen == 1, count - 1, -1)

    def hits(g):
        return rank[g][:, None, :] == slot

    segment_row = segment_ref[...]
    segment_column = jnp.broadcast_to(segment_row, (HEAD, length)).T

    loads = width // LOAD

    @pl.loop(0, loads)
    def _(i):
        load_qkv(i).wait()

        @pl.loop(0, LOAD // TURN)
        def _(t):
            some = staged[lax.rem(i, 2), pl.ds(pl.multiple_of(t * TURN, TURN), TURN)]
            rows = pl.ds(pl.multiple_of(i * LOAD + t * TURN, TURN), TURN)
            for head in range(heads):
                w_qkv[rows, head * columns : (head + 1) * columns] = some[:, head, :]

        @pl.when(i < loads - 2)
        def _():
            load_qkv(i + 2).start()

    load_out.wait()
    load_gate_up.start()
    load_down.start()
    own_in.wait_recv()
    for i in range(PARTS // 2):
        gather_in[i].wait_recv()
        pass_out[i].start()
    project(half)
    rank_tokens()
    for i in range(PARTS // 2, PARTS):
        gather_in[i].wait_recv()
        pass_out[i].start()
    for i in range(PARTS):
        pass_in[i].wait_recv()
    project(1 - half)

    def page_copy(j):
        to_blk = place_at(blk, j, core, 1)
        return pltpu.make_async_remote_copy(
            src_ref=pages_ref.at[to_blk],
            dst_ref=kv_ref.at[blk],
            send_sem=kv_send.at[j],
            recv_sem=kv_recv.at[j],
            device_id=(seq, to_blk),
            device_id_type=MESH,
        )

    def page_arrival(j):
        from_blk = place_at(blk, j, core, -1)
        return pltpu.make_async_remote_copy(
            src_ref=pages_ref.at[from_blk],
            dst_ref=kv_ref.at[from_blk],
            send_sem=kv_send.at[j],
            recv_sem=kv_recv.at[j],
            device_id=(seq, from_blk),
            device_id_type=MESH,
        )

    def attend(index):
        rows = two_blocks(index)
        picked = jnp.where(index == 0, segment_column[0 : 2 * tok], segment_column[2 * tok :])
        same = picked[:, 0:1] == segment_row

        @pl.loop(0, heads)
        def _(head):
            cols = pl.ds(pl.multiple_of(head * HEAD, HEAD), HEAD)
            k_cols = pl.ds(pl.multiple_of(head * 2 * HEAD, HEAD), HEAD)
            v_cols = pl.ds(pl.multiple_of(head * 2 * HEAD + HEAD, HEAD), HEAD)
            scores = lax.dot_general(
                queries[rows, cols],
                keys_values[:, k_cols],
                (((1,), (1,)), ((), ())),
                preferred_element_type=jnp.float32,
            ) * (1.0 / math.sqrt(HEAD))
            scores = jnp.where(same, scores, -1e30)
            weights = jnp.exp(scores - jnp.max(scores, axis=-1, keepdims=True))
            probs = (weights / jnp.sum(weights, axis=-1, keepdims=True)).astype(jnp.bfloat16)
            context[rows, cols] = jnp.dot(
                probs, keys_values[:, v_cols], preferred_element_type=jnp.float32
            ).astype(jnp.bfloat16)

    def column(n):
        return pl.ds(n * SPAN, SPAN)

    def strip(r):
        return pl.ds(r * PIECE, PIECE)

    def near_copy(which, r):
        return send(
            near_send.at[which, strip(r)],
            near_recv.at[which, strip(r)],
            near_send_sems.at[which, r],
            near_recv_sems.at[which, r],
            mate,
        )

    def far_copy(r):
        return send(
            far_send.at[strip(r)],
            far_recv.at[strip(r)],
            far_send_sems.at[r],
            far_recv_sems.at[r],
            far,
        )

    strips = tok // PIECE

    def mix(which, index):
        for n in range(width // SPAN):
            partial[:, column(n)] = jnp.dot(
                context[two_blocks(index), :],
                w_out[:, column(n)],
                preferred_element_type=jnp.float32,
            )
            near_send[which, :, column(n)] = partial[block(1 - core), column(n)].astype(
                jnp.bfloat16
            )
        for r in range(strips):
            near_copy(which, r).start()

    def reduced(which, r):
        near_copy(which, r).wait_recv()
        own = partial[pl.ds(pl.multiple_of(core * tok + r * PIECE, PIECE), PIECE), :]
        return own + near_recv[which, strip(r), :].astype(jnp.float32)

    def ring_piece(g, i):
        rows = pl.ds(pl.multiple_of(OWN * tokens + i * PIECE, PIECE), PIECE)
        to_rows = pl.ds(pl.multiple_of(g * tokens + i * PIECE, PIECE), PIECE)
        return pltpu.make_async_remote_copy(
            src_ref=blocks.at[rows],
            dst_ref=blocks.at[to_rows],
            send_sem=ring_send.at[g],
            recv_sem=ring_recv.at[g],
            device_id=(seq, along_ring(blk, core, SHIFTS[g])),
            device_id_type=MESH,
        )

    page = length // NPOS
    spread_owner = lax.div(
        lax.broadcasted_iota(jnp.int32, (NPOS, length), 1), page
    ) == lax.broadcasted_iota(jnp.int32, (NPOS, length), 0)
    owners = jnp.dot(
        jnp.broadcast_to(owner_ref[...], (8, NPOS)).astype(jnp.bfloat16),
        jnp.where(spread_owner, 1.0, 0.0).astype(jnp.bfloat16),
        preferred_element_type=jnp.float32,
    ).astype(jnp.int32)[0:1]
    to_row = lax.broadcasted_iota(jnp.int32, (length, length), 0)
    from_row = lax.broadcasted_iota(jnp.int32, (length, length), 1)
    moves = (lax.rem(to_row, page) == lax.rem(from_row, page)) & (
        lax.div(to_row, page) == owners
    )
    pages_ref[...] = (
        jnp.dot(
            jnp.where(moves, 1.0, 0.0).astype(jnp.bfloat16),
            keys_values[...],
            preferred_element_type=jnp.float32,
        )
        .astype(jnp.bfloat16)
        .reshape(pages_ref.shape)
    )
    own_page = pltpu.make_async_copy(pages_ref.at[blk], kv_ref.at[blk], kv_local_sem)
    own_page.start()
    lax.fori_loop(1, NPOS, lambda j, _: (page_copy(j).start(), 0)[1], 0)

    attend(1 - half)
    mix(0, 1 - half)
    for r in range(strips):
        far_send[strip(r), :] = reduced(0, r).astype(jnp.bfloat16)
        far_copy(r).start()
    attend(half)
    mix(1, half)
    for r in range(strips):
        mixed = reduced(1, r)
        far_copy(r).wait_recv()
        mixed = mixed + far_recv[strip(r), :].astype(jnp.float32)
        summed = (rows_ref[strip(r), :].astype(jnp.float32) + mixed).astype(jnp.bfloat16)
        resid[strip(r), :] = summed
        blocks[pl.ds(OWN * tokens + r * PIECE, PIECE), :] = norm(
            summed.astype(jnp.float32), ffn_gain_ref
        )
        for g in range(OWN):
            ring_piece(g, r).start()
    own_out.wait_send()
    for i in range(PARTS):
        gather_out[i].wait_send()
        pass_out[i].wait_send()

    def ring_all(g):
        return pltpu.make_async_remote_copy(
            src_ref=blocks.at[own_rows],
            dst_ref=blocks.at[pl.ds(g * tokens, tokens)],
            send_sem=ring_send.at[g],
            recv_sem=ring_recv.at[g],
            device_id=(mate, blk),
            device_id_type=MESH,
        )

    def sum_piece(g, i):
        rows = pl.ds(pl.multiple_of(i * PIECE, PIECE), PIECE)
        return pltpu.make_async_remote_copy(
            src_ref=sums_out.at[g, rows],
            dst_ref=sums_in.at[g, rows],
            send_sem=sum_send.at[g],
            recv_sem=sum_recv.at[g],
            device_id=(seq, along_ring(blk, core, -SHIFTS[g])),
            device_id_type=MESH,
        )

    def sum_all(g):
        return pltpu.make_async_remote_copy(
            src_ref=sums_out.at[g],
            dst_ref=sums_in.at[g],
            send_sem=sum_send.at[g],
            recv_sem=sum_recv.at[g],
            device_id=(mate, blk),
            device_id_type=MESH,
        )

    def slab(g, p):
        return pl.ds(pl.multiple_of(g * ROWS + p * CAP, SUB), CAP)

    def others(g):
        return pl.ds(pl.multiple_of(g * ROWS + CAP, SUB), ROWS - CAP)

    def nth(g, i):
        p = lax.rem((lax.rem(i, PLANE - 1) + 1) * 3, PLANE)
        start = g * ROWS + p * CAP + lax.div(i, PLANE - 1) * SUB
        return p, pl.ds(pl.multiple_of(start, SUB), SUB)

    def dispatch(g, i):
        p, rows = nth(g, i)
        return pltpu.make_async_remote_copy(
            src_ref=packed.at[rows],
            dst_ref=recv.at[rows],
            send_sem=out_send.at[g],
            recv_sem=out_recv.at[g],
            device_id=plane_peer(blk, seq, p, 1),
            device_id_type=MESH,
        )

    def give_back(g, i):
        p, rows = nth(g, i)
        return pltpu.make_async_remote_copy(
            src_ref=sent.at[rows],
            dst_ref=ret.at[rows],
            send_sem=back_send.at[g],
            recv_sem=back_recv.at[g],
            device_id=plane_peer(blk, seq, p, -1),
            device_id_type=MESH,
        )

    def dispatch_all(g):
        return pltpu.make_async_remote_copy(
            src_ref=packed.at[others(g)],
            dst_ref=recv.at[others(g)],
            send_sem=out_send.at[g],
            recv_sem=out_recv.at[g],
            device_id=(mate, blk),
            device_id_type=MESH,
        )

    def give_back_all(g):
        return pltpu.make_async_remote_copy(
            src_ref=sent.at[others(g)],
            dst_ref=ret.at[others(g)],
            send_sem=back_send.at[g],
            recv_sem=back_recv.at[g],
            device_id=(mate, blk),
            device_id_type=MESH,
        )

    def pack(g):
        one_hot = jnp.where(hits(g), 1.0, 0.0).reshape(ROWS, tokens).astype(jnp.bfloat16)
        rows = pl.ds(g * ROWS, ROWS)

        @pl.loop(0, width // 512)
        def _(n):
            cols = pl.ds(pl.multiple_of(n * 512, 512), 512)
            packed[rows, cols] = jnp.dot(
                one_hot,
                blocks[g * tokens : (g + 1) * tokens, cols],
                preferred_element_type=jnp.float32,
            ).astype(jnp.bfloat16)

    copies = (PLANE - 1) * (CAP // SUB)
    pieces = tokens // PIECE
    for g in (OWN, 0, 1, 2):
        if g != OWN:
            ring_all(g).wait_recv()
        pack(g)
        lax.fori_loop(0, copies, lambda i, _: (dispatch(g, i).start(), 0)[1], 0)
        recv[slab(g, 0), :] = packed[slab(g, 0), :]

    order = jnp.where(
        expert == lax.broadcasted_iota(jnp.int32, (PLANE, NPOS), 1), 1.0, 0.0
    ).astype(jnp.bfloat16)
    for g in range(RING):
        logits = lax.dot_general(
            router_ref[...],
            blocks[g * tokens : (g + 1) * tokens, :],
            (((1,), (1,)), ((), ())),
            preferred_element_type=jnp.float32,
        )
        gates[g] = jnp.dot(
            order,
            jax.nn.sigmoid(logits).astype(jnp.bfloat16),
            preferred_element_type=jnp.float32,
        )

    load_gate_up.wait()
    load_down.wait()
    ff = down.shape[0]

    @pl.loop(0, RING)
    def _(g):
        dispatch_all(g).wait_recv()
        rows = pl.ds(pl.multiple_of(g * ROWS, ROWS), ROWS)

        @pl.loop(0, ff // TILE)
        def _(f):
            cols = pl.ds(pl.multiple_of(f * TILE, TILE), TILE)
            up_cols = pl.ds(pl.multiple_of(ff + f * TILE, TILE), TILE)
            gate = jnp.dot(recv[rows, :], gate_up[:, cols], preferred_element_type=jnp.float32)
            up = jnp.dot(recv[rows, :], gate_up[:, up_cols], preferred_element_type=jnp.float32)
            hidden[:, cols] = (jax.nn.silu(gate) * up).astype(jnp.bfloat16)

        @pl.loop(0, width // TILE)
        def _(n):
            cols = pl.ds(pl.multiple_of(n * TILE, TILE), TILE)
            sent[rows, cols] = jnp.dot(
                hidden[...], down[:, cols], preferred_element_type=jnp.float32
            ).astype(jnp.bfloat16)

        lax.fori_loop(0, copies, lambda i, _: (give_back(g, i).start(), 0)[1], 0)
        ret[slab(g, 0), :] = sent[slab(g, 0), :]

    for g in range(RING):
        spread = jnp.where(hits(g), gates[g][:, None, :], 0.0).reshape(ROWS, tokens)
        spread = spread.T.astype(jnp.bfloat16)
        give_back_all(g).wait_recv()

        @pl.loop(0, width // 512)
        def _(n):
            cols = pl.ds(pl.multiple_of(n * 512, 512), 512)
            mixture = jnp.dot(
                spread,
                ret[g * ROWS : (g + 1) * ROWS, cols],
                preferred_element_type=jnp.float32,
            )
            if g == OWN:
                total[:, cols] = resid[:, cols].astype(jnp.float32) + mixture
            else:
                sums_out[g, :, cols] = mixture.astype(jnp.bfloat16)

        if g != OWN:
            lax.fori_loop(0, pieces, lambda i, _: (sum_piece(g, i).start(), 0)[1], 0)

    for g in range(OWN):
        sum_all(g).wait_recv()
    summed = total[...]
    for g in range(OWN):
        summed = summed + sums_in[g].astype(jnp.float32)
    out_ref[...] = summed.astype(jnp.bfloat16)

    def drain(j, _):
        page_arrival(j).wait_recv()
        page_copy(j).wait_send()
        return 0

    lax.fori_loop(1, NPOS, drain, 0)
    for g in range(RING):
        dispatch_all(g).wait_send()
        give_back_all(g).wait_send()
        if g != OWN:
            route_copy(g).wait_send()
            ring_all(g).wait_send()
            sum_all(g).wait_send()
    own_page.wait()
    for r in range(strips):
        near_copy(0, r).wait_send()
        near_copy(1, r).wait_send()
        far_copy(r).wait_send()


def hand_over_kernel(rows_ref, pages_ref, out_ref, kv_ref, rows, pages, in_sems, out_sems):
    moves = []
    for which, (src, stage, dst) in enumerate(
        [(rows_ref, rows, out_ref), (pages_ref, pages, kv_ref)]
    ):
        for i in range(4):
            size = src.shape[0] // 4
            part = slice(i * size, (i + 1) * size)
            moves.append(
                (
                    pltpu.make_async_copy(src.at[part], stage.at[part], in_sems.at[which, i]),
                    pltpu.make_async_copy(stage.at[part], dst.at[part], out_sems.at[which, i]),
                )
            )
    for fetch, _ in moves:
        fetch.start()
    for fetch, put in moves:
        fetch.wait()
        put.start()
    for _, put in moves:
        put.wait()


def on_device(
    residual_in,
    segment_ids,
    attn_gain,
    w_qkv,
    w_out,
    ffn_gain,
    w_router,
    routes,
    w_gate_up,
    w_down,
    page_owner,
):
    tokens, width = residual_in.shape[1:]
    heads = w_qkv.shape[1]
    length = segment_ids.shape[1]
    page = length // NPOS
    ff = w_down.shape[1]
    slots = NPOS * CAP
    vmem = pl.BlockSpec(memory_space=pltpu.VMEM)
    hbm = pl.BlockSpec(memory_space=pl.ANY)
    dma = pltpu.SemaphoreType.DMA
    bf16 = jnp.bfloat16
    strips = tokens // PIECE
    residual_out, kv_cache = pl.pallas_call(
        layer_kernel,
        out_shape=(
            jax.ShapeDtypeStruct((tokens, width), bf16),
            jax.ShapeDtypeStruct((NPOS, page, heads * 2 * HEAD), bf16),
        ),
        in_specs=[vmem] * 7 + [hbm] * 4,
        out_specs=(vmem, hbm),
        scratch_shapes=[
            pltpu.VMEM((length, heads * HEAD), bf16),
            pltpu.VMEM((length, heads * 2 * HEAD), bf16),
            pltpu.VMEM((NPOS, page, heads * 2 * HEAD), bf16),
            pltpu.VMEM((length, heads * HEAD), bf16),
            pltpu.VMEM((2 * tokens, width), jnp.float32),
            pltpu.VMEM((2, tokens, width), bf16),
            pltpu.VMEM((2, tokens, width), bf16),
            pltpu.VMEM((tokens, width), bf16),
            pltpu.VMEM((tokens, width), bf16),
            pltpu.VMEM((tokens, width), bf16),
            pltpu.VMEM((RING * tokens, width), bf16),
            pltpu.VMEM((RING,) + routes.shape[2:] + (tokens,), jnp.int32),
            pltpu.VMEM((RING - 1, tokens, width), bf16),
            pltpu.VMEM((RING - 1, tokens, width), bf16),
            pltpu.VMEM((RING, PLANE, tokens), jnp.int32),
            pltpu.VMEM((RING, PLANE, tokens), jnp.float32),
            pltpu.VMEM((slots, width), bf16),
            pltpu.VMEM((slots, width), bf16),
            pltpu.VMEM((max(slots, width), width), bf16),
            pltpu.VMEM((slots, width), bf16),
            pltpu.VMEM((ROWS, ff), bf16),
            pltpu.VMEM((width, 2 * ff), bf16),
            pltpu.VMEM((ff, width), bf16),
            pltpu.VMEM((tokens, width), jnp.float32),
            dma((4,)),
            dma,
            dma((RING,)),
            dma((RING,)),
            dma((RING,)),
            dma((RING,)),
            dma((NPOS,)),
            dma((NPOS,)),
            dma((2,)),
            dma((PARTS,)),
            dma((PARTS,)),
            dma((PARTS,)),
            dma((PARTS,)),
            dma((2, strips)),
            dma((2, strips)),
            dma((strips,)),
            dma((strips,)),
            pltpu.VMEM((2, LOAD) + w_qkv.shape[1:], bf16),
            dma((2,)),
            dma((RING,)),
            dma((RING,)),
            dma((RING,)),
            dma((RING,)),
            dma((RING,)),
            dma((RING,)),
        ],
        compiler_params=pltpu.CompilerParams(
            collective_id=0, has_side_effects=True, vmem_limit_bytes=60 << 20
        ),
    )(
        residual_in[0],
        segment_ids,
        page_owner,
        attn_gain,
        ffn_gain,
        w_router.T,
        routes[0].T,
        w_qkv,
        w_out.reshape(heads * HEAD, width),
        w_gate_up[0],
        w_down[0],
    )
    residual_out, kv_cache = pl.pallas_call(
        hand_over_kernel,
        out_shape=(
            jax.ShapeDtypeStruct(residual_out.shape, bf16),
            jax.ShapeDtypeStruct(kv_cache.shape, bf16),
        ),
        in_specs=[hbm] * 2,
        out_specs=(hbm, hbm),
        scratch_shapes=[
            pltpu.VMEM(residual_out.shape, bf16),
            pltpu.VMEM(kv_cache.shape, bf16),
            dma((2, 4)),
            dma((2, 4)),
        ],
    )(residual_out, kv_cache)
    return (residual_out[None], kv_cache[None])


def solution(mesh):
    in_specs = (
        P("blk", "seq", None),
        P("blk", None),
        P(),
        P(None, "seq", None),
        P("seq", None, None),
        P(),
        P(),
        P("blk", "seq", None),
        P("blk", None, None),
        P("blk", None, None),
        P("blk", None),
    )
    out_specs = (P("blk", "seq", None), P("blk", None, None, "seq"))
    return jax.shard_map(
        on_device, mesh=mesh, in_specs=in_specs, out_specs=out_specs, check_vma=False
    )
```

```python
import math

import jax
import jax.numpy as jnp
from jax import lax
from jax.experimental import pallas as pl
from jax.experimental.pallas import tpu as pltpu
from jax.sharding import PartitionSpec as P

EPS = 1e-06
NPOS = 32
CAP = 48
SUB = 16
RING = 4
PLANE = 8
ROWS = PLANE * CAP
PIECE = 32
LOAD = 256
TURN = 64
TILE = 256
HEAD = 128
PARTS = 4
SPAN = 512
MESH = pl.DeviceIdType.MESH
SHIFTS = (2, 1, 3, 0)
OWN = RING - 1


def step_of(position, core):
    k = lax.rem(position * 11, NPOS)
    dx, dz, dy = lax.div(k, 16), lax.rem(lax.div(k, 4), 4), lax.rem(k, 4)
    return dx, dz + core * (dy - dz), dy + core * (dz - dy)


def place_at(blk, position, core, sign):
    dx, dz, dy = step_of(position, core)
    x, z, y = lax.div(blk, 16), lax.rem(lax.div(blk, 4), 4), lax.rem(blk, 4)
    x = lax.rem(x + dx, 2)
    z = lax.rem(z + 4 + sign * dz, 4)
    y = lax.rem(y + 4 + sign * dy, 4)
    return (x * 4 + z) * 4 + y


def locate(blk, core):
    x, z, y = lax.div(blk, 16), lax.rem(lax.div(blk, 4), 4), lax.rem(blk, 4)
    return x, z + core * (y - z), y + core * (z - y)


def index_of(x, u, v, core):
    z, y = u + core * (v - u), v + core * (u - v)
    return (x * 4 + z) * 4 + y


def along_ring(blk, core, shift):
    x, u, v = locate(blk, core)
    return index_of(x, lax.rem(u + 4 + shift, 4), v, core)


def in_plane(blk, core, position, sign):
    x, u, v = locate(blk, core)
    dx, dv = lax.div(position, 4), lax.rem(position, 4)
    return index_of(lax.rem(x + dx, 2), u, lax.rem(v + 4 + sign * dv, 4), core)


def plane_peer(blk, seq, position, sign):
    core = lax.rem(seq, 2)
    dx, dv = lax.div(position, 4), lax.rem(position, 4)
    other = 2 * dx * (1 - lax.rem(dv, 2))
    return lax.rem(seq + other, 4), in_plane(blk, core, position, sign)


def layer_kernel(
    rows_ref,
    segment_ref,
    owner_ref,
    attn_gain_ref,
    ffn_gain_ref,
    router_ref,
    routes_ref,
    qkv_hbm,
    out_hbm,
    gate_up_hbm,
    down_hbm,
    out_ref,
    kv_ref,
    queries,
    keys_values,
    pages_ref,
    context,
    partial,
    near_send,
    near_recv,
    far_send,
    far_recv,
    resid,
    blocks,
    routed,
    sums_out,
    sums_in,
    rank,
    gates,
    packed,
    recv,
    sent,
    ret,
    hidden,
    gate_up,
    down,
    total,
    weight_sems,
    kv_local_sem,
    out_send,
    out_recv,
    back_send,
    back_recv,
    kv_send,
    kv_recv,
    own_sems,
    gather_send,
    gather_recv,
    pass_send,
    pass_recv,
    near_send_sems,
    near_recv_sems,
    far_send_sems,
    far_recv_sems,
    staged,
    stage_sems,
    route_send,
    route_recv,
    ring_send,
    ring_recv,
    sum_send,
    sum_recv,
):
    blk = lax.axis_index("blk")
    seq = lax.axis_index("seq")
    half = lax.div(seq, 2)
    core = lax.rem(seq, 2)
    mate = seq + 1 - 2 * core
    far = lax.rem(seq + 2, 4)
    tok = rows_ref.shape[0]
    width = rows_ref.shape[1]
    length = 4 * tok
    heads = out_hbm.shape[0] // HEAD
    columns = qkv_hbm.shape[2]
    w_qkv = sent.at[0:width, 0 : heads * columns]
    w_out = packed.at[0 : out_hbm.shape[0]]
    everyone = packed.at[out_hbm.shape[0] : out_hbm.shape[0] + length]

    def load_qkv(i):
        rows = pl.ds(pl.multiple_of(i * LOAD, LOAD), LOAD)
        return pltpu.make_async_copy(
            qkv_hbm.at[rows], staged.at[lax.rem(i, 2)], stage_sems.at[lax.rem(i, 2)]
        )

    load_out = pltpu.make_async_copy(out_hbm, w_out, weight_sems.at[3])
    load_gate_up = pltpu.make_async_copy(gate_up_hbm, gate_up, weight_sems.at[0])
    load_down = pltpu.make_async_copy(down_hbm, down, weight_sems.at[1])
    load_qkv(0).start()
    load_qkv(1).start()
    load_out.start()

    barrier = pltpu.get_barrier_semaphore()

    def greet(j, _):
        pl.semaphore_signal(
            barrier,
            inc=1,
            device_id=(seq, place_at(blk, j, core, 1)),
            device_id_type=MESH,
        )
        return 0

    lax.fori_loop(1, NPOS, greet, 0)
    for crossing in (4, 6):
        pl.semaphore_signal(
            barrier,
            inc=1,
            device_id=plane_peer(blk, seq, crossing, 1),
            device_id_type=MESH,
        )
    for other in (mate, far):
        pl.semaphore_signal(barrier, inc=1, device_id=(other, blk), device_id_type=MESH)

    def block(index):
        return pl.ds(pl.multiple_of(index * tok, tok), tok)

    def norm(wide, gain_ref):
        scale = lax.rsqrt(jnp.mean(wide * wide, axis=-1, keepdims=True) + EPS)
        return (wide * scale * gain_ref[...].astype(jnp.float32).reshape(1, width)).astype(jnp.bfloat16)

    def send(src, dst, send_sem, recv_sem, to):
        return pltpu.make_async_remote_copy(
            src_ref=src,
            dst_ref=dst,
            send_sem=send_sem,
            recv_sem=recv_sem,
            device_id=(to, blk),
            device_id_type=MESH,
        )

    def piece(index, i):
        rows = tok // PARTS
        return everyone.at[pl.ds(pl.multiple_of(index * tok + i * rows, rows), rows)]

    everyone[block(seq), :] = norm(rows_ref[...].astype(jnp.float32), attn_gain_ref)
    pl.semaphore_wait(barrier, NPOS - 1 + 2 + 2)

    def route_copy(g):
        return pltpu.make_async_remote_copy(
            src_ref=routes_ref,
            dst_ref=routed.at[g],
            send_sem=route_send.at[g],
            recv_sem=route_recv.at[g],
            device_id=(seq, along_ring(blk, core, SHIFTS[g])),
            device_id_type=MESH,
        )


    own_out = send(
        everyone.at[block(seq)], everyone.at[block(seq)], own_sems.at[0], own_sems.at[1], mate
    )
    own_in = send(
        everyone.at[block(mate)], everyone.at[block(mate)], own_sems.at[0], own_sems.at[1], mate
    )
    gather_out = [
        send(piece(seq, i), piece(seq, i), gather_send.at[i], gather_recv.at[i], far)
        for i in range(PARTS)
    ]
    gather_in = [
        send(piece(far, i), piece(far, i), gather_send.at[i], gather_recv.at[i], far)
        for i in range(PARTS)
    ]
    far_mate = lax.rem(mate + 2, 4)
    pass_out = [
        send(piece(far, i), piece(far, i), pass_send.at[i], pass_recv.at[i], mate)
        for i in range(PARTS)
    ]
    pass_in = [
        send(piece(far_mate, i), piece(far_mate, i), pass_send.at[i], pass_recv.at[i], mate)
        for i in range(PARTS)
    ]
    for copy in gather_out:
        copy.start()
    own_out.start()
    for g in range(OWN):
        route_copy(g).start()

    def two_blocks(index):
        return pl.ds(pl.multiple_of(index * 2 * tok, 2 * tok), 2 * tok)

    def project(index):
        rows = two_blocks(index)

        @pl.loop(0, heads // 2)
        def _(p):
            cols = pl.ds(pl.multiple_of(p * 6 * HEAD, 6 * HEAD), 6 * HEAD)
            both = jnp.dot(
                everyone[rows, :], w_qkv[:, cols], preferred_element_type=jnp.float32
            ).astype(jnp.bfloat16)
            q_cols = pl.ds(pl.multiple_of(p * 2 * HEAD, 2 * HEAD), 2 * HEAD)
            kv_cols = pl.ds(pl.multiple_of(p * 4 * HEAD, 4 * HEAD), 4 * HEAD)
            queries[rows, q_cols] = jnp.concatenate(
                [both[:, 0:HEAD], both[:, 3 * HEAD : 4 * HEAD]], axis=1
            )
            keys_values[rows, kv_cols] = jnp.concatenate(
                [both[:, HEAD : 3 * HEAD], both[:, 4 * HEAD :]], axis=1
            )

    tokens = tok
    expert = in_plane(blk, core, lax.broadcasted_iota(jnp.int32, (PLANE, 1), 0), 1)
    slot = lax.broadcasted_iota(jnp.int32, (PLANE, CAP, tokens), 1)

    own_rows = slice(OWN * tokens, RING * tokens)

    def rank_tokens():
        upto = lax.broadcasted_iota(jnp.int32, (tokens, tokens), 0) <= lax.broadcasted_iota(
            jnp.int32, (tokens, tokens), 1
        )
        for g in range(RING):
            if g != OWN:
                route_copy(g).wait_recv()
            chosen = jnp.zeros((PLANE, tokens), jnp.int32)
            for k in range(routes_ref.shape[0]):
                named = routes_ref[k : k + 1, :] if g == OWN else routed[g, k : k + 1, :]
                chosen = jnp.where(named == expert, 1, chosen)
            count = jnp.dot(
                chosen.astype(jnp.bfloat16),
                jnp.where(upto, 1.0, 0.0).astype(jnp.bfloat16),
                preferred_element_type=jnp.float32,
            ).astype(jnp.int32)
            rank[g] = jnp.where(chosen == 1, count - 1, -1)

    def hits(g):
        return rank[g][:, None, :] == slot

    segment_row = segment_ref[...]
    segment_column = jnp.broadcast_to(segment_row, (HEAD, length)).T

    loads = width // LOAD

    @pl.loop(0, loads)
    def _(i):
        load_qkv(i).wait()

        @pl.loop(0, LOAD // TURN)
        def _(t):
            some = staged[lax.rem(i, 2), pl.ds(pl.multiple_of(t * TURN, TURN), TURN)]
            rows = pl.ds(pl.multiple_of(i * LOAD + t * TURN, TURN), TURN)
            for head in range(heads):
                w_qkv[rows, head * columns : (head + 1) * columns] = some[:, head, :]

        @pl.when(i < loads - 2)
        def _():
            load_qkv(i + 2).start()

    load_out.wait()
    own_in.wait_recv()
    for i in range(PARTS // 2):
        gather_in[i].wait_recv()
        pass_out[i].start()
    project(half)
    rank_tokens()
    for i in range(PARTS // 2, PARTS):
        gather_in[i].wait_recv()
        pass_out[i].start()
    for i in range(PARTS):
        pass_in[i].wait_recv()
    project(1 - half)

    def page_copy(j):
        to_blk = place_at(blk, j, core, 1)
        return pltpu.make_async_remote_copy(
            src_ref=pages_ref.at[to_blk],
            dst_ref=kv_ref.at[blk],
            send_sem=kv_send.at[j],
            recv_sem=kv_recv.at[j],
            device_id=(seq, to_blk),
            device_id_type=MESH,
        )

    def page_arrival(j):
        from_blk = place_at(blk, j, core, -1)
        return pltpu.make_async_remote_copy(
            src_ref=pages_ref.at[from_blk],
            dst_ref=kv_ref.at[from_blk],
            send_sem=kv_send.at[j],
            recv_sem=kv_recv.at[j],
            device_id=(seq, from_blk),
            device_id_type=MESH,
        )

    def attend(index):
        rows = two_blocks(index)
        picked = jnp.where(index == 0, segment_column[0 : 2 * tok], segment_column[2 * tok :])
        same = picked[:, 0:1] == segment_row

        @pl.loop(0, heads)
        def _(head):
            cols = pl.ds(pl.multiple_of(head * HEAD, HEAD), HEAD)
            k_cols = pl.ds(pl.multiple_of(head * 2 * HEAD, HEAD), HEAD)
            v_cols = pl.ds(pl.multiple_of(head * 2 * HEAD + HEAD, HEAD), HEAD)
            scores = lax.dot_general(
                queries[rows, cols],
                keys_values[:, k_cols],
                (((1,), (1,)), ((), ())),
                preferred_element_type=jnp.float32,
            ) * (1.0 / math.sqrt(HEAD))
            scores = jnp.where(same, scores, -1e30)
            weights = jnp.exp(scores - jnp.max(scores, axis=-1, keepdims=True))
            probs = (weights / jnp.sum(weights, axis=-1, keepdims=True)).astype(jnp.bfloat16)
            context[rows, cols] = jnp.dot(
                probs, keys_values[:, v_cols], preferred_element_type=jnp.float32
            ).astype(jnp.bfloat16)

    def column(n):
        return pl.ds(n * SPAN, SPAN)

    def strip(r):
        return pl.ds(r * PIECE, PIECE)

    def near_copy(which, r):
        return send(
            near_send.at[which, strip(r)],
            near_recv.at[which, strip(r)],
            near_send_sems.at[which, r],
            near_recv_sems.at[which, r],
            mate,
        )

    def far_copy(r):
        return send(
            far_send.at[strip(r)],
            far_recv.at[strip(r)],
            far_send_sems.at[r],
            far_recv_sems.at[r],
            far,
        )

    strips = tok // PIECE

    def mix(which, index):
        for n in range(width // SPAN):
            partial[:, column(n)] = jnp.dot(
                context[two_blocks(index), :],
                w_out[:, column(n)],
                preferred_element_type=jnp.float32,
            )
            near_send[which, :, column(n)] = partial[block(1 - core), column(n)].astype(
                jnp.bfloat16
            )
        for r in range(strips):
            near_copy(which, r).start()

    def reduced(which, r):
        near_copy(which, r).wait_recv()
        own = partial[pl.ds(pl.multiple_of(core * tok + r * PIECE, PIECE), PIECE), :]
        return own + near_recv[which, strip(r), :].astype(jnp.float32)

    def ring_piece(g, i):
        rows = pl.ds(pl.multiple_of(OWN * tokens + i * PIECE, PIECE), PIECE)
        to_rows = pl.ds(pl.multiple_of(g * tokens + i * PIECE, PIECE), PIECE)
        return pltpu.make_async_remote_copy(
            src_ref=blocks.at[rows],
            dst_ref=blocks.at[to_rows],
            send_sem=ring_send.at[g],
            recv_sem=ring_recv.at[g],
            device_id=(seq, along_ring(blk, core, SHIFTS[g])),
            device_id_type=MESH,
        )

    page = length // NPOS
    spread_owner = lax.div(
        lax.broadcasted_iota(jnp.int32, (NPOS, length), 1), page
    ) == lax.broadcasted_iota(jnp.int32, (NPOS, length), 0)
    owners = jnp.dot(
        jnp.broadcast_to(owner_ref[...], (8, NPOS)).astype(jnp.bfloat16),
        jnp.where(spread_owner, 1.0, 0.0).astype(jnp.bfloat16),
        preferred_element_type=jnp.float32,
    ).astype(jnp.int32)[0:1]
    to_row = lax.broadcasted_iota(jnp.int32, (length, length), 0)
    from_row = lax.broadcasted_iota(jnp.int32, (length, length), 1)
    moves = (lax.rem(to_row, page) == lax.rem(from_row, page)) & (
        lax.div(to_row, page) == owners
    )
    pages_ref[...] = (
        jnp.dot(
            jnp.where(moves, 1.0, 0.0).astype(jnp.bfloat16),
            keys_values[...],
            preferred_element_type=jnp.float32,
        )
        .astype(jnp.bfloat16)
        .reshape(pages_ref.shape)
    )
    own_page = pltpu.make_async_copy(pages_ref.at[blk], kv_ref.at[blk], kv_local_sem)
    own_page.start()
    lax.fori_loop(1, NPOS, lambda j, _: (page_copy(j).start(), 0)[1], 0)

    attend(1 - half)
    mix(0, 1 - half)
    for r in range(strips):
        far_send[strip(r), :] = reduced(0, r).astype(jnp.bfloat16)
        far_copy(r).start()
    load_gate_up.start()
    load_down.start()
    attend(half)
    mix(1, half)
    for r in range(strips):
        mixed = reduced(1, r)
        far_copy(r).wait_recv()
        mixed = mixed + far_recv[strip(r), :].astype(jnp.float32)
        summed = (rows_ref[strip(r), :].astype(jnp.float32) + mixed).astype(jnp.bfloat16)
        resid[strip(r), :] = summed
        blocks[pl.ds(OWN * tokens + r * PIECE, PIECE), :] = norm(
            summed.astype(jnp.float32), ffn_gain_ref
        )
        for g in range(OWN):
            ring_piece(g, r).start()
    own_out.wait_send()
    for i in range(PARTS):
        gather_out[i].wait_send()
        pass_out[i].wait_send()

    def ring_all(g):
        return pltpu.make_async_remote_copy(
            src_ref=blocks.at[own_rows],
            dst_ref=blocks.at[pl.ds(g * tokens, tokens)],
            send_sem=ring_send.at[g],
            recv_sem=ring_recv.at[g],
            device_id=(mate, blk),
            device_id_type=MESH,
        )

    def sum_piece(g, i):
        rows = pl.ds(pl.multiple_of(i * PIECE, PIECE), PIECE)
        return pltpu.make_async_remote_copy(
            src_ref=sums_out.at[g, rows],
            dst_ref=sums_in.at[g, rows],
            send_sem=sum_send.at[g],
            recv_sem=sum_recv.at[g],
            device_id=(seq, along_ring(blk, core, -SHIFTS[g])),
            device_id_type=MESH,
        )

    def sum_all(g):
        return pltpu.make_async_remote_copy(
            src_ref=sums_out.at[g],
            dst_ref=sums_in.at[g],
            send_sem=sum_send.at[g],
            recv_sem=sum_recv.at[g],
            device_id=(mate, blk),
            device_id_type=MESH,
        )

    def slab(g, p):
        return pl.ds(pl.multiple_of(g * ROWS + p * CAP, SUB), CAP)

    def others(g):
        return pl.ds(pl.multiple_of(g * ROWS + CAP, SUB), ROWS - CAP)

    def nth(g, i):
        p = lax.rem((lax.rem(i, PLANE - 1) + 1) * 3, PLANE)
        start = g * ROWS + p * CAP + lax.div(i, PLANE - 1) * SUB
        return p, pl.ds(pl.multiple_of(start, SUB), SUB)

    def dispatch(g, i):
        p, rows = nth(g, i)
        return pltpu.make_async_remote_copy(
            src_ref=packed.at[rows],
            dst_ref=recv.at[rows],
            send_sem=out_send.at[g],
            recv_sem=out_recv.at[g],
            device_id=plane_peer(blk, seq, p, 1),
            device_id_type=MESH,
        )

    def give_back(g, i):
        p, rows = nth(g, i)
        return pltpu.make_async_remote_copy(
            src_ref=sent.at[rows],
            dst_ref=ret.at[rows],
            send_sem=back_send.at[g],
            recv_sem=back_recv.at[g],
            device_id=plane_peer(blk, seq, p, -1),
            device_id_type=MESH,
        )

    def dispatch_all(g):
        return pltpu.make_async_remote_copy(
            src_ref=packed.at[others(g)],
            dst_ref=recv.at[others(g)],
            send_sem=out_send.at[g],
            recv_sem=out_recv.at[g],
            device_id=(mate, blk),
            device_id_type=MESH,
        )

    def give_back_all(g):
        return pltpu.make_async_remote_copy(
            src_ref=sent.at[others(g)],
            dst_ref=ret.at[others(g)],
            send_sem=back_send.at[g],
            recv_sem=back_recv.at[g],
            device_id=(mate, blk),
            device_id_type=MESH,
        )

    def pack(g):
        one_hot = jnp.where(hits(g), 1.0, 0.0).reshape(ROWS, tokens).astype(jnp.bfloat16)
        rows = pl.ds(g * ROWS, ROWS)

        @pl.loop(0, width // 512)
        def _(n):
            cols = pl.ds(pl.multiple_of(n * 512, 512), 512)
            packed[rows, cols] = jnp.dot(
                one_hot,
                blocks[g * tokens : (g + 1) * tokens, cols],
                preferred_element_type=jnp.float32,
            ).astype(jnp.bfloat16)

    copies = (PLANE - 1) * (CAP // SUB)
    pieces = tokens // PIECE
    for g in (OWN, 0, 1, 2):
        if g != OWN:
            ring_all(g).wait_recv()
        pack(g)
        lax.fori_loop(0, copies, lambda i, _: (dispatch(g, i).start(), 0)[1], 0)
        recv[slab(g, 0), :] = packed[slab(g, 0), :]

    order = jnp.where(
        expert == lax.broadcasted_iota(jnp.int32, (PLANE, NPOS), 1), 1.0, 0.0
    ).astype(jnp.bfloat16)
    for g in range(RING):
        logits = lax.dot_general(
            router_ref[...],
            blocks[g * tokens : (g + 1) * tokens, :],
            (((1,), (1,)), ((), ())),
            preferred_element_type=jnp.float32,
        )
        gates[g] = jnp.dot(
            order,
            jax.nn.sigmoid(logits).astype(jnp.bfloat16),
            preferred_element_type=jnp.float32,
        )

    load_gate_up.wait()
    load_down.wait()
    ff = down.shape[0]

    @pl.loop(0, RING)
    def _(g):
        dispatch_all(g).wait_recv()
        rows = pl.ds(pl.multiple_of(g * ROWS, ROWS), ROWS)

        @pl.loop(0, ff // TILE)
        def _(f):
            cols = pl.ds(pl.multiple_of(f * TILE, TILE), TILE)
            up_cols = pl.ds(pl.multiple_of(ff + f * TILE, TILE), TILE)
            gate = jnp.dot(recv[rows, :], gate_up[:, cols], preferred_element_type=jnp.float32)
            up = jnp.dot(recv[rows, :], gate_up[:, up_cols], preferred_element_type=jnp.float32)
            hidden[:, cols] = (jax.nn.silu(gate) * up).astype(jnp.bfloat16)

        @pl.loop(0, width // TILE)
        def _(n):
            cols = pl.ds(pl.multiple_of(n * TILE, TILE), TILE)
            sent[rows, cols] = jnp.dot(
                hidden[...], down[:, cols], preferred_element_type=jnp.float32
            ).astype(jnp.bfloat16)

        lax.fori_loop(0, copies, lambda i, _: (give_back(g, i).start(), 0)[1], 0)
        ret[slab(g, 0), :] = sent[slab(g, 0), :]

    for g in range(RING):
        spread = jnp.where(hits(g), gates[g][:, None, :], 0.0).reshape(ROWS, tokens)
        spread = spread.T.astype(jnp.bfloat16)
        give_back_all(g).wait_recv()

        @pl.loop(0, width // 512)
        def _(n):
            cols = pl.ds(pl.multiple_of(n * 512, 512), 512)
            mixture = jnp.dot(
                spread,
                ret[g * ROWS : (g + 1) * ROWS, cols],
                preferred_element_type=jnp.float32,
            )
            if g == OWN:
                total[:, cols] = resid[:, cols].astype(jnp.float32) + mixture
            else:
                sums_out[g, :, cols] = mixture.astype(jnp.bfloat16)

        if g != OWN:
            lax.fori_loop(0, pieces, lambda i, _: (sum_piece(g, i).start(), 0)[1], 0)

    for g in range(OWN):
        sum_all(g).wait_recv()
    summed = total[...]
    for g in range(OWN):
        summed = summed + sums_in[g].astype(jnp.float32)
    out_ref[...] = summed.astype(jnp.bfloat16)

    def drain(j, _):
        page_arrival(j).wait_recv()
        page_copy(j).wait_send()
        return 0

    lax.fori_loop(1, NPOS, drain, 0)
    for g in range(RING):
        dispatch_all(g).wait_send()
        give_back_all(g).wait_send()
        if g != OWN:
            route_copy(g).wait_send()
            ring_all(g).wait_send()
            sum_all(g).wait_send()
    own_page.wait()
    for r in range(strips):
        near_copy(0, r).wait_send()
        near_copy(1, r).wait_send()
        far_copy(r).wait_send()


def hand_over_kernel(rows_ref, pages_ref, out_ref, kv_ref, rows, pages, in_sems, out_sems):
    moves = []
    for which, (src, stage, dst) in enumerate(
        [(rows_ref, rows, out_ref), (pages_ref, pages, kv_ref)]
    ):
        for i in range(4):
            size = src.shape[0] // 4
            part = slice(i * size, (i + 1) * size)
            moves.append(
                (
                    pltpu.make_async_copy(src.at[part], stage.at[part], in_sems.at[which, i]),
                    pltpu.make_async_copy(stage.at[part], dst.at[part], out_sems.at[which, i]),
                )
            )
    for fetch, _ in moves:
        fetch.start()
    for fetch, put in moves:
        fetch.wait()
        put.start()
    for _, put in moves:
        put.wait()


def on_device(
    residual_in,
    segment_ids,
    attn_gain,
    w_qkv,
    w_out,
    ffn_gain,
    w_router,
    routes,
    w_gate_up,
    w_down,
    page_owner,
):
    tokens, width = residual_in.shape[1:]
    heads = w_qkv.shape[1]
    length = segment_ids.shape[1]
    page = length // NPOS
    ff = w_down.shape[1]
    slots = NPOS * CAP
    vmem = pl.BlockSpec(memory_space=pltpu.VMEM)
    hbm = pl.BlockSpec(memory_space=pl.ANY)
    dma = pltpu.SemaphoreType.DMA
    bf16 = jnp.bfloat16
    strips = tokens // PIECE
    residual_out, kv_cache = pl.pallas_call(
        layer_kernel,
        out_shape=(
            jax.ShapeDtypeStruct((tokens, width), bf16),
            jax.ShapeDtypeStruct((NPOS, page, heads * 2 * HEAD), bf16),
        ),
        in_specs=[vmem] * 7 + [hbm] * 4,
        out_specs=(vmem, hbm),
        scratch_shapes=[
            pltpu.VMEM((length, heads * HEAD), bf16),
            pltpu.VMEM((length, heads * 2 * HEAD), bf16),
            pltpu.VMEM((NPOS, page, heads * 2 * HEAD), bf16),
            pltpu.VMEM((length, heads * HEAD), bf16),
            pltpu.VMEM((2 * tokens, width), jnp.float32),
            pltpu.VMEM((2, tokens, width), bf16),
            pltpu.VMEM((2, tokens, width), bf16),
            pltpu.VMEM((tokens, width), bf16),
            pltpu.VMEM((tokens, width), bf16),
            pltpu.VMEM((tokens, width), bf16),
            pltpu.VMEM((RING * tokens, width), bf16),
            pltpu.VMEM((RING,) + routes.shape[2:] + (tokens,), jnp.int32),
            pltpu.VMEM((RING - 1, tokens, width), bf16),
            pltpu.VMEM((RING - 1, tokens, width), bf16),
            pltpu.VMEM((RING, PLANE, tokens), jnp.int32),
            pltpu.VMEM((RING, PLANE, tokens), jnp.float32),
            pltpu.VMEM((slots, width), bf16),
            pltpu.VMEM((slots, width), bf16),
            pltpu.VMEM((max(slots, width), width), bf16),
            pltpu.VMEM((slots, width), bf16),
            pltpu.VMEM((ROWS, ff), bf16),
            pltpu.VMEM((width, 2 * ff), bf16),
            pltpu.VMEM((ff, width), bf16),
            pltpu.VMEM((tokens, width), jnp.float32),
            dma((4,)),
            dma,
            dma((RING,)),
            dma((RING,)),
            dma((RING,)),
            dma((RING,)),
            dma((NPOS,)),
            dma((NPOS,)),
            dma((2,)),
            dma((PARTS,)),
            dma((PARTS,)),
            dma((PARTS,)),
            dma((PARTS,)),
            dma((2, strips)),
            dma((2, strips)),
            dma((strips,)),
            dma((strips,)),
            pltpu.VMEM((2, LOAD) + w_qkv.shape[1:], bf16),
            dma((2,)),
            dma((RING,)),
            dma((RING,)),
            dma((RING,)),
            dma((RING,)),
            dma((RING,)),
            dma((RING,)),
        ],
        compiler_params=pltpu.CompilerParams(
            collective_id=0, has_side_effects=True, vmem_limit_bytes=60 << 20
        ),
    )(
        residual_in[0],
        segment_ids,
        page_owner,
        attn_gain,
        ffn_gain,
        w_router.T,
        routes[0].T,
        w_qkv,
        w_out.reshape(heads * HEAD, width),
        w_gate_up[0],
        w_down[0],
    )
    residual_out, kv_cache = pl.pallas_call(
        hand_over_kernel,
        out_shape=(
            jax.ShapeDtypeStruct(residual_out.shape, bf16),
            jax.ShapeDtypeStruct(kv_cache.shape, bf16),
        ),
        in_specs=[hbm] * 2,
        out_specs=(hbm, hbm),
        scratch_shapes=[
            pltpu.VMEM(residual_out.shape, bf16),
            pltpu.VMEM(kv_cache.shape, bf16),
            dma((2, 4)),
            dma((2, 4)),
        ],
    )(residual_out, kv_cache)
    return (residual_out[None], kv_cache[None])


def solution(mesh):
    in_specs = (
        P("blk", "seq", None),
        P("blk", None),
        P(),
        P(None, "seq", None),
        P("seq", None, None),
        P(),
        P(),
        P("blk", "seq", None),
        P("blk", None, None),
        P("blk", None, None),
        P("blk", None),
    )
    out_specs = (P("blk", "seq", None), P("blk", None, None, "seq"))
    return jax.shard_map(
        on_device, mesh=mesh, in_specs=in_specs, out_specs=out_specs, check_vma=False
    )
```
